128 devices in a mesh: dp: 32 (over x, z, y_lo), mp: 4 (over y_hi, core).
Axes of the slice: x: 4, y: 4 (y_hi: 2, y_lo: 2; y = y_hi * 2 + y_lo), z: 4, core: 2. Of those that a mesh axis runs over, the one named last changes fastest.
Arguments:
- tokens: bfloat16 [8192, 2048], P('dp'), may hold values from -6 to 6
- targets: bfloat16 [8192, 2048], P('dp'), may hold values from -6 to 6
- loss_weights: float32 [8192], P('dp'), may hold values from 0.4 to 14, as said below
- segments: int32 [32, 256], P('dp'), may hold values from 0 to 3, never falling along the last dimension, each value on 1 to 128 neighbouring positions
- probe_model: int32 [32, 2048], P('dp'), may hold values from 0 to 1
- probe_heads: int32 [32, 2, 2048], P('dp', None, 'mp'), may hold values from 0 to 1
- norm_gain: float32 [2048], replicated, may hold values from 0.5 to 1.5
- w_query: bfloat16 [2048, 2048], P(None, 'mp'), may hold values from -0.125 to 0.125
- w_key: bfloat16 [2048, 2048], P(None, 'mp'), may hold values from -0.125 to 0.125
- w_value: bfloat16 [2048, 2048], P(None, 'mp'), may hold values from -0.125 to 0.125
- w_out: bfloat16 [2048, 2048], P('mp'), may hold values from -0.125 to 0.125
Outputs:
- diag_query: float32 [2048, 2048], P('dp', 'mp')
- diag_key: float32 [2048, 2048], P('dp', 'mp')
- mean_diag: float32 [2], replicated
The draws below stay inside these ranges and needn't reach their ends.
Inputs may be any that keep to these rules, and one draw needn't show every extreme that they name: `segments`: the documents of a sequence are runs of 1 to 128 tokens, numbered upwards from 0. `loss_weights`: positive weights.
All inputs are finite; a program needn't handle non-finite values.
Results may differ from the reference program's by a relative error of at most 0.0099.
Values may be sent and summed in bfloat16 or wider, within the bound.
No kernel may reach another device: no remote copies, remote signals or barrier semaphores. Data moves between devices by JAX's collectives and lax.ppermute only.
A program may use at most 128 MiB of HBM per device.

```python
import math
import jax
import jax.numpy as jnp
import numpy as np
from jax import lax

D = 2048
HEAD_DIM = 128
SEQ = 256
DOCS = 4
GROUPS = 32
TOKENS = 8192
FEAT = 2048


def draw_loss_weights(key, part):
    group_index = (jnp.arange(TOKENS, dtype=jnp.int32) // SEQ).astype(jnp.float32)
    rising = 1.0 + 2.0 * group_index / max(GROUPS - 1, 1)
    base_values = jnp.exp(jax.random.uniform(key, (TOKENS,), jnp.float32, jnp.log(0.5), jnp.log(2.0)))
    return (rising * base_values).astype(jnp.float32)


def plant(values, key, least, largest):
    place = [jax.random.randint(jax.random.fold_in(key, axis), (), 0, length) for axis, length in enumerate(values.shape)]
    widest = values.shape.index(max(values.shape))
    next_to = place[:widest] + [(place[widest] + 1) % values.shape[widest]] + place[widest + 1:]
    return values.at[tuple(place)].set(least).at[tuple(next_to)].set(largest)


def with_spikes(array, stream_key, source, target, blocks, factor):
    owner, partner = [(jnp.arange(array.shape[axis_at]) // (array.shape[axis_at] // blocks)).reshape([-1 if axis == axis_at else 1 for axis in range(array.ndim)]) for axis_at in (source, target)]
    chosen = jax.random.permutation(stream_key, blocks)[partner]
    strong = (owner == chosen) | (owner == (partner + blocks // 2) % blocks)
    return jnp.where(strong, factor * array, array)


def block_scale(stream_key, dims, shards, low, top_value):
    level, own = 1.0, jax.random.fold_in(stream_key, 6)
    for dim, blocks in shards:
        steps = jnp.exp(jax.random.uniform(jax.random.fold_in(own, dim), (blocks,), jnp.float32, low / len(shards), top_value / len(shards)))
        level = level * jnp.repeat(steps, dims[dim] // blocks).reshape([-1 if axis == dim else 1 for axis in range(len(dims))])
    return level


def profile(count, total, reach, skew):
    loads = [(1 << 20) // math.isqrt(standing ** skew) + 1 for standing in range(2, count + 1)]
    surplus, given = total - reach - (count - 1), [1] * (count - 1)
    while surplus > 0:
        movable = [i for i in range(count - 1) if given[i] < reach]
        whole, left = sum([loads[i] for i in movable]), surplus
        for i in movable:
            extra = min(reach - given[i], max(1, left * loads[i] // whole), surplus)
            given[i] = given[i] + extra
            surplus = surplus - extra
    return np.array([reach] + given)


def ragged_sizes(rng, amount, total, most, slope):
    if amount == 2:
        one = jax.random.randint(rng, (), max(1, total - most), min(most, total - 1) + 1)
        return jnp.stack([one, total - one])
    sizes = jnp.asarray(profile(amount, total, most, slope), jnp.int32)
    twos = (amount - 1) // 2
    source_of, sink = sizes[1:1 + 2 * twos:2], sizes[2:2 + 2 * twos:2]
    slack = jnp.minimum(source_of - 1, most - sink)
    moved = jax.random.randint(jax.random.fold_in(rng, 1), (twos,), 0, 1 << 20) % (slack + 1)
    sizes = sizes.at[1:1 + 2 * twos:2].set(source_of - moved).at[2:2 + 2 * twos:2].set(sink + moved)
    return sizes[jax.random.permutation(jax.random.fold_in(rng, 2), amount)]


def gaussian(key, dims, spread, most, split=(), kind=jnp.bfloat16):
    gain = block_scale(key, dims, split, -0.22, 0.18) if split else 1.0
    values = jax.random.normal(key, dims, jnp.float32) * spread * gain
    return jnp.minimum(jnp.maximum(values, -most), most).astype(kind)


def heavy_noise(key, shape, scale, limit, pieces, heavy, kind=jnp.bfloat16):
    values = scale * jax.random.normal(key, shape, jnp.float32)
    if pieces:
        values = values * block_scale(key, shape, pieces, -0.22, 0.18)
    return jnp.clip(with_spikes(values, jax.random.fold_in(key, 3), *heavy), -limit, limit).astype(kind)


def setup_inputs(seed: int = 0) -> dict:
    seeds = jax.random.split(jax.random.key(seed), 12)
    tokens = heavy_noise(seeds[0], (TOKENS, D), 1.0, 6.0, ((0, 32),), (0, 1, 32, 2.75))
    targets = heavy_noise(seeds[1], (TOKENS, D), 1.0, 6.0, ((0, 32),), (0, 1, 32, 2.75))
    loss_weights = draw_loss_weights(jax.random.fold_in(seeds[11], 71), 0)
    segments = jax.vmap(lambda own: jnp.searchsorted(jnp.cumsum(ragged_sizes(own, DOCS, SEQ, SEQ // 2, 0)), jnp.arange(SEQ), side="right"))(jax.random.split(seeds[3], GROUPS)).reshape((GROUPS, SEQ)).astype(jnp.int32)
    probe_model = plant(jax.random.randint(seeds[4], (GROUPS, D), 0, 2), jax.random.fold_in(seeds[4], 1), 0, 1).astype(jnp.int32)
    probe_heads = plant(jax.random.randint(seeds[5], (GROUPS, 2, FEAT), 0, 2), jax.random.fold_in(seeds[5], 1), 0, 1).astype(jnp.int32)
    norm_gain = jnp.clip(1.0 + 0.1 * jax.random.normal(seeds[6], (D,), jnp.float32), 0.5, 1.5)
    w_query = gaussian(seeds[7], (D, FEAT), D ** -0.5, 0.125, ((1, 4),))
    w_key = gaussian(seeds[8], (D, FEAT), D ** -0.5, 0.125, ((1, 4),))
    w_value = gaussian(seeds[9], (D, FEAT), D ** -0.5, 0.125, ((1, 4),))
    w_out = gaussian(seeds[10], (FEAT, D), FEAT ** -0.5, 0.125, ((0, 4),))
    return dict(tokens=tokens, targets=targets, loss_weights=loss_weights, segments=segments, probe_model=probe_model, probe_heads=probe_heads, norm_gain=norm_gain, w_query=w_query, w_key=w_key, w_value=w_value, w_out=w_out)


exact_mode = lax.Precision.HIGHEST
norm_epsilon = 1e-06

def sign_pattern(row_index, col_index):
    mixed_index = (row_index[:, None] * 1103 + col_index[None, :] * 2713 + 7) % 32749
    mixed_index = mixed_index * mixed_index % 32749
    return 1.0 - 2.0 * (mixed_index // 5 % 2).astype(jnp.float32)

def rope_tables(length):
    position = jnp.arange(length, dtype=jnp.int32).astype(jnp.float32)
    exponent = jnp.arange(0, HEAD_DIM, 2, dtype=jnp.int32).astype(jnp.float32) / HEAD_DIM
    frequency = 10000.0 ** (-exponent)
    angles = position[:, None] * frequency[None, :]
    return (jnp.cos(angles)[:, None, :], jnp.sin(angles)[:, None, :])

def rotate(packed, cosine, sine_table):
    half_dim = packed.shape[-1] // 2
    front_half = packed[..., :half_dim]
    back_half = packed[..., half_dim:]
    return jnp.concatenate([front_half * cosine - back_half * sine_table, back_half * cosine + front_half * sine_table], axis=-1)

def attend(query, keys, values, doc_ids):
    length = query.shape[0]
    head_count = query.shape[1] // HEAD_DIM
    cosine, sine_table = rope_tables(length)
    rotated_query = rotate(query.reshape(length, head_count, HEAD_DIM), cosine, sine_table)
    rotated_keys = rotate(keys.reshape(length, head_count, HEAD_DIM), cosine, sine_table)
    scores = jnp.einsum('qhd,khd->hqk', rotated_query, rotated_keys, precision=exact_mode) * HEAD_DIM ** (-0.5)
    position = jnp.arange(length, dtype=jnp.int32)
    allowed = (position[:, None] >= position[None, :]) & (doc_ids[:, None] == doc_ids[None, :])
    raised = jnp.where(allowed[None], jnp.exp(scores), 0.0)
    attention_weights = raised / lax.optimization_barrier(jnp.sum(raised, axis=-1, keepdims=True))
    mixed_values = jnp.einsum('hqk,khd->qhd', attention_weights, values.reshape(length, head_count, HEAD_DIM), precision=exact_mode)
    return mixed_values.reshape(length, head_count * HEAD_DIM)

def tangent_of(query, keys, values, doc_ids, tangents):

    def forward(query_in, keys_in, values_in):
        return attend(query_in, keys_in, values_in, doc_ids)
    result, pullback = jax.vjp(forward, query, keys, values)

    def pulled(cotangent):
        return pullback(cotangent)
    unused, pushforward = jax.vjp(pulled, jnp.zeros_like(result))
    return (result, pushforward((tangents[0], tangents[1], jnp.zeros_like(values)))[0])

def second_order(query, keys, values, doc_ids, back_grad, tangents, back_tangent):

    def inner(query_in, keys_in):

        def paired(query_at, keys_at):
            return jnp.sum(attend(query_at, keys_at, values, doc_ids) * back_grad)
        gradients = jax.grad(paired, argnums=(0, 1))(query_in, keys_in)
        summed = jnp.sum(gradients[0] * tangents[0]) + jnp.sum(gradients[1] * tangents[1])
        return summed + jnp.sum(attend(query_in, keys_in, values, doc_ids) * back_tangent)
    return jax.grad(inner, argnums=(0, 1))(query, keys)

def bf_dot(left, right):
    return jnp.dot(left, right, preferred_element_type=jnp.float32)

def reference(tokens, targets, loss_weights, segments, probe_model, probe_heads, norm_gain, w_query, w_key, w_value, w_out):
    pattern = sign_pattern(jnp.arange(D, dtype=jnp.int32), jnp.arange(FEAT, dtype=jnp.int32))

    def group_step(carry, inputs):
        group_tokens, group_targets, group_weights, doc_ids, model_bits, head_bits = inputs
        model_sign = 2.0 * model_bits.astype(jnp.float32) - 1.0
        head_sign = 2.0 * head_bits.astype(jnp.float32) - 1.0
        probe_query = (model_sign[:, None] * head_sign[0][None, :] * pattern).astype(jnp.bfloat16)
        probe_key = (model_sign[:, None] * head_sign[1][None, :] * pattern).astype(jnp.bfloat16)
        token_float = group_tokens.astype(jnp.float32)
        inverse_rms = lax.rsqrt(lax.optimization_barrier(jnp.mean(token_float * token_float, axis=1, keepdims=True)) + norm_epsilon)
        normed = (token_float * inverse_rms * norm_gain).astype(jnp.bfloat16)
        query = bf_dot(normed, w_query)
        keys = bf_dot(normed, w_key)
        values = bf_dot(normed, w_value)
        d_query = bf_dot(normed, probe_query)
        d_keys = bf_dot(normed, probe_key)
        attended_full, d_attended_full = tangent_of(query, keys, values, doc_ids, (d_query, d_keys))
        attended = attended_full.astype(jnp.bfloat16)
        d_attended = d_attended_full.astype(jnp.bfloat16)
        weight_rows = group_weights / SEQ
        output = token_float + bf_dot(attended, w_out)
        residual = ((output - group_targets.astype(jnp.float32)) * weight_rows[:, None]).astype(jnp.bfloat16)
        d_output = bf_dot(d_attended, w_out)
        d_residual = (d_output * weight_rows[:, None]).astype(jnp.bfloat16)
        back_grad = bf_dot(residual, w_out.T)
        back_tangent = bf_dot(d_residual, w_out.T)
        h_query, h_keys = second_order(query, keys, values, doc_ids, back_grad, (d_query, d_keys), back_tangent)
        est_query = probe_query.astype(jnp.float32) * bf_dot(normed.T, h_query.astype(jnp.bfloat16))
        est_key = probe_key.astype(jnp.float32) * bf_dot(normed.T, h_keys.astype(jnp.bfloat16))
        return ((carry[0] + est_query, carry[1] + est_key), None)
    zero_feat = jnp.zeros((D, FEAT), jnp.float32)
    inputs = (tokens.reshape(GROUPS, SEQ, D), targets.reshape(GROUPS, SEQ, D), loss_weights.reshape(GROUPS, SEQ), segments, probe_model, probe_heads)
    sums, unused = lax.scan(group_step, (zero_feat, zero_feat), inputs)
    diag_query = sums[0] / GROUPS
    diag_key = sums[1] / GROUPS
    mean_diag = jnp.stack([jnp.sum(diag_query), jnp.sum(diag_key)]) / (D * FEAT)
    return (diag_query, diag_key, mean_diag)
```

```python
import functools

import jax
import jax.numpy as jnp
import numpy as np
from jax import lax
from jax.experimental import pallas as pl
from jax.experimental.pallas import tpu as pltpu
from jax.sharding import Mesh
from jax.sharding import PartitionSpec as P


HEAD_DIM = 128
PRIME = 32749
EPSILON = 1e-06
SCALE = HEAD_DIM**-0.5
MIB = 1 << 20
DP = ("x", "z", "yl")
MP = ("yh", "c")
bf16, f32, i32 = jnp.bfloat16, jnp.float32, jnp.int32
VMEM = pl.BlockSpec(memory_space=pltpu.VMEM)
ANY = pl.BlockSpec(memory_space=pl.ANY)


def shape(dims, kind):
    return jax.ShapeDtypeStruct(dims, kind)


def call(body, outs, ins, scratch=(), name=None, flops=0, moved=0, limit=24):
    return pl.pallas_call(
        body,
        out_shape=outs,
        in_specs=ins,
        out_specs=jax.tree.map(lambda _: VMEM, outs),
        scratch_shapes=scratch,
        name=name,
        cost_estimate=pl.CostEstimate(flops=flops, bytes_accessed=moved, transcendentals=0),
        compiler_params=pltpu.CompilerParams(vmem_limit_bytes=limit * MIB),
    )


def dot(a, b):
    return jnp.dot(a, b, preferred_element_type=f32)


def dot_nt(a, b):
    return lax.dot_general(a, b, (((1,), (1,)), ((), ())), preferred_element_type=f32)


def dot_tn(a, b):
    return lax.dot_general(a, b, (((0,), (0,)), ((), ())), preferred_element_type=f32)


def head(h):
    return slice(h * HEAD_DIM, (h + 1) * HEAD_DIM)


def rotate(x, cosine, sine):
    return x * cosine + pltpu.roll(x, HEAD_DIM // 2, 1) * sine


def rope_tables(length):
    position = np.arange(length, dtype=np.float32)
    exponent = np.arange(0, HEAD_DIM, 2, dtype=np.float32) / np.float32(HEAD_DIM)
    frequency = np.power(10000.0, -exponent.astype(np.float64)).astype(np.float32)
    angles = (position[:, None] * frequency[None, :]).astype(np.float64)
    cosine, sine = np.cos(angles), np.sin(angles)
    return (
        np.concatenate([cosine, cosine], axis=1).astype(np.float32),
        np.concatenate([-sine, sine], axis=1).astype(np.float32),
    )


def split3(value):
    high = value.astype(bf16)
    rest = value - high.astype(f32)
    middle = rest.astype(bf16)
    low = (rest - middle.astype(f32)).astype(bf16)
    return high, middle, low


def forward_body(
    tok_hbm, gain, seg, cosine, sine, wq_hbm, wk_hbm, wv_hbm, wo_hbm,
    normed_out, q_out, k_out, v_out, p_out, send_out, own_out,
    tok, wq, wk, wv, wo, sems,
):
    pairs = ((tok_hbm, tok), (wq_hbm, wq), (wk_hbm, wk), (wv_hbm, wv), (wo_hbm, wo))
    copies = [pltpu.make_async_copy(s, d, sems.at[i]) for i, (s, d) in enumerate(pairs)]
    for copy in copies:
        copy.start()
    length = tok.shape[0]
    heads = q_out.shape[1] // HEAD_DIM
    half = send_out.shape[1]
    core = lax.axis_index("c")
    copies[0].wait()
    tokens = tok[...].astype(f32)
    inverse = lax.rsqrt(jnp.mean(tokens * tokens, axis=1, keepdims=True) + EPSILON)
    normed = (tokens * inverse * gain[...]).astype(bf16)
    normed_out[...] = normed
    copies[1].wait()
    query = dot(normed, wq[...])
    copies[2].wait()
    keys = dot(normed, wk[...])
    copies[3].wait()
    values = dot(normed, wv[...]).astype(bf16)
    v_out[...] = values
    document = jnp.broadcast_to(seg[...].astype(f32), (length, length))
    row = lax.broadcasted_iota(i32, (length, length), 0)
    col = lax.broadcasted_iota(i32, (length, length), 1)
    allowed = (row >= col) & (document == document.T)
    attended = []
    for h in range(heads):
        q = rotate(query[:, head(h)], cosine[...], sine[...])
        k = rotate(keys[:, head(h)], cosine[...], sine[...])
        q_high, k_high = q.astype(bf16), k.astype(bf16)
        q_low = (q - q_high.astype(f32)).astype(bf16)
        k_low = (k - k_high.astype(f32)).astype(bf16)
        q_out[:, head(h)] = q_high
        k_out[:, head(h)] = k_high
        scores = dot_nt(
            jnp.concatenate([q_high, q_low], axis=1), jnp.concatenate([k_high, k_high], axis=1)
        ) + dot_nt(q_high, k_low)
        raised = jnp.where(allowed, jnp.exp(scores * SCALE), 0.0)
        weights = raised * (1.0 / jnp.sum(raised, axis=1, keepdims=True))
        p_out[h] = weights
        attended.append(dot(weights.astype(bf16), values[:, head(h)]).astype(bf16))
    attended = jnp.concatenate(attended, axis=1)
    copies[4].wait()
    mine = pl.multiple_of(core * half, half)
    other = pl.multiple_of((1 - core) * half, half)
    send_out[...] = dot(attended, wo[:, pl.ds(other, half)]).astype(bf16)
    own_out[...] = dot(attended, wo[:, pl.ds(mine, half)])


def small_mod(value):
    estimate = jnp.floor(value.astype(f32) * (1.0 / PRIME)).astype(i32)
    rest = value - estimate * PRIME
    rest = jnp.where(rest < 0, rest + PRIME, rest)
    return jnp.where(rest >= PRIME, rest - PRIME, rest)


def square_state(row0, col0, dims):
    row = row0 + lax.broadcasted_iota(i32, dims, 0)
    col = col0 + lax.broadcasted_iota(i32, dims, 1)
    mixed = small_mod(row * 1103 + col * 2713 + 7)
    return mixed, small_mod(mixed * mixed)


def sign_of(square):
    tenth = square * 0.1 + 0.05
    return jnp.where(tenth - jnp.floor(tenth) < 0.5, 1.0, -1.0)


STEP = 16
SHIFT = (1103 * STEP) % PRIME


def wrap(value):
    return jnp.where(value >= PRIME, value - PRIME, value)


def fill_pattern(col0, out):
    width, columns = out.shape
    mixed, square = square_state(0, col0, (STEP, columns))
    change = small_mod(mixed * (2 * SHIFT % PRIME) + SHIFT * SHIFT % PRIME)
    second = float(2 * SHIFT * SHIFT % PRIME)

    def step(i, state):
        square, change = state
        out[pl.ds(pl.multiple_of(i * STEP, STEP), STEP), :] = sign_of(square).astype(bf16)
        return wrap(square + change), wrap(change + second)

    lax.fori_loop(0, width // STEP, step, (square.astype(f32), change.astype(f32)))


def tangent_body(
    normed, model_bits, head_bits, cosine, sine, q_ref, k_ref, v_ref, p_ref, wo,
    dq_out, dk_out, r_out, ds_out, send_out, own_out,
    pattern,
):
    heads = q_ref.shape[1] // HEAD_DIM
    half = send_out.shape[1]
    feat = q_ref.shape[1]
    core = lax.axis_index("c")
    fill_pattern((lax.axis_index("yh") * 2 + core) * feat, pattern)
    sign = (2 * model_bits[...] - 1).astype(f32).astype(bf16)
    product = dot(normed[...] * sign, pattern[...])
    r_out[...] = product
    signs = (2 * head_bits[...] - 1).astype(f32)
    d_query = product * signs[0:1, :]
    d_keys = product * signs[1:2, :]
    tangents = []
    for h in range(heads):
        dq = rotate(d_query[:, head(h)], cosine[...], sine[...]).astype(bf16)
        dk = rotate(d_keys[:, head(h)], cosine[...], sine[...]).astype(bf16)
        dq_out[:, head(h)] = dq
        dk_out[:, head(h)] = dk
        d_scores = dot_nt(
            jnp.concatenate([dq, q_ref[:, head(h)]], axis=1),
            jnp.concatenate([k_ref[:, head(h)], dk], axis=1),
        ) * SCALE
        weights = p_ref[h]
        centred = d_scores - jnp.sum(weights * d_scores, axis=1, keepdims=True)
        ds_out[h] = centred
        tangents.append(dot((weights * centred).astype(bf16), v_ref[:, head(h)]).astype(bf16))
    tangents = jnp.concatenate(tangents, axis=1)
    mine = pl.multiple_of(core * half, half)
    other = pl.multiple_of((1 - core) * half, half)
    send_out[...] = dot(tangents, wo[:, pl.ds(other, half)]).astype(bf16)
    own_out[...] = dot(tangents, wo[:, pl.ds(mine, half)])


def base_body(tokens, targets, loss_weights, base_out, weight_out):
    half = base_out.shape[1]
    length = base_out.shape[0]
    mine = pl.multiple_of(lax.axis_index("c") * half, half)
    base_out[...] = tokens[:, pl.ds(mine, half)].astype(f32) - targets[:, pl.ds(mine, half)].astype(f32)
    weight_out[...] = jnp.broadcast_to(loss_weights[...] * (1.0 / length), (HEAD_DIM, length)).T


def residual_body(near, far, base, weight, out):
    out[...] = ((near[...].astype(f32) + far[...].astype(f32) + base[...]) * weight[:, 0:1]).astype(bf16)


def d_residual_body(near, far, weight, out):
    out[...] = ((near[...].astype(f32) + far[...].astype(f32)) * weight[:, 0:1]).astype(bf16)


def back_of(res_own, res_mate, wo):
    half = res_own.shape[1]
    core = lax.axis_index("c")
    mine = pl.multiple_of(core * half, half)
    other = pl.multiple_of((1 - core) * half, half)
    return (
        dot_nt(res_own[...], wo[:, pl.ds(mine, half)])
        + dot_nt(res_mate[...], wo[:, pl.ds(other, half)])
    ).astype(bf16)


def second_body(res_own, res_mate, wo, q_ref, k_ref, v_ref, dq_ref, dk_ref, p_ref, ds_ref, hq_out, hk_out):
    back = back_of(res_own, res_mate, wo)
    for h in range(q_ref.shape[1] // HEAD_DIM):
        s = head(h)
        weights = p_ref[h]
        u = dot_nt(back[:, s], v_ref[:, s])
        first = weights * (u - jnp.sum(weights * u, axis=1, keepdims=True))
        curved = first * ds_ref[h]
        second = curved - weights * jnp.sum(curved, axis=1, keepdims=True)
        first, second = first.astype(bf16), second.astype(bf16)
        hq_out[:, s] = dot(first, dk_ref[:, s]) + dot(second, k_ref[:, s])
        hk_out[:, s] = dot_tn(first, dq_ref[:, s]) + dot_tn(second, q_ref[:, s])


def third_body(
    res_own, res_mate, wo, q_ref, k_ref, v_ref, p_ref, hq_ref, hk_ref, r_ref, head_bits, cosine, sine,
    y_out, sum_out,
):
    feat = q_ref.shape[1]
    back = back_of(res_own, res_mate, wo)
    signs = (2 * head_bits[...] - 1).astype(f32)
    totals = [0.0, 0.0]
    for h in range(feat // HEAD_DIM):
        s = head(h)
        weights = p_ref[h]
        u = dot_nt(back[:, s], v_ref[:, s])
        first = (weights * (u - jnp.sum(weights * u, axis=1, keepdims=True))).astype(bf16)
        hq = (hq_ref[:, s] + dot(first, k_ref[:, s])) * SCALE
        hk = (hk_ref[:, s] + dot_tn(first, q_ref[:, s])) * SCALE
        product = r_ref[:, s]
        for i, gradient in enumerate((hq, hk)):
            y = rotate(gradient, cosine[...], -sine[...]) * signs[i : i + 1, s]
            y = y.astype(bf16)
            y_out[:, i * feat + h * HEAD_DIM : i * feat + (h + 1) * HEAD_DIM] = y
            totals[i] = totals[i] + jnp.sum(product * y.astype(f32), axis=0, keepdims=True)
    pair = [jnp.sum(t, axis=1, keepdims=True) for t in totals]
    lane = lax.broadcasted_iota(i32, sum_out.shape, 1)
    sum_out[...] = jnp.where(lane == 0, pair[0], jnp.where(lane == 1, pair[1], 0.0))


def transpose_body(normed, model_bits, own_out, send_out, whole):
    sign = (2 * model_bits[...] - 1).astype(f32).astype(bf16)
    signed = normed[...] * sign
    for i in range(whole.shape[0] // HEAD_DIM):
        whole[i * HEAD_DIM : (i + 1) * HEAD_DIM, :] = signed[:, i * HEAD_DIM : (i + 1) * HEAD_DIM].T
    rows = whole.shape[0] // 32
    x, z, yl = lax.axis_index("x"), lax.axis_index("z"), lax.axis_index("yl")
    for out, base in ((own_out, x), (send_out, x + 1 - 2 * lax.rem(x, 2))):
        for ez in range(4):
            for ex in range(2):
                for ey in range(2):
                    to_x = base if ex == 0 else 3 - base
                    to_z = lax.rem(z + ez, 4)
                    to_y = yl if ey == 0 else 1 - yl
                    start = pl.multiple_of(((to_x * 4 + to_z) * 2 + to_y) * rows, rows)
                    at = ((ez * 2 + ex) * 2 + ey) * rows
                    out[at : at + rows, :] = whole[pl.ds(start, rows), :]


def estimate_body(x_own, x_mate, y_own, y_mate, sums, a0, a1, a2, a3, b0, b1, b2, b3):
    group = b0.shape[0]
    rows = group // 4
    feat = b0.shape[1]
    pieces = jnp.concatenate(
        [part for part in split3(sums[...])] + [jnp.zeros((sums.shape[0], HEAD_DIM), bf16)], axis=1
    )
    for ez, out in enumerate((a0, a1, a2, a3)):
        at = slice(ez * group, (ez + 1) * group)
        part = dot(x_own[at, :], y_own[...]) + dot(x_mate[at, :], y_mate[...])
        if ez == 0:
            out[...] = part[:, :feat]
        else:
            out[:group, :] = part[:, :feat].astype(bf16)
            out[group:, :] = pieces
        for e, to in enumerate((b0, b1, b2, b3)):
            to[ez * rows : (ez + 1) * rows, :] = part[e * rows : (e + 1) * rows, feat:].astype(to.dtype)


def read_sums(part):
    return sum(part[:, i * HEAD_DIM : (i + 1) * HEAD_DIM].astype(f32) for i in range(3))


def middle_body(a0, a1, a2, a3, b0, b1, b2, b3, sums, *outs):
    group = b0.shape[0]
    rows = group // 4
    a = a0[...] + sum(r[:group, :].astype(f32) for r in (a1, a2, a3))
    b = b0[...] + sum(r[...].astype(f32) for r in (b1, b2, b3))
    total = sums[...] + sum(read_sums(r[group:, :]) for r in (a1, a2, a3))
    pieces = jnp.concatenate(list(split3(total)) + [jnp.zeros(total.shape, bf16)], axis=1)
    a_outs, b_outs, sum_out = outs[:4], outs[4:8], outs[8]
    for e, out in enumerate(a_outs):
        part = a[e * rows : (e + 1) * rows, :]
        if e == 0:
            out[...] = part
        else:
            out[:rows, :] = part.astype(bf16)
            out[rows:, :] = pieces
    for e, out in enumerate(b_outs):
        out[...] = b[e * rows : (e + 1) * rows, :].astype(out.dtype)
    sum_out[...] = total


def final_body(a0, a1, a2, a3, b0, b1, b2, b3, sums, diag_query, diag_key, mean_out, *, groups, entries):
    rows, feat = b0.shape
    x, z, yl = lax.axis_index("x"), lax.axis_index("z"), lax.axis_index("yl")
    row0 = ((x * 4 + z) * 2 + yl) * rows
    col0 = (lax.axis_index("yh") * 2 + lax.axis_index("c")) * feat
    _, square = square_state(row0, col0, (rows, feat))
    sign = sign_of(square.astype(f32)) * (1.0 / groups)
    diag_query[...] = sign * (a0[...] + sum(r[:rows, :].astype(f32) for r in (a1, a2, a3)))
    diag_key[...] = sign * (b0[...] + sum(r[...].astype(f32) for r in (b1, b2, b3)))
    total = sums[...] + sum(read_sums(r[rows:, :]) for r in (a1, a2, a3))
    mean_out[...] = total * (1.0 / (groups * entries))


def flip(value, moves):
    axes = tuple(axis for axis, _ in moves)
    sizes = [lax.axis_size(axis) for axis in axes]

    def target(index):
        where = []
        for size in reversed(sizes):
            where.append(index % size)
            index //= size
        where = [f(w) for (_, f), w in zip(moves, reversed(where))]
        result = 0
        for w, size in zip(where, sizes):
            result = result * size + w
        return result

    count = int(np.prod(sizes))
    return lax.ppermute(value, axes if len(axes) > 1 else axes[0], [(i, target(i)) for i in range(count)])


def xor(axis, mask):
    return (axis, lambda i: i ^ mask)


def add(axis, k):
    return (axis, lambda i: (i + k) % lax.axis_size(axis))


def local(tokens, targets, loss_weights, segments, probe_model, probe_heads, norm_gain, w_query, w_key, w_value, w_out):
    length, width = tokens.shape
    feat = w_query.shape[1]
    heads = feat // HEAD_DIM
    half = width // 2
    groups = lax.axis_size(DP)
    entries = width * feat * lax.axis_size(MP)
    cosine, sine = (jnp.asarray(t) for t in rope_tables(length))
    head_bits = probe_heads[0]
    mat = shape((length, feat), bf16)
    square = shape((heads, length, length), f32)
    half16, half32 = shape((length, half), bf16), shape((length, half), f32)
    product = 2 * length * width * feat
    small = 2 * length * length * HEAD_DIM * heads
    weight = pltpu.VMEM((width, feat), bf16)

    normed, q, k, v, p, send, own = call(
        forward_body,
        (shape((length, width), bf16), mat, mat, mat, square, half16, half32),
        [ANY, VMEM, VMEM, VMEM, VMEM, ANY, ANY, ANY, ANY],
        [pltpu.VMEM((length, width), bf16), weight, weight, weight, pltpu.VMEM((feat, width), bf16), pltpu.SemaphoreType.DMA((5,))],
        "forward", 4 * product + 4 * small, 12 * MIB, 40,
    )(tokens, norm_gain[None, :], segments, cosine, sine, w_query, w_key, w_value, w_out)
    mate = [xor("c", 1)]
    far = [xor("yh", 1)]
    near = (own + flip(send, mate).astype(f32)).astype(bf16)
    there = flip(near, far)

    dq, dk, r, ds, d_send, d_own = call(
        tangent_body,
        (mat, mat, shape((length, feat), f32), square, half16, half32),
        [VMEM] * 10,
        [pltpu.VMEM((width, feat), bf16)],
        "tangent", 2 * product + 4 * small, 8 * MIB, 32,
    )(normed, probe_model, head_bits, cosine, sine, q, k, v, p, w_out)
    d_near = (d_own + flip(d_send, mate).astype(f32)).astype(bf16)
    d_there = flip(d_near, far)

    x_own, x_send = call(
        transpose_body,
        (shape((width // 2, length), bf16),) * 2,
        [VMEM] * 2,
        [pltpu.VMEM((width, length), bf16)],
        "rows", 0, 3 * MIB, 16,
    )(normed, probe_model)
    x_mate = flip(x_send, [xor("x", 1)])

    base, row_weight = call(
        base_body,
        (half32, shape((length, HEAD_DIM), f32)),
        [VMEM] * 3,
        (), "base", 0, 3 * MIB, 16,
    )(tokens, targets, loss_weights[None, :])

    res_own = call(residual_body, half16, [VMEM] * 4, (), "residual", 0, 3 * MIB, 16)(near, there, base, row_weight)
    res_mate = flip(res_own, mate)
    hq, hk = call(
        second_body,
        (shape((length, feat), f32),) * 2,
        [VMEM] * 10,
        (), "second", product + 5 * small, 6 * MIB, 24,
    )(res_own, res_mate, w_out, q, k, v, dq, dk, p, ds)

    d_res_own = call(d_residual_body, half16, [VMEM] * 3, (), "d_residual", 0, 2 * MIB, 16)(d_near, d_there, row_weight)
    d_res_mate = flip(d_res_own, mate)
    y, sums = call(
        third_body,
        (shape((length, 2 * feat), bf16), shape((16, HEAD_DIM), f32)),
        [VMEM] * 13,
        (), "third", product + 3 * small, 6 * MIB, 24,
    )(d_res_own, d_res_mate, w_out, q, k, v, p, hq, hk, r, head_bits, cosine, sine)

    y_mate = flip(y, [xor("x", 1)])
    sums = sums + flip(sums, mate)
    sums = sums + flip(sums, far) + flip(sums, [xor("x", 1)]) + flip(sums, [xor("x", 1), xor("yh", 1)])

    rows = width // 32
    group = 4 * rows
    a_out, b_out = shape((group + 16, feat), bf16), shape((group, feat), bf16)
    keep = shape((group, feat), f32)
    parts = call(
        estimate_body,
        (keep, a_out, a_out, a_out, keep, b_out, b_out, b_out),
        [VMEM] * 5,
        (), "estimate", 2 * product, 6 * MIB, 24,
    )(x_own, x_mate, y, y_mate, sums)
    along = [[add("z", 1)], [add("z", 2)], [add("z", 3)]]
    across = [[xor("yl", 1)], [xor("x", 3)], [xor("x", 3), xor("yl", 1)]]
    a_in = [flip(m, where) for m, where in zip(parts[1:4], along)]
    b_in = [flip(m, where) for m, where in zip(parts[5:8], across)]
    a_out, b_out = shape((rows + 16, feat), bf16), shape((rows, feat), bf16)
    keep = shape((rows, feat), f32)
    parts = call(
        middle_body,
        (keep, a_out, a_out, a_out, keep, b_out, b_out, b_out, shape((16, HEAD_DIM), f32)),
        [VMEM] * 9,
        (), "middle", 0, 3 * MIB, 24,
    )(parts[0], *a_in, parts[4], *b_in, sums)
    a_in = [flip(m, where) for m, where in zip(parts[1:4], across)]
    b_in = [flip(m, where) for m, where in zip(parts[5:8], along)]
    diag_query, diag_key, mean = call(
        functools.partial(final_body, groups=groups, entries=entries),
        (keep, keep, shape((16, HEAD_DIM), f32)),
        [VMEM] * 9,
        (), "final", 0, MIB, 16,
    )(parts[0], *a_in, parts[4], *b_in, parts[8])
    return diag_query, diag_key, mean[0, :2]


def solution(mesh):
    torus = Mesh(mesh.devices.reshape(4, 4, 2, 2, 2), ("x", "z", "yl", "yh", "c"))
    return jax.shard_map(
        local,
        mesh=torus,
        in_specs=(
            P(DP, None),
            P(DP, None),
            P(DP),
            P(DP, None),
            P(DP, None),
            P(DP, None, MP),
            P(),
            P(None, MP),
            P(None, MP),
            P(None, MP),
            P(MP, None),
        ),
        out_specs=(P(DP, MP), P(DP, MP), P()),
        check_vma=False,
    )
```

```python
import functools

import jax
import jax.numpy as jnp
import numpy as np
from jax import lax
from jax.experimental import pallas as pl
from jax.experimental.pallas import tpu as pltpu
from jax.sharding import Mesh
from jax.sharding import PartitionSpec as P


HEAD_DIM = 128
PRIME = 32749
EPSILON = 1e-06
SCALE = HEAD_DIM**-0.5
MIB = 1 << 20
DP = ("xh", "xl", "z", "yl")
MP = ("yh", "c")
bf16, f32, i32 = jnp.bfloat16, jnp.float32, jnp.int32
VMEM = pl.BlockSpec(memory_space=pltpu.VMEM)
ANY = pl.BlockSpec(memory_space=pl.ANY)
HBM = pl.BlockSpec(memory_space=pltpu.HBM)


def shape(dims, kind):
    return jax.ShapeDtypeStruct(dims, kind)


def call(body, outs, ins, scratch=(), flops=0, moved=0, limit=24, after=()):
    count = len(ins)

    def whole(*refs):
        return body(*refs[:count], *refs[count + len(after) :])

    kernel = pl.pallas_call(
        whole,
        out_shape=outs,
        in_specs=list(ins) + [ANY] * len(after),
        out_specs=jax.tree.map(lambda _: VMEM, outs),
        scratch_shapes=scratch,
        cost_estimate=pl.CostEstimate(flops=flops, bytes_accessed=moved, transcendentals=0),
        compiler_params=pltpu.CompilerParams(vmem_limit_bytes=limit * MIB),
    )

    def run(*args):
        return kernel(*args, *after)

    return run


def dot(a, b):
    return jnp.dot(a, b, preferred_element_type=f32)


def dot_nt(a, b):
    return lax.dot_general(a, b, (((1,), (1,)), ((), ())), preferred_element_type=f32)


def dot_tn(a, b):
    return lax.dot_general(a, b, (((0,), (0,)), ((), ())), preferred_element_type=f32)


def head(h):
    return slice(h * HEAD_DIM, (h + 1) * HEAD_DIM)


def rotate(x, cosine, sine):
    return x * cosine + pltpu.roll(x, HEAD_DIM // 2, 1) * sine


def rope_tables(length):
    position = np.arange(length, dtype=np.float32)
    exponent = np.arange(0, HEAD_DIM, 2, dtype=np.float32) / np.float32(HEAD_DIM)
    frequency = np.power(10000.0, -exponent.astype(np.float64)).astype(np.float32)
    angles = (position[:, None] * frequency[None, :]).astype(np.float64)
    cosine, sine = np.cos(angles), np.sin(angles)
    return (
        np.concatenate([cosine, cosine], axis=1).astype(np.float32),
        np.concatenate([-sine, sine], axis=1).astype(np.float32),
    )


def split3(value):
    high = value.astype(bf16)
    rest = value - high.astype(f32)
    middle = rest.astype(bf16)
    low = (rest - middle.astype(f32)).astype(bf16)
    return high, middle, low


def forward_body(
    tok_hbm, gain_hbm, wq_hbm, wk_hbm, table_hbm, seg_hbm, wv_hbm, wo_hbm,
    normed_out, q_out, k_out, v_out, p_out, send_out, own_out,
    tok, gain, wq, wk, table, seg, wv, wo, sems,
):
    sources = (tok_hbm, gain_hbm, wq_hbm, wk_hbm, table_hbm, seg_hbm, wv_hbm, wo_hbm)
    places = (tok, gain, wq, wk, table, seg, wv, wo)
    copies = [pltpu.make_async_copy(s, d, sems.at[i]) for i, (s, d) in enumerate(zip(sources, places))]
    for copy in copies:
        copy.start()
    length = tok.shape[0]
    heads = q_out.shape[1] // HEAD_DIM
    half = send_out.shape[1]
    core = lax.axis_index("c")
    copies[0].wait()
    copies[1].wait()
    tokens = tok[...].astype(f32)
    inverse = lax.rsqrt(jnp.mean(tokens * tokens, axis=1, keepdims=True) + EPSILON)
    normed = (tokens * inverse * gain[...]).astype(bf16)
    normed_out[...] = normed
    copies[2].wait()
    query = dot(normed, wq[...])
    copies[3].wait()
    keys = dot(normed, wk[...])
    for copy in copies[4:7]:
        copy.wait()
    values = dot(normed, wv[...]).astype(bf16)
    v_out[...] = values
    document = jnp.broadcast_to(seg[...].astype(f32), (length, length))
    row = lax.broadcasted_iota(i32, (length, length), 0)
    col = lax.broadcasted_iota(i32, (length, length), 1)
    allowed = (row >= col) & (document == document.T)
    attended = []
    for h in range(heads):
        q = rotate(query[:, head(h)], table[:length], table[length:])
        k = rotate(keys[:, head(h)], table[:length], table[length:])
        q_high, k_high = q.astype(bf16), k.astype(bf16)
        q_low = (q - q_high.astype(f32)).astype(bf16)
        k_low = (k - k_high.astype(f32)).astype(bf16)
        q_out[:, head(h)] = q_high
        k_out[:, head(h)] = k_high
        scores = dot_nt(
            jnp.concatenate([q_high, q_low], axis=1), jnp.concatenate([k_high, k_high], axis=1)
        ) + dot_nt(q_high, k_low)
        raised = jnp.where(allowed, jnp.exp(scores * SCALE), 0.0)
        weights = raised * (1.0 / jnp.sum(raised, axis=1, keepdims=True))
        p_out[h] = weights
        attended.append(dot(weights.astype(bf16), values[:, head(h)]).astype(bf16))
    attended = jnp.concatenate(attended, axis=1)
    copies[7].wait()
    mine = pl.multiple_of(core * half, half)
    other = pl.multiple_of((1 - core) * half, half)
    send_out[...] = dot(attended, wo[:, pl.ds(other, half)]).astype(bf16)
    own_out[...] = dot(attended, wo[:, pl.ds(mine, half)])


def small_mod(value):
    estimate = jnp.floor(value.astype(f32) * (1.0 / PRIME)).astype(i32)
    rest = value - estimate * PRIME
    rest = jnp.where(rest < 0, rest + PRIME, rest)
    return jnp.where(rest >= PRIME, rest - PRIME, rest)


def square_state(row0, col0, dims):
    row = row0 + lax.broadcasted_iota(i32, dims, 0)
    col = col0 + lax.broadcasted_iota(i32, dims, 1)
    mixed = small_mod(row * 1103 + col * 2713 + 7)
    return mixed, small_mod(mixed * mixed)


def sign_of(square):
    tenth = square * 0.1 + 0.05
    return jnp.where(tenth - jnp.floor(tenth) < 0.5, 1.0, -1.0)


STEP = 16
SHIFT = (1103 * STEP) % PRIME


def wrap(value):
    return jnp.where(value >= PRIME, value - PRIME, value)


def fill_pattern(col0, out):
    width, columns = out.shape
    mixed, square = square_state(0, col0, (STEP, columns))
    change = small_mod(mixed * (2 * SHIFT % PRIME) + SHIFT * SHIFT % PRIME)
    second = float(2 * SHIFT * SHIFT % PRIME)

    def step(i, state):
        square, change = state
        out[pl.ds(pl.multiple_of(i * STEP, STEP), STEP), :] = sign_of(square).astype(bf16)
        return wrap(square + change), wrap(change + second)

    lax.fori_loop(0, width // STEP, step, (square.astype(f32), change.astype(f32)))


def tangent_body(
    normed, model_bits, head_bits, table, q_ref, k_ref, v_ref, p_ref, wo,
    dq_out, dk_out, r_out, ds_out, send_out, own_out,
    pattern,
):
    heads = q_ref.shape[1] // HEAD_DIM
    half = send_out.shape[1]
    feat = q_ref.shape[1]
    core = lax.axis_index("c")
    fill_pattern((lax.axis_index("yh") * 2 + core) * feat, pattern)
    sign = (2 * model_bits[...] - 1).astype(f32).astype(bf16)
    product = dot(normed[...] * sign, pattern[...])
    r_out[...] = product
    signs = (2 * head_bits[...] - 1).astype(f32)
    d_query = product * signs[0:1, :]
    d_keys = product * signs[1:2, :]
    cosine, sine = table[: table.shape[0] // 2], table[table.shape[0] // 2 :]
    tangents = []
    for h in range(heads):
        dq = rotate(d_query[:, head(h)], cosine, sine).astype(bf16)
        dk = rotate(d_keys[:, head(h)], cosine, sine).astype(bf16)
        dq_out[:, head(h)] = dq
        dk_out[:, head(h)] = dk
        d_scores = dot_nt(
            jnp.concatenate([dq, q_ref[:, head(h)]], axis=1),
            jnp.concatenate([k_ref[:, head(h)], dk], axis=1),
        ) * SCALE
        weights = p_ref[h]
        centred = d_scores - jnp.sum(weights * d_scores, axis=1, keepdims=True)
        ds_out[h] = centred
        tangents.append(dot((weights * centred).astype(bf16), v_ref[:, head(h)]).astype(bf16))
    tangents = jnp.concatenate(tangents, axis=1)
    mine = pl.multiple_of(core * half, half)
    other = pl.multiple_of((1 - core) * half, half)
    send_out[...] = dot(tangents, wo[:, pl.ds(other, half)]).astype(bf16)
    own_out[...] = dot(tangents, wo[:, pl.ds(mine, half)])


def base_body(tokens, targets, loss_weights, base_out, weight_out):
    half = base_out.shape[1]
    length = base_out.shape[0]
    mine = pl.multiple_of(lax.axis_index("c") * half, half)
    base_out[...] = tokens[:, pl.ds(mine, half)].astype(f32) - targets[:, pl.ds(mine, half)].astype(f32)
    weight_out[...] = jnp.broadcast_to(loss_weights[...] * (1.0 / length), (HEAD_DIM, length)).T


def residual_body(near, far, base, weight, out):
    out[...] = ((near[...].astype(f32) + far[...].astype(f32) + base[...]) * weight[:, 0:1]).astype(bf16)


def d_residual_body(near, far, weight, out):
    out[...] = ((near[...].astype(f32) + far[...].astype(f32)) * weight[:, 0:1]).astype(bf16)


def back_of(res_own, res_mate, wo):
    half = res_own.shape[1]
    core = lax.axis_index("c")
    mine = pl.multiple_of(core * half, half)
    other = pl.multiple_of((1 - core) * half, half)
    return (
        dot_nt(res_own[...], wo[:, pl.ds(mine, half)])
        + dot_nt(res_mate[...], wo[:, pl.ds(other, half)])
    ).astype(bf16)


def second_body(res_own, res_mate, wo, q_ref, k_ref, v_ref, dq_ref, dk_ref, p_ref, ds_ref, hq_out, hk_out):
    back = back_of(res_own, res_mate, wo)
    for h in range(q_ref.shape[1] // HEAD_DIM):
        s = head(h)
        weights = p_ref[h]
        u = dot_nt(back[:, s], v_ref[:, s])
        first = weights * (u - jnp.sum(weights * u, axis=1, keepdims=True))
        curved = first * ds_ref[h]
        second = curved - weights * jnp.sum(curved, axis=1, keepdims=True)
        first, second = first.astype(bf16), second.astype(bf16)
        hq_out[:, s] = dot(first, dk_ref[:, s]) + dot(second, k_ref[:, s])
        hk_out[:, s] = dot_tn(first, dq_ref[:, s]) + dot_tn(second, q_ref[:, s])


def third_body(
    res_own, res_mate, wo, q_ref, k_ref, v_ref, p_ref, hq_ref, hk_ref, r_ref, head_bits, table,
    y_out, sum_out,
):
    feat = q_ref.shape[1]
    back = back_of(res_own, res_mate, wo)
    signs = (2 * head_bits[...] - 1).astype(f32)
    cosine, sine = table[: table.shape[0] // 2], table[table.shape[0] // 2 :]
    totals = [0.0, 0.0]
    for h in range(feat // HEAD_DIM):
        s = head(h)
        weights = p_ref[h]
        u = dot_nt(back[:, s], v_ref[:, s])
        first = (weights * (u - jnp.sum(weights * u, axis=1, keepdims=True))).astype(bf16)
        hq = (hq_ref[:, s] + dot(first, k_ref[:, s])) * SCALE
        hk = (hk_ref[:, s] + dot_tn(first, q_ref[:, s])) * SCALE
        product = r_ref[:, s]
        for i, gradient in enumerate((hq, hk)):
            y = rotate(gradient, cosine, -sine) * signs[i : i + 1, s]
            y = y.astype(bf16)
            y_out[:, i * feat + h * HEAD_DIM : i * feat + (h + 1) * HEAD_DIM] = y
            totals[i] = totals[i] + jnp.sum(product * y.astype(f32), axis=0, keepdims=True)
    pair = [jnp.sum(t, axis=1, keepdims=True) for t in totals]
    lane = lax.broadcasted_iota(i32, sum_out.shape, 1)
    sum_out[...] = jnp.where(lane == 0, pair[0], jnp.where(lane == 1, pair[1], 0.0))


def transpose_body(normed, model_bits, own_out, send_out, whole):
    sign = (2 * model_bits[...] - 1).astype(f32).astype(bf16)
    signed = normed[...] * sign
    for i in range(whole.shape[0] // HEAD_DIM):
        whole[i * HEAD_DIM : (i + 1) * HEAD_DIM, :] = signed[:, i * HEAD_DIM : (i + 1) * HEAD_DIM].T
    rows = whole.shape[0] // 32
    xh, xl, z, yl = (lax.axis_index(axis) for axis in DP)
    for out, low in ((own_out, xl), (send_out, 1 - xl)):
        for ez in range(4):
            for ex in range(2):
                for ey in range(2):
                    to_x = 2 * (xh if ex == 0 else 1 - xh) + low
                    to_z = lax.rem(z + ez, 4)
                    to_y = yl if ey == 0 else 1 - yl
                    start = pl.multiple_of(((to_x * 4 + to_z) * 2 + to_y) * rows, rows)
                    at = ((ez * 2 + ex) * 2 + ey) * rows
                    out[at : at + rows, :] = whole[pl.ds(start, rows), :]


def estimate_body(x_own, x_mate, y_own, y_mate, sums, a0, a1, a2, a3, b0, b1, b2, b3):
    group = b0.shape[0]
    rows = group // 4
    feat = b0.shape[1]
    pieces = jnp.concatenate(
        [part for part in split3(sums[...])] + [jnp.zeros((sums.shape[0], HEAD_DIM), bf16)], axis=1
    )
    for ez, out in enumerate((a0, a1, a2, a3)):
        at = slice(ez * group, (ez + 1) * group)
        part = dot(x_own[at, :], y_own[...]) + dot(x_mate[at, :], y_mate[...])
        if ez == 0:
            out[...] = part[:, :feat]
        else:
            out[:group, :] = part[:, :feat].astype(bf16)
            out[group:, :] = pieces
        for e, to in enumerate((b0, b1, b2, b3)):
            to[ez * rows : (ez + 1) * rows, :] = part[e * rows : (e + 1) * rows, feat:].astype(to.dtype)


def read_sums(part):
    return sum(part[:, i * HEAD_DIM : (i + 1) * HEAD_DIM].astype(f32) for i in range(3))


def middle_body(a0, a1, a2, a3, b0, b1, b2, b3, sums, *outs):
    group = b0.shape[0]
    rows = group // 4
    a = a0[...] + sum(r[:group, :].astype(f32) for r in (a1, a2, a3))
    b = b0[...] + sum(r[...].astype(f32) for r in (b1, b2, b3))
    total = sums[...] + sum(read_sums(r[group:, :]) for r in (a1, a2, a3))
    pieces = jnp.concatenate(list(split3(total)) + [jnp.zeros(total.shape, bf16)], axis=1)
    a_outs, b_outs, sum_out = outs[:4], outs[4:8], outs[8]
    for e, out in enumerate(a_outs):
        part = a[e * rows : (e + 1) * rows, :]
        if e == 0:
            out[...] = part
        else:
            out[:rows, :] = part.astype(bf16)
            out[rows:, :] = pieces
    for e, out in enumerate(b_outs):
        out[...] = b[e * rows : (e + 1) * rows, :].astype(out.dtype)
    sum_out[...] = total


def final_body(a0, a1, a2, a3, b0, b1, b2, b3, sums, diag_query, diag_key, mean_out, *, groups, entries):
    rows, feat = b0.shape
    xh, xl, z, yl = (lax.axis_index(axis) for axis in DP)
    row0 = (((xh * 2 + xl) * 4 + z) * 2 + yl) * rows
    col0 = (lax.axis_index("yh") * 2 + lax.axis_index("c")) * feat
    _, square = square_state(row0, col0, (rows, feat))
    sign = sign_of(square.astype(f32)) * (1.0 / groups)
    diag_query[...] = sign * (a0[...] + sum(r[:rows, :].astype(f32) for r in (a1, a2, a3)))
    diag_key[...] = sign * (b0[...] + sum(r[...].astype(f32) for r in (b1, b2, b3)))
    total = sums[...] + sum(read_sums(r[rows:, :]) for r in (a1, a2, a3))
    mean_out[...] = total * (1.0 / (groups * entries))


def flip(value, moves):
    axes = tuple(axis for axis, _ in moves)
    sizes = [lax.axis_size(axis) for axis in axes]

    def target(index):
        where = []
        for size in reversed(sizes):
            where.append(index % size)
            index //= size
        where = [f(w) for (_, f), w in zip(moves, reversed(where))]
        result = 0
        for w, size in zip(where, sizes):
            result = result * size + w
        return result

    count = int(np.prod(sizes))
    return lax.ppermute(value, axes if len(axes) > 1 else axes[0], [(i, target(i)) for i in range(count)])


def xor(axis, mask):
    return (axis, lambda i: i ^ mask)


def add(axis, k):
    return (axis, lambda i: (i + k) % lax.axis_size(axis))


def local(tokens, targets, loss_weights, segments, probe_model, probe_heads, norm_gain, w_query, w_key, w_value, w_out):
    length, width = tokens.shape
    feat = w_query.shape[1]
    heads = feat // HEAD_DIM
    half = width // 2
    groups = lax.axis_size(DP)
    entries = width * feat * lax.axis_size(MP)
    table = jnp.asarray(np.concatenate(rope_tables(length)))
    head_bits = probe_heads[0]
    mat = shape((length, feat), bf16)
    square = shape((heads, length, length), f32)
    half16, half32 = shape((length, half), bf16), shape((length, half), f32)
    product = 2 * length * width * feat
    small = 2 * length * length * HEAD_DIM * heads
    weight = pltpu.VMEM((width, feat), bf16)

    normed, q, k, v, p, send, own = call(
        forward_body,
        (shape((length, width), bf16), mat, mat, mat, square, half16, half32),
        [HBM] * 8,
        [
            pltpu.VMEM((length, width), bf16), pltpu.VMEM((1, width), f32), weight, weight,
            pltpu.VMEM((2 * length, HEAD_DIM), f32), pltpu.VMEM((1, length), i32),
            weight, pltpu.VMEM((feat, width), bf16), pltpu.SemaphoreType.DMA((8,)),
        ],
        4 * product + 4 * small, 12 * MIB, 50,
    )(tokens, norm_gain[None, :], w_query, w_key, table, segments, w_value, w_out)
    mate = [xor("c", 1)]
    far = [xor("yh", 1)]
    pair = [xor("xl", 1)]
    came = flip(send, mate)
    x_own, x_send = call(
        transpose_body,
        (shape((width // 2, length), bf16),) * 2,
        [VMEM] * 2,
        [pltpu.VMEM((width, length), bf16)],
        0, 3 * MIB, 16,
    )(normed, probe_model)
    x_mate = flip(x_send, pair)
    near = (own + came.astype(f32)).astype(bf16)
    there = flip(near, far)

    dq, dk, r, ds, d_send, d_own = call(
        tangent_body,
        (mat, mat, shape((length, feat), f32), square, half16, half32),
        [VMEM] * 9,
        [pltpu.VMEM((width, feat), bf16)],
        2 * product + 4 * small, 8 * MIB, 32, (near, x_send),
    )(normed, probe_model, head_bits, table, q, k, v, p, w_out)
    d_near = (d_own + flip(d_send, mate).astype(f32)).astype(bf16)
    d_there = flip(d_near, far)

    base, row_weight = call(
        base_body,
        (half32, shape((length, HEAD_DIM), f32)),
        [VMEM] * 3,
        (), 0, 3 * MIB, 16, (d_own,),
    )(tokens, targets, loss_weights[None, :])

    res_own = call(residual_body, half16, [VMEM] * 4, (), 0, 3 * MIB, 16, (d_near, x_mate))(near, there, base, row_weight)
    res_mate = flip(res_own, mate)
    hq, hk = call(
        second_body,
        (shape((length, feat), f32),) * 2,
        [VMEM] * 10,
        (), product + 5 * small, 6 * MIB, 24,
    )(res_own, res_mate, w_out, q, k, v, dq, dk, p, ds)

    d_res_own = call(d_residual_body, half16, [VMEM] * 3, (), 0, 2 * MIB, 16, (hq,))(d_near, d_there, row_weight)
    d_res_mate = flip(d_res_own, mate)
    y, sums = call(
        third_body,
        (shape((length, 2 * feat), bf16), shape((16, HEAD_DIM), f32)),
        [VMEM] * 12,
        (), product + 3 * small, 6 * MIB, 24,
    )(d_res_own, d_res_mate, w_out, q, k, v, p, hq, hk, r, head_bits, table)

    y_mate = flip(y, pair)
    sums = sums + flip(sums, mate)
    sums = sums + flip(sums, far) + flip(sums, pair) + flip(sums, pair + far)

    rows = width // 32
    group = 4 * rows
    a_out, b_out = shape((group + 16, feat), bf16), shape((group, feat), bf16)
    keep = shape((group, feat), f32)
    parts = call(
        estimate_body,
        (keep, a_out, a_out, a_out, keep, b_out, b_out, b_out),
        [VMEM] * 5,
        (), 2 * product, 6 * MIB, 24,
    )(x_own, x_mate, y, y_mate, sums)
    along = [[add("z", 1)], [add("z", 2)], [add("z", 3)]]
    across = [[xor("yl", 1)], [xor("xh", 1)], [xor("xh", 1), xor("yl", 1)]]
    a_in = [flip(m, where) for m, where in zip(parts[1:4], along)]
    b_in = [flip(m, where) for m, where in zip(parts[5:8], across)]
    a_out, b_out = shape((rows + 16, feat), bf16), shape((rows, feat), bf16)
    keep = shape((rows, feat), f32)
    parts = call(
        middle_body,
        (keep, a_out, a_out, a_out, keep, b_out, b_out, b_out, shape((16, HEAD_DIM), f32)),
        [VMEM] * 9,
        (), 0, 3 * MIB, 24,
    )(parts[0], *a_in, parts[4], *b_in, sums)
    a_in = [flip(m, where) for m, where in zip(parts[1:4], across)]
    b_in = [flip(m, where) for m, where in zip(parts[5:8], along)]
    diag_query, diag_key, mean = call(
        functools.partial(final_body, groups=groups, entries=entries),
        (keep, keep, shape((16, HEAD_DIM), f32)),
        [VMEM] * 9,
        (), 0, MIB, 16,
    )(parts[0], *a_in, parts[4], *b_in, parts[8])
    return diag_query, diag_key, mean[0, :2]


def solution(mesh):
    torus = Mesh(mesh.devices.reshape(2, 2, 4, 2, 2, 2), ("xh", "xl", "z", "yl", "yh", "c"))
    return jax.shard_map(
        local,
        mesh=torus,
        in_specs=(
            P(DP, None),
            P(DP, None),
            P(DP),
            P(DP, None),
            P(DP, None),
            P(DP, None, MP),
            P(),
            P(None, MP),
            P(None, MP),
            P(None, MP),
            P(MP, None),
        ),
        out_specs=(P(DP, MP), P(DP, MP), P()),
        check_vma=False,
    )
```

```python
import functools

import jax
import jax.numpy as jnp
import numpy as np
from jax import lax
from jax.experimental import pallas as pl
from jax.experimental.pallas import tpu as pltpu
from jax.sharding import Mesh
from jax.sharding import PartitionSpec as P


HEAD_DIM = 128
PRIME = 32749
EPSILON = 1e-06
SCALE = HEAD_DIM**-0.5
MIB = 1 << 20
DP = ("x", "z", "yl")
MP = ("yh", "c")
bf16, f32, i32 = jnp.bfloat16, jnp.float32, jnp.int32
VMEM = pl.BlockSpec(memory_space=pltpu.VMEM)
ANY = pl.BlockSpec(memory_space=pl.ANY)
HBM = pl.BlockSpec(memory_space=pltpu.HBM)


def shape(dims, kind):
    return jax.ShapeDtypeStruct(dims, kind)


def call(body, outs, ins, scratch=(), flops=0, moved=0, limit=24, after=()):
    count = len(ins)

    def whole(*refs):
        return body(*refs[:count], *refs[count + len(after) :])

    kernel = pl.pallas_call(
        whole,
        out_shape=outs,
        in_specs=list(ins) + [ANY] * len(after),
        out_specs=jax.tree.map(lambda _: VMEM, outs),
        scratch_shapes=scratch,
        cost_estimate=pl.CostEstimate(flops=flops, bytes_accessed=moved, transcendentals=0),
        compiler_params=pltpu.CompilerParams(vmem_limit_bytes=limit * MIB),
    )

    def run(*args):
        return kernel(*args, *after)

    return run


def in_hbm(value):
    return pltpu.with_memory_space_constraint(value, pltpu.HBM)


def dot(a, b):
    return jnp.dot(a, b, preferred_element_type=f32)


def dot_nt(a, b):
    return lax.dot_general(a, b, (((1,), (1,)), ((), ())), preferred_element_type=f32)


def dot_tn(a, b):
    return lax.dot_general(a, b, (((0,), (0,)), ((), ())), preferred_element_type=f32)


def head(h):
    return slice(h * HEAD_DIM, (h + 1) * HEAD_DIM)


def rotate(x, cosine, sine):
    return x * cosine + pltpu.roll(x, HEAD_DIM // 2, 1) * sine


def rope_tables(length):
    position = np.arange(length, dtype=np.float32)
    exponent = np.arange(0, HEAD_DIM, 2, dtype=np.float32) / np.float32(HEAD_DIM)
    frequency = np.power(10000.0, -exponent.astype(np.float64)).astype(np.float32)
    angles = (position[:, None] * frequency[None, :]).astype(np.float64)
    cosine, sine = np.cos(angles), np.sin(angles)
    return (
        np.concatenate([cosine, cosine], axis=1).astype(np.float32),
        np.concatenate([-sine, sine], axis=1).astype(np.float32),
    )


def split3(value):
    high = value.astype(bf16)
    rest = value - high.astype(f32)
    middle = rest.astype(bf16)
    low = (rest - middle.astype(f32)).astype(bf16)
    return high, middle, low


def pieces_of(value):
    return jnp.concatenate(list(split3(value)) + [jnp.zeros(value.shape, bf16)], axis=1)


def read_sums(part):
    return sum(part[:, i * HEAD_DIM : (i + 1) * HEAD_DIM].astype(f32) for i in range(3))


def in_pairs(own, first, second, third):
    return (own + second) + (first + third)


def forward_body(
    tok_hbm, gain_hbm, wq_hbm, wk_hbm, table_hbm, seg_hbm, wv_hbm, wo_hbm,
    normed_out, q_out, k_out, v_out, p_out, send_out, own_out,
    tok, gain, wq, wk, table, seg, wv, wo, sems,
):
    sources = (tok_hbm, gain_hbm, wq_hbm, wk_hbm, table_hbm, seg_hbm, wv_hbm, wo_hbm)
    places = (tok, gain, wq, wk, table, seg, wv, wo)
    copies = [pltpu.make_async_copy(s, d, sems.at[i]) for i, (s, d) in enumerate(zip(sources, places))]
    for copy in copies[:3]:
        copy.start()
    length = tok.shape[0]
    heads = q_out.shape[1] // HEAD_DIM
    half = send_out.shape[1]
    core = lax.axis_index("c")
    copies[0].wait()
    for copy in copies[3:]:
        copy.start()
    copies[1].wait()
    tokens = tok[...].astype(f32)
    inverse = lax.rsqrt(jnp.mean(tokens * tokens, axis=1, keepdims=True) + EPSILON)
    normed = (tokens * inverse * gain[...]).astype(bf16)
    normed_out[...] = normed
    copies[2].wait()
    query = dot(normed, wq[...])
    copies[3].wait()
    keys = dot(normed, wk[...])
    for copy in copies[4:7]:
        copy.wait()
    values = dot(normed, wv[...]).astype(bf16)
    v_out[...] = values
    document = jnp.broadcast_to(seg[...].astype(f32), (length, length))
    row = lax.broadcasted_iota(i32, (length, length), 0)
    col = lax.broadcasted_iota(i32, (length, length), 1)
    allowed = (row >= col) & (document == document.T)
    attended = []
    for h in range(heads):
        q = rotate(query[:, head(h)], table[:length], table[length:])
        k = rotate(keys[:, head(h)], table[:length], table[length:])
        q_high, k_high = q.astype(bf16), k.astype(bf16)
        q_low = (q - q_high.astype(f32)).astype(bf16)
        k_low = (k - k_high.astype(f32)).astype(bf16)
        q_out[:, head(h)] = q_high
        k_out[:, head(h)] = k_high
        scores = dot_nt(
            jnp.concatenate([q_high, q_low], axis=1), jnp.concatenate([k_high, k_high], axis=1)
        ) + dot_nt(q_high, k_low)
        raised = jnp.where(allowed, jnp.exp(scores * SCALE), 0.0)
        weights = raised * (1.0 / jnp.sum(raised, axis=1, keepdims=True))
        p_out[h] = weights
        attended.append(dot(weights.astype(bf16), values[:, head(h)]).astype(bf16))
    attended = jnp.concatenate(attended, axis=1)
    copies[7].wait()
    mine = pl.multiple_of(core * half, half)
    other = pl.multiple_of((1 - core) * half, half)
    send_out[...] = dot(attended, wo[:, pl.ds(other, half)]).astype(bf16)
    own_out[...] = dot(attended, wo[:, pl.ds(mine, half)])


def small_mod(value):
    estimate = jnp.floor(value.astype(f32) * (1.0 / PRIME)).astype(i32)
    rest = value - estimate * PRIME
    rest = jnp.where(rest < 0, rest + PRIME, rest)
    return jnp.where(rest >= PRIME, rest - PRIME, rest)


def square_state(row0, col0, dims):
    row = row0 + lax.broadcasted_iota(i32, dims, 0)
    col = col0 + lax.broadcasted_iota(i32, dims, 1)
    mixed = small_mod(row * 1103 + col * 2713 + 7)
    return mixed, small_mod(mixed * mixed)


def sign_of(square):
    tenth = square * 0.1 + 0.05
    return jnp.where(tenth - jnp.floor(tenth) < 0.5, 1.0, -1.0)


STEP = 16
SHIFT = (1103 * STEP) % PRIME


def wrap(value):
    return jnp.where(value >= PRIME, value - PRIME, value)


def fill_pattern(col0, out):
    width, columns = out.shape
    mixed, square = square_state(0, col0, (STEP, columns))
    change = small_mod(mixed * (2 * SHIFT % PRIME) + SHIFT * SHIFT % PRIME)
    second = float(2 * SHIFT * SHIFT % PRIME)

    def step(i, state):
        square, change = state
        out[pl.ds(pl.multiple_of(i * STEP, STEP), STEP), :] = sign_of(square).astype(bf16)
        return wrap(square + change), wrap(change + second)

    lax.fori_loop(0, width // STEP, step, (square.astype(f32), change.astype(f32)))


def tangent_body(
    normed, model_bits, head_bits, table, q_ref, k_ref, v_ref, p_ref, wo,
    dq_out, dk_out, r_out, ds_out, send_out, own_out,
    pattern,
):
    heads = q_ref.shape[1] // HEAD_DIM
    half = send_out.shape[1]
    feat = q_ref.shape[1]
    core = lax.axis_index("c")
    fill_pattern((lax.axis_index("yh") * 2 + core) * feat, pattern)
    sign = (2 * model_bits[...] - 1).astype(f32).astype(bf16)
    product = dot(normed[...] * sign, pattern[...])
    r_out[...] = product
    signs = (2 * head_bits[...] - 1).astype(f32)
    d_query = product * signs[0:1, :]
    d_keys = product * signs[1:2, :]
    cosine, sine = table[: table.shape[0] // 2], table[table.shape[0] // 2 :]
    tangents = []
    for h in range(heads):
        dq = rotate(d_query[:, head(h)], cosine, sine).astype(bf16)
        dk = rotate(d_keys[:, head(h)], cosine, sine).astype(bf16)
        dq_out[:, head(h)] = dq
        dk_out[:, head(h)] = dk
        d_scores = dot_nt(
            jnp.concatenate([dq, q_ref[:, head(h)]], axis=1),
            jnp.concatenate([k_ref[:, head(h)], dk], axis=1),
        ) * SCALE
        weights = p_ref[h]
        centred = d_scores - jnp.sum(weights * d_scores, axis=1, keepdims=True)
        ds_out[h] = centred
        tangents.append(dot((weights * centred).astype(bf16), v_ref[:, head(h)]).astype(bf16))
    tangents = jnp.concatenate(tangents, axis=1)
    mine = pl.multiple_of(core * half, half)
    other = pl.multiple_of((1 - core) * half, half)
    send_out[...] = dot(tangents, wo[:, pl.ds(other, half)]).astype(bf16)
    own_out[...] = dot(tangents, wo[:, pl.ds(mine, half)])


def base_body(tokens, targets, loss_weights, base_out, weight_out):
    half = base_out.shape[1]
    length = base_out.shape[0]
    mine = pl.multiple_of(lax.axis_index("c") * half, half)
    base_out[...] = tokens[:, pl.ds(mine, half)].astype(f32) - targets[:, pl.ds(mine, half)].astype(f32)
    weight_out[...] = jnp.broadcast_to(loss_weights[...] * (1.0 / length), (HEAD_DIM, length)).T


def residual_body(near, far, base, weight, out):
    out[...] = ((near[...].astype(f32) + far[...].astype(f32) + base[...]) * weight[:, 0:1]).astype(bf16)


def d_residual_body(near, far, weight, out):
    out[...] = ((near[...].astype(f32) + far[...].astype(f32)) * weight[:, 0:1]).astype(bf16)


def back_of(res_own, res_mate, wo):
    half = res_own.shape[1]
    core = lax.axis_index("c")
    mine = pl.multiple_of(core * half, half)
    other = pl.multiple_of((1 - core) * half, half)
    return (
        dot_nt(res_own[...], wo[:, pl.ds(mine, half)])
        + dot_nt(res_mate[...], wo[:, pl.ds(other, half)])
    ).astype(bf16)


def second_body(res_own, res_mate, wo, q_ref, k_ref, v_ref, dq_ref, dk_ref, p_ref, ds_ref, hq_out, hk_out):
    back = back_of(res_own, res_mate, wo)
    for h in range(q_ref.shape[1] // HEAD_DIM):
        s = head(h)
        weights = p_ref[h]
        u = dot_nt(back[:, s], v_ref[:, s])
        first = weights * (u - jnp.sum(weights * u, axis=1, keepdims=True))
        curved = first * ds_ref[h]
        second = curved - weights * jnp.sum(curved, axis=1, keepdims=True)
        first, second = first.astype(bf16), second.astype(bf16)
        hq_out[:, s] = dot(first, dk_ref[:, s]) + dot(second, k_ref[:, s])
        hk_out[:, s] = dot_tn(first, dq_ref[:, s]) + dot_tn(second, q_ref[:, s])


def third_body(
    res_own, res_mate, wo, q_ref, k_ref, v_ref, p_ref, hq_ref, hk_ref, r_ref, head_bits, table,
    yq_out, yk_out, sum_out,
):
    feat = q_ref.shape[1]
    back = back_of(res_own, res_mate, wo)
    signs = (2 * head_bits[...] - 1).astype(f32)
    cosine, sine = table[: table.shape[0] // 2], table[table.shape[0] // 2 :]
    totals = [0.0, 0.0]
    for h in range(feat // HEAD_DIM):
        s = head(h)
        weights = p_ref[h]
        u = dot_nt(back[:, s], v_ref[:, s])
        first = (weights * (u - jnp.sum(weights * u, axis=1, keepdims=True))).astype(bf16)
        hq = (hq_ref[:, s] + dot(first, k_ref[:, s])) * SCALE
        hk = (hk_ref[:, s] + dot_tn(first, q_ref[:, s])) * SCALE
        product = r_ref[:, s]
        for i, (gradient, y_out) in enumerate(((hq, yq_out), (hk, yk_out))):
            y = rotate(gradient, cosine, -sine) * signs[i : i + 1, s]
            y = y.astype(bf16)
            y_out[: y.shape[0], s] = y
            totals[i] = totals[i] + jnp.sum(product * y.astype(f32), axis=0, keepdims=True)
    pair = [jnp.sum(t, axis=1, keepdims=True) for t in totals]
    lane = lax.broadcasted_iota(i32, sum_out.shape, 1)
    total = jnp.where(lane == 0, pair[0], jnp.where(lane == 1, pair[1], 0.0))
    sum_out[...] = total
    yq_out[yk_out.shape[0] :, :] = pieces_of(total)


def transpose_body(normed, model_bits, *refs):
    outs, whole = refs[:8], refs[8]
    sign = (2 * model_bits[...] - 1).astype(f32).astype(bf16)
    signed = normed[...] * sign
    for i in range(whole.shape[0] // HEAD_DIM):
        whole[i * HEAD_DIM : (i + 1) * HEAD_DIM, :] = signed[:, i * HEAD_DIM : (i + 1) * HEAD_DIM].T
    rows = whole.shape[0] // 32
    x, z, yl = (lax.axis_index(axis) for axis in DP)
    for which in range(2):
        for far in range(4):
            for step in range(4):
                to_x = lax.rem(x + (step if which == 0 else far), 4)
                to_z = lax.rem(z + (far if which == 0 else step), 4)
                for ey in range(2):
                    to_y = yl if ey == 0 else 1 - yl
                    start = pl.multiple_of(((to_x * 4 + to_z) * 2 + to_y) * rows, rows)
                    at = (step * 2 + ey) * rows
                    outs[which * 4 + far][at : at + rows, :] = whole[pl.ds(start, rows), :]


def rows_times(x_parts, y_parts):
    length = x_parts[0].shape[1]
    return sum(dot(a[...], b[:length, :]) for a, b in zip(x_parts, y_parts))


def estimate_q_body(*refs):
    y_parts, sums, outs, sum_out = refs[4:8], refs[8], refs[9:13], refs[13]
    length = refs[0].shape[1]
    group = outs[0].shape[0]
    total = in_pairs(sums[...], *(read_sums(y[length:, :]) for y in y_parts[1:]))
    sum_out[...] = total
    whole = rows_times(refs[:4], y_parts)
    for step, out in enumerate(outs):
        out[:group, :] = whole[step * group : (step + 1) * group, :].astype(out.dtype)
        if step > 0:
            out[group:, :] = pieces_of(total)


def estimate_k_body(*refs):
    outs = refs[8:]
    group = outs[0].shape[0]
    whole = rows_times(refs[:4], refs[4:8])
    for step, out in enumerate(outs):
        out[...] = whole[step * group : (step + 1) * group, :].astype(out.dtype)


def middle_body(a0, a1, a2, a3, b0, b1, b2, b3, sums, keep, send, sum_out):
    group, feat = b0.shape
    rows = group // 2
    a = a0[...] + sum(r[:group, :].astype(f32) for r in (a1, a2, a3))
    b = b0[...] + sum(r[...].astype(f32) for r in (b1, b2, b3))
    keep[:, :feat] = a[:rows, :]
    keep[:, feat:] = b[:rows, :]
    send[:, :feat] = a[rows:, :].astype(bf16)
    send[:, feat:] = b[rows:, :].astype(bf16)
    sum_out[...] = in_pairs(sums[...], *(read_sums(r[group:, :]) for r in (a1, a2, a3)))


def final_body(keep, came, s0, s1, s2, s3, diag_query, diag_key, mean_out, *, groups, entries):
    rows, feat = diag_query.shape
    x, z, yl = (lax.axis_index(axis) for axis in DP)
    row0 = ((x * 4 + z) * 2 + yl) * rows
    col0 = (lax.axis_index("yh") * 2 + lax.axis_index("c")) * feat
    _, square = square_state(row0, col0, (rows, feat))
    sign = sign_of(square.astype(f32)) * (1.0 / groups)
    diag_query[...] = sign * (keep[:, :feat] + came[:, :feat].astype(f32))
    diag_key[...] = sign * (keep[:, feat:] + came[:, feat:].astype(f32))
    mean_out[...] = in_pairs(s0[...], s1[...], s2[...], s3[...]) * (1.0 / (groups * entries))


def flip(value, moves):
    axes = tuple(axis for axis, _ in moves)
    sizes = [lax.axis_size(axis) for axis in axes]

    def target(index):
        where = []
        for size in reversed(sizes):
            where.append(index % size)
            index //= size
        where = [f(w) for (_, f), w in zip(moves, reversed(where))]
        result = 0
        for w, size in zip(where, sizes):
            result = result * size + w
        return result

    count = int(np.prod(sizes))
    return lax.ppermute(value, axes if len(axes) > 1 else axes[0], [(i, target(i)) for i in range(count)])


def xor(axis, mask):
    return (axis, lambda i: i ^ mask)


def add(axis, k):
    return (axis, lambda i: (i + k) % lax.axis_size(axis))


def local(tokens, targets, loss_weights, segments, probe_model, probe_heads, norm_gain, w_query, w_key, w_value, w_out):
    length, width = tokens.shape
    feat = w_query.shape[1]
    heads = feat // HEAD_DIM
    half = width // 2
    groups = lax.axis_size(DP)
    entries = width * feat * lax.axis_size(MP)
    table = jnp.asarray(np.concatenate(rope_tables(length)))
    head_bits = probe_heads[0]
    mat = shape((length, feat), bf16)
    square = shape((heads, length, length), f32)
    half16, half32 = shape((length, half), bf16), shape((length, half), f32)
    product = 2 * length * width * feat
    small = 2 * length * length * HEAD_DIM * heads
    weight = pltpu.VMEM((width, feat), bf16)

    normed, q, k, v, p, send, own = call(
        forward_body,
        (shape((length, width), bf16), mat, mat, mat, square, half16, half32),
        [HBM] * 8,
        [
            pltpu.VMEM((length, width), bf16), pltpu.VMEM((1, width), f32), weight, weight,
            pltpu.VMEM((2 * length, HEAD_DIM), f32), pltpu.VMEM((1, length), i32),
            weight, pltpu.VMEM((feat, width), bf16), pltpu.SemaphoreType.DMA((8,)),
        ],
        4 * product + 4 * small, 12 * MIB, 32,
    )(*map(in_hbm, (tokens, norm_gain[None, :], w_query, w_key, table, segments, w_value, w_out)))
    mate = [xor("c", 1)]
    far = [xor("yh", 1)]
    came = flip(send, mate)
    along_z, along_x = [[add("z", i)] for i in (1, 2, 3)], [[add("x", i)] for i in (1, 2, 3)]
    sends = call(
        transpose_body,
        (shape((width // 4, length), bf16),) * 8,
        [VMEM] * 2,
        [pltpu.VMEM((width, length), bf16)],
        0, 3 * MIB, 16,
    )(normed, probe_model)
    near = (own + came.astype(f32)).astype(bf16)
    there = flip(near, far)

    dq, dk, r, ds, d_send, d_own = call(
        tangent_body,
        (mat, mat, shape((length, feat), f32), square, half16, half32),
        [VMEM] * 9,
        [pltpu.VMEM((width, feat), bf16)],
        2 * product + 4 * small, 8 * MIB, 32, (near, sends[0]),
    )(normed, probe_model, head_bits, table, q, k, v, p, w_out)
    d_near = (d_own + flip(d_send, mate).astype(f32)).astype(bf16)
    d_there = flip(d_near, far)
    xq = [sends[0]] + [flip(m, where) for m, where in zip(sends[1:4], along_z)]
    xk = [sends[4]] + [flip(m, where) for m, where in zip(sends[5:8], along_x)]

    base, row_weight = call(
        base_body,
        (half32, shape((length, HEAD_DIM), f32)),
        [VMEM] * 3,
        (), 0, 3 * MIB, 16, (d_own,),
    )(tokens, targets, loss_weights[None, :])

    res_own = call(residual_body, half16, [VMEM] * 4, (), 0, 3 * MIB, 16, (d_near,))(near, there, base, row_weight)
    res_mate = flip(res_own, mate)
    hq, hk = call(
        second_body,
        (shape((length, feat), f32),) * 2,
        [VMEM] * 10,
        (), product + 5 * small, 6 * MIB, 24,
    )(res_own, res_mate, w_out, q, k, v, dq, dk, p, ds)

    d_res_own = call(d_residual_body, half16, [VMEM] * 3, (), 0, 2 * MIB, 16, (hq,))(d_near, d_there, row_weight)
    d_res_mate = flip(d_res_own, mate)
    yq, yk, sums = call(
        third_body,
        (shape((length + 16, feat), bf16), mat, shape((16, HEAD_DIM), f32)),
        [VMEM] * 12,
        (), product + 3 * small, 6 * MIB, 24,
    )(d_res_own, d_res_mate, w_out, q, k, v, p, hq, hk, r, head_bits, table)
    yq_in = [yq] + [flip(yq, where) for where in along_z]
    yk_in = [yk] + [flip(yk, where) for where in along_x]

    rows = width // 32
    group = 2 * rows
    a_out, b_out = shape((group + 16, feat), bf16), shape((group, feat), bf16)
    keep = shape((group, feat), f32)
    *parts, sums = call(
        estimate_q_body,
        (keep, a_out, a_out, a_out, shape((16, HEAD_DIM), f32)),
        [VMEM] * 9,
        (), product, 3 * MIB, 24,
    )(*xq, *yq_in, sums)
    parts += call(
        estimate_k_body,
        (keep, b_out, b_out, b_out),
        [VMEM] * 8,
        (), product, 3 * MIB, 24,
    )(*xk, *yk_in)
    a_in, b_in = [], []
    for i in range(3):
        a_in.append(flip(parts[1 + i], along_x[i]))
        b_in.append(flip(parts[5 + i], along_z[i]))
    keep, send, sums = call(
        middle_body,
        (shape((rows, 2 * feat), f32), shape((rows, 2 * feat), bf16), shape((16, HEAD_DIM), f32)),
        [VMEM] * 9,
        (), 0, 3 * MIB, 24,
    )(parts[0], *a_in, parts[4], *b_in, sums)
    side = [xor("yl", 1)]
    came = flip(send, side)
    sums = sums + flip(sums, mate)
    sums = [sums] + [flip(sums, where) for where in (far, side, side + far)]
    diag_query, diag_key, mean = call(
        functools.partial(final_body, groups=groups, entries=entries),
        (shape((rows, feat), f32), shape((rows, feat), f32), shape((16, HEAD_DIM), f32)),
        [VMEM] * 6,
        (), 0, MIB, 16,
    )(keep, came, *sums)
    return diag_query, diag_key, mean[0, :2]


def solution(mesh):
    torus = Mesh(mesh.devices.reshape(4, 4, 2, 2, 2), ("x", "z", "yl", "yh", "c"))
    return jax.shard_map(
        local,
        mesh=torus,
        in_specs=(
            P(DP, None),
            P(DP, None),
            P(DP),
            P(DP, None),
            P(DP, None),
            P(DP, None, MP),
            P(),
            P(None, MP),
            P(None, MP),
            P(None, MP),
            P(MP, None),
        ),
        out_specs=(P(DP, MP), P(DP, MP), P()),
        check_vma=False,
    )
```

```python
import functools

import jax
import jax.numpy as jnp
import numpy as np
from jax import lax
from jax.experimental import pallas as pl
from jax.experimental.pallas import tpu as pltpu
from jax.sharding import Mesh
from jax.sharding import PartitionSpec as P


HEAD_DIM = 128
PRIME = 32749
EPSILON = 1e-06
SCALE = HEAD_DIM**-0.5
MIB = 1 << 20
DP = ("x", "z", "yl")
MP = ("yh", "c")
bf16, f32, i32 = jnp.bfloat16, jnp.float32, jnp.int32
VMEM = pl.BlockSpec(memory_space=pltpu.VMEM)
ANY = pl.BlockSpec(memory_space=pl.ANY)
HBM = pl.BlockSpec(memory_space=pltpu.HBM)
SMEM = pl.BlockSpec(memory_space=pltpu.SMEM)


def shape(dims, kind):
    return jax.ShapeDtypeStruct(dims, kind)


def call(body, outs, ins, scratch=(), flops=0, moved=0, limit=24, after=()):
    count = len(ins)

    def whole(*refs):
        return body(*refs[:count], *refs[count + len(after) :])

    kernel = pl.pallas_call(
        whole,
        out_shape=outs,
        in_specs=list(ins) + [ANY] * len(after),
        out_specs=jax.tree.map(lambda out: VMEM if len(out.shape) > 1 else SMEM, outs),
        scratch_shapes=scratch,
        cost_estimate=pl.CostEstimate(flops=flops, bytes_accessed=moved, transcendentals=0),
        compiler_params=pltpu.CompilerParams(vmem_limit_bytes=limit * MIB),
    )

    def run(*args):
        return kernel(*args, *after)

    return run


def in_hbm(value):
    return pltpu.with_memory_space_constraint(value, pltpu.HBM)


def dot(a, b):
    return jnp.dot(a, b, preferred_element_type=f32)


def dot_nt(a, b):
    return lax.dot_general(a, b, (((1,), (1,)), ((), ())), preferred_element_type=f32)


def dot_tn(a, b):
    return lax.dot_general(a, b, (((0,), (0,)), ((), ())), preferred_element_type=f32)


def head(h):
    return slice(h * HEAD_DIM, (h + 1) * HEAD_DIM)


def rotate(x, cosine, sine):
    return x * cosine + pltpu.roll(x, HEAD_DIM // 2, 1) * sine


def rope_tables(length):
    position = np.arange(length, dtype=np.float32)
    exponent = np.arange(0, HEAD_DIM, 2, dtype=np.float32) / np.float32(HEAD_DIM)
    frequency = np.power(10000.0, -exponent.astype(np.float64)).astype(np.float32)
    angles = (position[:, None] * frequency[None, :]).astype(np.float64)
    cosine, sine = np.cos(angles), np.sin(angles)
    return (
        np.concatenate([cosine, cosine], axis=1).astype(np.float32),
        np.concatenate([-sine, sine], axis=1).astype(np.float32),
    )


def split3(value):
    high = value.astype(bf16)
    rest = value - high.astype(f32)
    middle = rest.astype(bf16)
    low = (rest - middle.astype(f32)).astype(bf16)
    return high, middle, low


def pieces_of(value, columns):
    pieces = split3(value)
    blank = columns // value.shape[1] - len(pieces)
    return jnp.concatenate([*pieces] + [jnp.zeros(value.shape, bf16)] * blank, axis=1)


def read_sums(part):
    return sum(part[:, i * HEAD_DIM : (i + 1) * HEAD_DIM].astype(f32) for i in range(3))


def in_pairs(own, first, second, third):
    return (own + second) + (first + third)


def forward_body(
    tok_hbm, gain_hbm, wq_hbm, wk_hbm, table_hbm, seg_hbm, wv_hbm, wo_hbm,
    normed_out, q_out, k_out, v_out, p_out, send_out, own_out,
    tok, gain, wq, wk, table, seg, wv, wo, sems,
):
    sources = (tok_hbm, gain_hbm, wq_hbm, wk_hbm, table_hbm, seg_hbm, wv_hbm, wo_hbm)
    places = (tok, gain, wq, wk, table, seg, wv, wo)
    copies = [pltpu.make_async_copy(s, d, sems.at[i]) for i, (s, d) in enumerate(zip(sources, places))]
    for copy in copies[:3]:
        copy.start()
    length = tok.shape[0]
    heads = q_out.shape[1] // HEAD_DIM
    half = send_out.shape[1]
    core = lax.axis_index("c")
    copies[0].wait()
    for copy in copies[3:]:
        copy.start()
    copies[1].wait()
    tokens = tok[...].astype(f32)
    inverse = lax.rsqrt(jnp.mean(tokens * tokens, axis=1, keepdims=True) + EPSILON)
    normed = (tokens * inverse * gain[...]).astype(bf16)
    normed_out[...] = normed
    copies[2].wait()
    query = dot(normed, wq[...])
    copies[3].wait()
    keys = dot(normed, wk[...])
    for copy in copies[4:7]:
        copy.wait()
    values = dot(normed, wv[...]).astype(bf16)
    v_out[...] = values
    document = jnp.broadcast_to(seg[...].astype(f32), (length, length))
    row = lax.broadcasted_iota(i32, (length, length), 0)
    col = lax.broadcasted_iota(i32, (length, length), 1)
    allowed = (row >= col) & (document == document.T)
    attended = []
    for h in range(heads):
        q = rotate(query[:, head(h)], table[:length], table[length:])
        k = rotate(keys[:, head(h)], table[:length], table[length:])
        q_high, k_high = q.astype(bf16), k.astype(bf16)
        q_low = (q - q_high.astype(f32)).astype(bf16)
        k_low = (k - k_high.astype(f32)).astype(bf16)
        q_out[:, head(h)] = q_high
        k_out[:, head(h)] = k_high
        scores = dot_nt(
            jnp.concatenate([q_high, q_low], axis=1), jnp.concatenate([k_high, k_high], axis=1)
        ) + dot_nt(q_high, k_low)
        raised = jnp.where(allowed, jnp.exp(scores * SCALE), 0.0)
        weights = raised * (1.0 / jnp.sum(raised, axis=1, keepdims=True))
        p_out[h] = weights
        attended.append(dot(weights.astype(bf16), values[:, head(h)]).astype(bf16))
    attended = jnp.concatenate(attended, axis=1)
    copies[7].wait()
    mine = pl.multiple_of(core * half, half)
    other = pl.multiple_of((1 - core) * half, half)
    send_out[...] = dot(attended, wo[:, pl.ds(other, half)]).astype(bf16)
    own_out[...] = dot(attended, wo[:, pl.ds(mine, half)])


def small_mod(value):
    estimate = jnp.floor(value.astype(f32) * (1.0 / PRIME)).astype(i32)
    rest = value - estimate * PRIME
    rest = jnp.where(rest < 0, rest + PRIME, rest)
    return jnp.where(rest >= PRIME, rest - PRIME, rest)


def square_state(row0, col0, dims):
    row = row0 + lax.broadcasted_iota(i32, dims, 0)
    col = col0 + lax.broadcasted_iota(i32, dims, 1)
    mixed = small_mod(row * 1103 + col * 2713 + 7)
    return mixed, small_mod(mixed * mixed)


def sign_of(square):
    tenth = square * 0.1 + 0.05
    return jnp.where(tenth - jnp.floor(tenth) < 0.5, 1.0, -1.0)


STEP = 16
SHIFT = (1103 * STEP) % PRIME


def wrap(value):
    return jnp.where(value >= PRIME, value - PRIME, value)


def fill_pattern(col0, out):
    width, columns = out.shape
    mixed, square = square_state(0, col0, (STEP, columns))
    change = small_mod(mixed * (2 * SHIFT % PRIME) + SHIFT * SHIFT % PRIME)
    second = float(2 * SHIFT * SHIFT % PRIME)

    def step(i, state):
        square, change = state
        out[pl.ds(pl.multiple_of(i * STEP, STEP), STEP), :] = sign_of(square).astype(bf16)
        return wrap(square + change), wrap(change + second)

    lax.fori_loop(0, width // STEP, step, (square.astype(f32), change.astype(f32)))


def tangent_body(
    normed, model_bits, head_bits, table, q_ref, k_ref, v_ref, p_ref, wo,
    dq_out, dk_out, r_out, ds_out, send_out, own_out,
    pattern,
):
    heads = q_ref.shape[1] // HEAD_DIM
    half = send_out.shape[1]
    feat = q_ref.shape[1]
    core = lax.axis_index("c")
    fill_pattern((lax.axis_index("yh") * 2 + core) * feat, pattern)
    sign = (2 * model_bits[...] - 1).astype(f32).astype(bf16)
    product = dot(normed[...] * sign, pattern[...])
    r_out[...] = product
    signs = (2 * head_bits[...] - 1).astype(f32)
    d_query = product * signs[0:1, :]
    d_keys = product * signs[1:2, :]
    cosine, sine = table[: table.shape[0] // 2], table[table.shape[0] // 2 :]
    tangents = []
    for h in range(heads):
        dq = rotate(d_query[:, head(h)], cosine, sine).astype(bf16)
        dk = rotate(d_keys[:, head(h)], cosine, sine).astype(bf16)
        dq_out[:, head(h)] = dq
        dk_out[:, head(h)] = dk
        d_scores = dot_nt(
            jnp.concatenate([dq, q_ref[:, head(h)]], axis=1),
            jnp.concatenate([k_ref[:, head(h)], dk], axis=1),
        ) * SCALE
        weights = p_ref[h]
        centred = d_scores - jnp.sum(weights * d_scores, axis=1, keepdims=True)
        ds_out[h] = centred
        tangents.append(dot((weights * centred).astype(bf16), v_ref[:, head(h)]).astype(bf16))
    tangents = jnp.concatenate(tangents, axis=1)
    mine = pl.multiple_of(core * half, half)
    other = pl.multiple_of((1 - core) * half, half)
    send_out[...] = dot(tangents, wo[:, pl.ds(other, half)]).astype(bf16)
    own_out[...] = dot(tangents, wo[:, pl.ds(mine, half)])


def base_body(tokens, targets, loss_weights, base_out, weight_out, sign_out, *, groups):
    half = base_out.shape[1]
    length = base_out.shape[0]
    mine = pl.multiple_of(lax.axis_index("c") * half, half)
    base_out[...] = tokens[:, pl.ds(mine, half)].astype(f32) - targets[:, pl.ds(mine, half)].astype(f32)
    weight_out[...] = jnp.broadcast_to(loss_weights[...] * (1.0 / length), (HEAD_DIM, length)).T
    rows, feat = sign_out.shape
    x, z, yl = (lax.axis_index(axis) for axis in DP)
    row0 = ((x * 4 + z) * 2 + yl) * rows
    col0 = (lax.axis_index("yh") * 2 + lax.axis_index("c")) * feat
    _, square = square_state(row0, col0, (rows, feat))
    sign_out[...] = sign_of(square.astype(f32)) * (1.0 / groups)


def residual_body(near, far, base, weight, out):
    out[...] = ((near[...].astype(f32) + far[...].astype(f32) + base[...]) * weight[:, 0:1]).astype(bf16)


def d_residual_body(near, far, weight, out):
    out[...] = ((near[...].astype(f32) + far[...].astype(f32)) * weight[:, 0:1]).astype(bf16)


def back_of(res_own, res_mate, wo):
    half = res_own.shape[1]
    core = lax.axis_index("c")
    mine = pl.multiple_of(core * half, half)
    other = pl.multiple_of((1 - core) * half, half)
    return (
        dot_nt(res_own[...], wo[:, pl.ds(mine, half)])
        + dot_nt(res_mate[...], wo[:, pl.ds(other, half)])
    ).astype(bf16)


def second_body(res_own, res_mate, wo, q_ref, k_ref, v_ref, dq_ref, dk_ref, p_ref, ds_ref, hq_out, hk_out):
    back = back_of(res_own, res_mate, wo)
    for h in range(q_ref.shape[1] // HEAD_DIM):
        s = head(h)
        weights = p_ref[h]
        u = dot_nt(back[:, s], v_ref[:, s])
        first = weights * (u - jnp.sum(weights * u, axis=1, keepdims=True))
        curved = first * ds_ref[h]
        second = curved - weights * jnp.sum(curved, axis=1, keepdims=True)
        first, second = first.astype(bf16), second.astype(bf16)
        hq_out[:, s] = dot(first, dk_ref[:, s]) + dot(second, k_ref[:, s])
        hk_out[:, s] = dot_tn(first, dq_ref[:, s]) + dot_tn(second, q_ref[:, s])


def third_body(
    res_own, res_mate, wo, q_ref, k_ref, v_ref, p_ref, hq_ref, hk_ref, r_ref, head_bits, table,
    ya_out, yb_out, sum_out,
):
    feat = q_ref.shape[1]
    back = back_of(res_own, res_mate, wo)
    signs = (2 * head_bits[...] - 1).astype(f32)
    cosine, sine = table[: table.shape[0] // 2], table[table.shape[0] // 2 :]
    totals = [0.0, 0.0]
    for h in range(feat // HEAD_DIM):
        s = head(h)
        weights = p_ref[h]
        u = dot_nt(back[:, s], v_ref[:, s])
        first = (weights * (u - jnp.sum(weights * u, axis=1, keepdims=True))).astype(bf16)
        hq = (hq_ref[:, s] + dot(first, k_ref[:, s])) * SCALE
        hk = (hk_ref[:, s] + dot_tn(first, q_ref[:, s])) * SCALE
        product = r_ref[:, s]
        for i, gradient in enumerate((hq, hk)):
            y = rotate(gradient, cosine, -sine) * signs[i : i + 1, s]
            y = y.astype(bf16)
            column, cut = i * feat + h * HEAD_DIM, ya_out.shape[1]
            if column < cut:
                ya_out[:, column : column + HEAD_DIM] = y
            else:
                yb_out[:, column - cut : column - cut + HEAD_DIM] = y
            totals[i] = totals[i] + jnp.sum(product * y.astype(f32), axis=0, keepdims=True)
    pair = [jnp.sum(t, axis=1, keepdims=True) for t in totals]
    lane = lax.broadcasted_iota(i32, sum_out.shape, 1)
    total = jnp.where(lane == 0, pair[0], jnp.where(lane == 1, pair[1], 0.0))
    sum_out[...] = total


def stamp_body(y, near, far, out, sum_out):
    length = y.shape[0]
    total = near[...] + far[...]
    sum_out[...] = total
    out[:length, :] = y[...]
    out[length:, :] = pieces_of(total, out.shape[1])


def transpose_body(normed, model_bits, *refs):
    outs, whole = refs[:8], refs[8]
    sign = (2 * model_bits[...] - 1).astype(f32).astype(bf16)
    signed = normed[...] * sign
    for i in range(whole.shape[0] // HEAD_DIM):
        whole[i * HEAD_DIM : (i + 1) * HEAD_DIM, :] = signed[:, i * HEAD_DIM : (i + 1) * HEAD_DIM].T
    rows = whole.shape[0] // 32
    x, z, yl = (lax.axis_index(axis) for axis in DP)
    for which in range(2):
        for far in range(4):
            for step in range(4):
                to_x = lax.rem(x + (step if which == 0 else far), 4)
                to_z = lax.rem(z + (far if which == 0 else step), 4)
                for ey in range(2):
                    to_y = yl if ey == 0 else 1 - yl
                    start = pl.multiple_of(((to_x * 4 + to_z) * 2 + to_y) * rows, rows)
                    at = (step * 2 + ey) * rows
                    outs[which * 4 + far][at : at + rows, :] = whole[pl.ds(start, rows), :]


def rows_times(x_parts, y_parts):
    length = x_parts[0].shape[1]
    return sum(dot(a[...], b[:length, :]) for a, b in zip(x_parts, y_parts))


def estimate_a_body(*refs):
    outs = refs[8:]
    group = outs[0].shape[0]
    whole = rows_times(refs[:4], refs[4:8])
    for step, out in enumerate(outs):
        out[...] = whole[step * group : (step + 1) * group, :].astype(out.dtype)


def estimate_b_body(*refs):
    y_parts, sums, outs, sum_out = refs[4:8], refs[8], refs[9:13], refs[13]
    length = refs[0].shape[1]
    group = outs[0].shape[0]
    total = in_pairs(sums[...], *(read_sums(y[length:, :]) for y in y_parts[1:]))
    sum_out[...] = total
    whole = rows_times(refs[:4], y_parts)
    for step, out in enumerate(outs):
        out[:group, :] = whole[step * group : (step + 1) * group, :].astype(out.dtype)
        if step > 0:
            out[group:, :] = pieces_of(total, out.shape[1])


def middle_body(a0, a1, a2, a3, b0, b1, b2, b3, sums, keep, send, sum_out):
    group, cut = a0.shape
    rows = group // 2
    a = a0[...] + sum(r[...].astype(f32) for r in (a1, a2, a3))
    b = b0[...] + sum(r[:group, :].astype(f32) for r in (b1, b2, b3))
    keep[:, :cut] = a[:rows, :]
    keep[:, cut:] = b[:rows, :]
    send[:rows, :cut] = a[rows:, :].astype(bf16)
    send[:rows, cut:] = b[rows:, :].astype(bf16)
    total = in_pairs(sums[...], *(read_sums(r[group:, :]) for r in (b1, b2, b3)))
    sum_out[...] = total
    send[rows:, :] = pieces_of(total, send.shape[1])


def final_body(keep, came, sums, sign, diag_query, diag_key, mean_out, *, count):
    rows, feat = diag_query.shape
    diag_query[...] = sign[...] * (keep[:, :feat] + came[:rows, :feat].astype(f32))
    diag_key[...] = sign[...] * (keep[:, feat:] + came[:rows, feat:].astype(f32))
    total = sums[...] + read_sums(came[rows:, :])
    lane = lax.broadcasted_iota(i32, (1, total.shape[1]), 1)
    for i in range(2):
        mean_out[i] = jnp.sum(jnp.where(lane == i, total[0:1, :], 0.0)) * (1.0 / count)


def flip(value, moves):
    axes = tuple(axis for axis, _ in moves)
    sizes = [lax.axis_size(axis) for axis in axes]

    def target(index):
        where = []
        for size in reversed(sizes):
            where.append(index % size)
            index //= size
        where = [f(w) for (_, f), w in zip(moves, reversed(where))]
        result = 0
        for w, size in zip(where, sizes):
            result = result * size + w
        return result

    count = int(np.prod(sizes))
    return lax.ppermute(value, axes if len(axes) > 1 else axes[0], [(i, target(i)) for i in range(count)])


def xor(axis, mask):
    return (axis, lambda i: i ^ mask)


def add(axis, k):
    return (axis, lambda i: (i + k) % lax.axis_size(axis))


def local(tokens, targets, loss_weights, segments, probe_model, probe_heads, norm_gain, w_query, w_key, w_value, w_out):
    length, width = tokens.shape
    feat = w_query.shape[1]
    heads = feat // HEAD_DIM
    half = width // 2
    groups = lax.axis_size(DP)
    entries = width * feat * lax.axis_size(MP)
    table = jnp.asarray(np.concatenate(rope_tables(length)))
    head_bits = probe_heads[0]
    mat = shape((length, feat), bf16)
    square = shape((heads, length, length), f32)
    half16, half32 = shape((length, half), bf16), shape((length, half), f32)
    product = 2 * length * width * feat
    small = 2 * length * length * HEAD_DIM * heads
    weight = pltpu.VMEM((width, feat), bf16)

    normed, q, k, v, p, send, own = call(
        forward_body,
        (shape((length, width), bf16), mat, mat, mat, square, half16, half32),
        [HBM] * 8,
        [
            pltpu.VMEM((length, width), bf16), pltpu.VMEM((1, width), f32), weight, weight,
            pltpu.VMEM((2 * length, HEAD_DIM), f32), pltpu.VMEM((1, length), i32),
            weight, pltpu.VMEM((feat, width), bf16), pltpu.SemaphoreType.DMA((8,)),
        ],
        4 * product + 4 * small, 12 * MIB, 32,
    )(*map(in_hbm, (tokens, norm_gain[None, :], w_query, w_key, table, segments, w_value, w_out)))
    mate = [xor("c", 1)]
    far = [xor("yh", 1)]
    came = flip(send, mate)
    along_z, along_x = [[add("z", i)] for i in (1, 2, 3)], [[add("x", i)] for i in (1, 2, 3)]
    sends = call(
        transpose_body,
        (shape((width // 4, length), bf16),) * 8,
        [VMEM] * 2,
        [pltpu.VMEM((width, length), bf16)],
        0, 3 * MIB, 16,
    )(normed, probe_model)
    near = (own + came.astype(f32)).astype(bf16)
    there = flip(near, far)

    dq, dk, r, ds, d_send, d_own = call(
        tangent_body,
        (mat, mat, shape((length, feat), f32), square, half16, half32),
        [VMEM] * 9,
        [pltpu.VMEM((width, feat), bf16)],
        2 * product + 4 * small, 8 * MIB, 32, (near, sends[0]),
    )(normed, probe_model, head_bits, table, q, k, v, p, w_out)
    d_near = (d_own + flip(d_send, mate).astype(f32)).astype(bf16)
    d_there = flip(d_near, far)
    xq = [sends[0]] + [flip(m, where) for m, where in zip(sends[1:4], along_z)]
    xk = [sends[4]] + [flip(m, where) for m, where in zip(sends[5:8], along_x)]

    rows = width // 32
    base, row_weight, sign = call(
        functools.partial(base_body, groups=groups),
        (half32, shape((length, HEAD_DIM), f32), shape((rows, feat), f32)),
        [VMEM] * 3,
        (), 0, 3 * MIB, 16, (d_own,),
    )(tokens, targets, loss_weights[None, :])

    res_own = call(residual_body, half16, [VMEM] * 4, (), 0, 3 * MIB, 16, (d_near,))(near, there, base, row_weight)
    res_mate = flip(res_own, mate)
    hq, hk = call(
        second_body,
        (shape((length, feat), f32),) * 2,
        [VMEM] * 10,
        (), product + 5 * small, 6 * MIB, 24,
    )(res_own, res_mate, w_out, q, k, v, dq, dk, p, ds)

    d_res_own = call(d_residual_body, half16, [VMEM] * 3, (), 0, 2 * MIB, 16, (hq,))(d_near, d_there, row_weight)
    d_res_mate = flip(d_res_own, mate)
    cut = 5 * feat // 4
    rest = 2 * feat - cut
    small_sums = shape((16, HEAD_DIM), f32)
    ya, yb, sums = call(
        third_body,
        (shape((length, cut), bf16), shape((length, rest), bf16), small_sums),
        [VMEM] * 12,
        (), product + 3 * small, 6 * MIB, 24,
    )(d_res_own, d_res_mate, w_out, q, k, v, p, hq, hk, r, head_bits, table)
    ya_in = [ya] + [flip(ya, where) for where in along_z]
    sums = sums + flip(sums, mate)
    yb, sums = call(stamp_body, (shape((length + 16, rest), bf16), small_sums), [VMEM] * 3, (), 0, MIB, 16)(
        yb, sums, flip(sums, far)
    )
    yb_in = [yb] + [flip(yb, where) for where in along_x]

    group = 2 * rows
    part, keep = shape((group, cut), bf16), shape((group, cut), f32)
    a = call(
        estimate_a_body,
        (keep, part, part, part),
        [VMEM] * 8,
        (), product, 3 * MIB, 24,
    )(*xq, *ya_in)
    part, keep = shape((group + 16, rest), bf16), shape((group, rest), f32)
    *b, sums = call(
        estimate_b_body,
        (keep, part, part, part, small_sums),
        [VMEM] * 9,
        (), product, 3 * MIB, 24,
    )(*xk, *yb_in, sums)
    a_in = [flip(part, where) for part, where in zip(a[1:], along_x)]
    b_in = [flip(part, where) for part, where in zip(b[1:], along_z)]
    keep, send, sums = call(
        middle_body,
        (shape((rows, 2 * feat), f32), shape((rows + 16, 2 * feat), bf16), small_sums),
        [VMEM] * 9,
        (), 0, 3 * MIB, 24,
    )(a[0], *a_in, b[0], *b_in, sums)
    diag_query, diag_key, mean = call(
        functools.partial(final_body, count=groups * entries),
        (shape((rows, feat), f32), shape((rows, feat), f32), shape((2,), f32)),
        [VMEM] * 4,
        (), 0, MIB, 16,
    )(keep, flip(send, [xor("yl", 1)]), sums, sign)
    return diag_query, diag_key, mean


def solution(mesh):
    torus = Mesh(mesh.devices.reshape(4, 4, 2, 2, 2), ("x", "z", "yl", "yh", "c"))
    return jax.shard_map(
        local,
        mesh=torus,
        in_specs=(
            P(DP, None),
            P(DP, None),
            P(DP),
            P(DP, None),
            P(DP, None),
            P(DP, None, MP),
            P(),
            P(None, MP),
            P(None, MP),
            P(None, MP),
            P(MP, None),
        ),
        out_specs=(P(DP, MP), P(DP, MP), P()),
        check_vma=False,
    )
```

```python
import functools

import jax
import jax.numpy as jnp
import numpy as np
from jax import lax
from jax.experimental import pallas as pl
from jax.experimental.pallas import tpu as pltpu
from jax.sharding import Mesh
from jax.sharding import PartitionSpec as P


HEAD_DIM = 128
PRIME = 32749
EPSILON = 1e-06
SCALE = HEAD_DIM**-0.5
MIB = 1 << 20
DP = ("x", "z", "yl")
MP = ("yh", "c")
bf16, f32, i32 = jnp.bfloat16, jnp.float32, jnp.int32
VMEM = pl.BlockSpec(memory_space=pltpu.VMEM)
ANY = pl.BlockSpec(memory_space=pl.ANY)
HBM = pl.BlockSpec(memory_space=pltpu.HBM)
SMEM = pl.BlockSpec(memory_space=pltpu.SMEM)


def shape(dims, kind):
    return jax.ShapeDtypeStruct(dims, kind)


def call(body, outs, ins, scratch=(), flops=0, moved=0, limit=24, after=()):
    count = len(ins)

    def whole(*refs):
        return body(*refs[:count], *refs[count + len(after) :])

    kernel = pl.pallas_call(
        whole,
        out_shape=outs,
        in_specs=list(ins) + [ANY] * len(after),
        out_specs=jax.tree.map(lambda out: VMEM if len(out.shape) > 1 else SMEM, outs),
        scratch_shapes=scratch,
        cost_estimate=pl.CostEstimate(flops=flops, bytes_accessed=moved, transcendentals=0),
        compiler_params=pltpu.CompilerParams(vmem_limit_bytes=limit * MIB),
    )

    def run(*args):
        return kernel(*args, *after)

    return run


def in_hbm(value):
    return pltpu.with_memory_space_constraint(value, pltpu.HBM)


def dot(a, b):
    return jnp.dot(a, b, preferred_element_type=f32)


def dot_nt(a, b):
    return lax.dot_general(a, b, (((1,), (1,)), ((), ())), preferred_element_type=f32)


def dot_tn(a, b):
    return lax.dot_general(a, b, (((0,), (0,)), ((), ())), preferred_element_type=f32)


def head(h):
    return slice(h * HEAD_DIM, (h + 1) * HEAD_DIM)


def rotate(x, cosine, sine):
    return x * cosine + pltpu.roll(x, HEAD_DIM // 2, 1) * sine


def rope_tables(length):
    position = np.arange(length, dtype=np.float32)
    exponent = np.arange(0, HEAD_DIM, 2, dtype=np.float32) / np.float32(HEAD_DIM)
    frequency = np.power(10000.0, -exponent.astype(np.float64)).astype(np.float32)
    angles = (position[:, None] * frequency[None, :]).astype(np.float64)
    cosine, sine = np.cos(angles), np.sin(angles)
    return (
        np.concatenate([cosine, cosine], axis=1).astype(np.float32),
        np.concatenate([-sine, sine], axis=1).astype(np.float32),
    )


def split3(value):
    high = value.astype(bf16)
    rest = value - high.astype(f32)
    middle = rest.astype(bf16)
    low = (rest - middle.astype(f32)).astype(bf16)
    return high, middle, low


def pieces_of(value, columns):
    pieces = split3(value)
    blank = columns // value.shape[1] - len(pieces)
    return jnp.concatenate([*pieces] + [jnp.zeros(value.shape, bf16)] * blank, axis=1)


def read_sums(part):
    return sum(part[:, i * HEAD_DIM : (i + 1) * HEAD_DIM].astype(f32) for i in range(3))


def in_pairs(own, first, second, third):
    return (own + second) + (first + third)


def columns_of(half, own):
    core = lax.axis_index("c")
    return pl.ds(pl.multiple_of((core if own else 1 - core) * half, half), half)


def forward_body(
    tok_hbm, gain_hbm, wq_hbm, wk_hbm, table_hbm, seg_hbm, wv_hbm, wo_hbm,
    normed_out, q_out, k_out, v_out, p_out, send_out, attended_out, wo,
    tok, gain, wq, wk, table, seg, wv, sems,
):
    sources = (tok_hbm, gain_hbm, wq_hbm, wk_hbm, table_hbm, seg_hbm, wv_hbm, wo_hbm)
    places = (tok, gain, wq, wk, table, seg, wv, wo)
    copies = [pltpu.make_async_copy(s, d, sems.at[i]) for i, (s, d) in enumerate(zip(sources, places))]
    for copy in copies[:3]:
        copy.start()
    length = tok.shape[0]
    heads = q_out.shape[1] // HEAD_DIM
    half = send_out.shape[1]
    copies[0].wait()
    for copy in copies[3:]:
        copy.start()
    copies[1].wait()
    tokens = tok[...].astype(f32)
    inverse = lax.rsqrt(jnp.mean(tokens * tokens, axis=1, keepdims=True) + EPSILON)
    normed = (tokens * inverse * gain[...]).astype(bf16)
    normed_out[...] = normed
    copies[2].wait()
    query = dot(normed, wq[...])
    copies[3].wait()
    keys = dot(normed, wk[...])
    for copy in copies[4:7]:
        copy.wait()
    values = dot(normed, wv[...]).astype(bf16)
    v_out[...] = values
    document = jnp.broadcast_to(seg[...].astype(f32), (length, length))
    row = lax.broadcasted_iota(i32, (length, length), 0)
    col = lax.broadcasted_iota(i32, (length, length), 1)
    allowed = (row >= col) & (document == document.T)
    attended = []
    for h in range(heads):
        q = rotate(query[:, head(h)], table[:length], table[length:])
        k = rotate(keys[:, head(h)], table[:length], table[length:])
        q_high, k_high = q.astype(bf16), k.astype(bf16)
        q_low = (q - q_high.astype(f32)).astype(bf16)
        k_low = (k - k_high.astype(f32)).astype(bf16)
        q_out[:, head(h)] = q_high
        k_out[:, head(h)] = k_high
        scores = dot_nt(
            jnp.concatenate([q_high, q_low], axis=1), jnp.concatenate([k_high, k_high], axis=1)
        ) + dot_nt(q_high, k_low)
        raised = jnp.where(allowed, jnp.exp(scores * SCALE), 0.0)
        weights = raised * (1.0 / jnp.sum(raised, axis=1, keepdims=True))
        p_out[h] = weights
        attended.append(dot(weights.astype(bf16), values[:, head(h)]).astype(bf16))
    attended = jnp.concatenate(attended, axis=1)
    copies[7].wait()
    attended_out[...] = attended
    send_out[...] = dot(attended, wo[:, columns_of(half, False)]).astype(bf16)


def out_own_body(attended, wo, out):
    out[...] = dot(attended[...], wo[:, columns_of(out.shape[1], True)])


def small_mod(value):
    estimate = jnp.floor(value.astype(f32) * (1.0 / PRIME)).astype(i32)
    rest = value - estimate * PRIME
    rest = jnp.where(rest < 0, rest + PRIME, rest)
    return jnp.where(rest >= PRIME, rest - PRIME, rest)


def square_state(row0, col0, dims):
    row = row0 + lax.broadcasted_iota(i32, dims, 0)
    col = col0 + lax.broadcasted_iota(i32, dims, 1)
    mixed = small_mod(row * 1103 + col * 2713 + 7)
    return mixed, small_mod(mixed * mixed)


def sign_of(square):
    tenth = square * 0.1 + 0.05
    return jnp.where(tenth - jnp.floor(tenth) < 0.5, 1.0, -1.0)


STEP = 16
SHIFT = (1103 * STEP) % PRIME


def wrap(value):
    return jnp.where(value >= PRIME, value - PRIME, value)


def fill_pattern(col0, out):
    width, columns = out.shape
    mixed, square = square_state(0, col0, (STEP, columns))
    change = small_mod(mixed * (2 * SHIFT % PRIME) + SHIFT * SHIFT % PRIME)
    second = float(2 * SHIFT * SHIFT % PRIME)

    def step(i, state):
        square, change = state
        out[pl.ds(pl.multiple_of(i * STEP, STEP), STEP), :] = sign_of(square).astype(bf16)
        return wrap(square + change), wrap(change + second)

    lax.fori_loop(0, width // STEP, step, (square.astype(f32), change.astype(f32)))


def tangent_body(
    normed, model_bits, head_bits, table, q_ref, k_ref, v_ref, p_ref, wo,
    dq_out, dk_out, r_out, ds_out, send_out, own_out,
    pattern,
):
    heads = q_ref.shape[1] // HEAD_DIM
    half = send_out.shape[1]
    feat = q_ref.shape[1]
    core = lax.axis_index("c")
    fill_pattern((lax.axis_index("yh") * 2 + core) * feat, pattern)
    sign = (2 * model_bits[...] - 1).astype(f32).astype(bf16)
    product = dot(normed[...] * sign, pattern[...])
    r_out[...] = product
    signs = (2 * head_bits[...] - 1).astype(f32)
    d_query = product * signs[0:1, :]
    d_keys = product * signs[1:2, :]
    cosine, sine = table[: table.shape[0] // 2], table[table.shape[0] // 2 :]
    tangents = []
    for h in range(heads):
        dq = rotate(d_query[:, head(h)], cosine, sine).astype(bf16)
        dk = rotate(d_keys[:, head(h)], cosine, sine).astype(bf16)
        dq_out[:, head(h)] = dq
        dk_out[:, head(h)] = dk
        d_scores = dot_nt(
            jnp.concatenate([dq, q_ref[:, head(h)]], axis=1),
            jnp.concatenate([k_ref[:, head(h)], dk], axis=1),
        ) * SCALE
        weights = p_ref[h]
        centred = d_scores - jnp.sum(weights * d_scores, axis=1, keepdims=True)
        ds_out[h] = centred
        tangents.append(dot((weights * centred).astype(bf16), v_ref[:, head(h)]).astype(bf16))
    tangents = jnp.concatenate(tangents, axis=1)
    mine = pl.multiple_of(core * half, half)
    other = pl.multiple_of((1 - core) * half, half)
    send_out[...] = dot(tangents, wo[:, pl.ds(other, half)]).astype(bf16)
    own_out[...] = dot(tangents, wo[:, pl.ds(mine, half)])


def base_body(tokens, targets, loss_weights, base_out, weight_out, sign_out, *, groups):
    half = base_out.shape[1]
    length = base_out.shape[0]
    mine = pl.multiple_of(lax.axis_index("c") * half, half)
    base_out[...] = tokens[:, pl.ds(mine, half)].astype(f32) - targets[:, pl.ds(mine, half)].astype(f32)
    weight_out[...] = jnp.broadcast_to(loss_weights[...] * (1.0 / length), (HEAD_DIM, length)).T
    rows, feat = sign_out.shape
    x, z, yl = (lax.axis_index(axis) for axis in DP)
    row0 = ((x * 4 + z) * 2 + yl) * rows
    col0 = (lax.axis_index("yh") * 2 + lax.axis_index("c")) * feat
    _, square = square_state(row0, col0, (rows, feat))
    sign_out[...] = sign_of(square.astype(f32)) * (1.0 / groups)


def residual_body(near, far, base, weight, out):
    out[...] = ((near[...].astype(f32) + far[...].astype(f32) + base[...]) * weight[:, 0:1]).astype(bf16)


def d_residual_body(near, far, weight, out):
    out[...] = ((near[...].astype(f32) + far[...].astype(f32)) * weight[:, 0:1]).astype(bf16)


def back_of(res_own, res_mate, wo):
    half = res_own.shape[1]
    own = dot_nt(res_own[...], wo[:, columns_of(half, True)])
    return (own + dot_nt(res_mate[...], wo[:, columns_of(half, False)])).astype(bf16)


def back_own_body(res_own, wo, out):
    out[...] = dot_nt(res_own[...], wo[:, columns_of(res_own.shape[1], True)])


def second_body(res_own, res_mate, wo, q_ref, k_ref, v_ref, dq_ref, dk_ref, p_ref, ds_ref, hq_out, hk_out):
    back = back_of(res_own, res_mate, wo)
    for h in range(q_ref.shape[1] // HEAD_DIM):
        s = head(h)
        weights = p_ref[h]
        u = dot_nt(back[:, s], v_ref[:, s])
        first = weights * (u - jnp.sum(weights * u, axis=1, keepdims=True))
        curved = first * ds_ref[h]
        second = curved - weights * jnp.sum(curved, axis=1, keepdims=True)
        first, second = first.astype(bf16), second.astype(bf16)
        hq_out[:, s] = dot(first, dk_ref[:, s]) + dot(second, k_ref[:, s])
        hk_out[:, s] = dot_tn(first, dq_ref[:, s]) + dot_tn(second, q_ref[:, s])


def third_body(
    back_own, res_mate, wo, q_ref, k_ref, v_ref, p_ref, hq_ref, hk_ref, r_ref, head_bits, table,
    ya_out, yb_out, sum_out,
):
    feat = q_ref.shape[1]
    back = (back_own[...] + dot_nt(res_mate[...], wo[:, columns_of(res_mate.shape[1], False)])).astype(bf16)
    signs = (2 * head_bits[...] - 1).astype(f32)
    cosine, sine = table[: table.shape[0] // 2], table[table.shape[0] // 2 :]
    totals = [0.0, 0.0]
    for h in range(feat // HEAD_DIM):
        s = head(h)
        weights = p_ref[h]
        u = dot_nt(back[:, s], v_ref[:, s])
        first = (weights * (u - jnp.sum(weights * u, axis=1, keepdims=True))).astype(bf16)
        hq = (hq_ref[:, s] + dot(first, k_ref[:, s])) * SCALE
        hk = (hk_ref[:, s] + dot_tn(first, q_ref[:, s])) * SCALE
        product = r_ref[:, s]
        for i, gradient in enumerate((hq, hk)):
            y = rotate(gradient, cosine, -sine) * signs[i : i + 1, s]
            y = y.astype(bf16)
            column, cut = i * feat + h * HEAD_DIM, ya_out.shape[1]
            if column < cut:
                ya_out[:, column : column + HEAD_DIM] = y
            else:
                yb_out[:, column - cut : column - cut + HEAD_DIM] = y
            totals[i] = totals[i] + jnp.sum(product * y.astype(f32), axis=0, keepdims=True)
    pair = [jnp.sum(t, axis=1, keepdims=True) for t in totals]
    lane = lax.broadcasted_iota(i32, sum_out.shape, 1)
    total = jnp.where(lane == 0, pair[0], jnp.where(lane == 1, pair[1], 0.0))
    sum_out[...] = total


def stamp_body(y, near, far, out, sum_out):
    length = y.shape[0]
    total = near[...] + far[...]
    sum_out[...] = total
    out[:length, :] = y[...]
    out[length:, :] = pieces_of(total, out.shape[1])


def transpose_body(normed, model_bits, *refs):
    outs, whole = refs[:8], refs[8]
    sign = (2 * model_bits[...] - 1).astype(f32).astype(bf16)
    signed = normed[...] * sign
    for i in range(whole.shape[0] // HEAD_DIM):
        whole[i * HEAD_DIM : (i + 1) * HEAD_DIM, :] = signed[:, i * HEAD_DIM : (i + 1) * HEAD_DIM].T
    rows = whole.shape[0] // 32
    x, z, yl = (lax.axis_index(axis) for axis in DP)
    for which in range(2):
        for far in range(4):
            for step in range(4):
                to_x = lax.rem(x + (step if which == 0 else far), 4)
                to_z = lax.rem(z + (far if which == 0 else step), 4)
                for ey in range(2):
                    to_y = yl if ey == 0 else 1 - yl
                    start = pl.multiple_of(((to_x * 4 + to_z) * 2 + to_y) * rows, rows)
                    at = (step * 2 + ey) * rows
                    outs[which * 4 + far][at : at + rows, :] = whole[pl.ds(start, rows), :]


def rows_times(x_parts, y_parts):
    length = x_parts[0].shape[1]
    return sum(dot(a[...], b[:length, :]) for a, b in zip(x_parts, y_parts))


def estimate_a_body(*refs):
    outs = refs[8:]
    group = outs[0].shape[0]
    whole = rows_times(refs[:4], refs[4:8])
    for step, out in enumerate(outs):
        out[...] = whole[step * group : (step + 1) * group, :].astype(out.dtype)


def estimate_b_body(*refs):
    y_parts, sums, outs, sum_out = refs[4:8], refs[8], refs[9:13], refs[13]
    length = refs[0].shape[1]
    group = outs[0].shape[0]
    total = in_pairs(sums[...], *(read_sums(y[length:, :]) for y in y_parts[1:]))
    sum_out[...] = total
    whole = rows_times(refs[:4], y_parts)
    for step, out in enumerate(outs):
        out[:group, :] = whole[step * group : (step + 1) * group, :].astype(out.dtype)
        if step > 0:
            out[group:, :] = pieces_of(total, out.shape[1])


def middle_a_body(a0, a1, a2, a3, keep, send):
    rows = keep.shape[0]
    a = a0[...] + sum(r[...].astype(f32) for r in (a1, a2, a3))
    keep[...] = a[:rows, :]
    send[...] = a[rows:, :].astype(bf16)


def middle_b_body(b0, b1, b2, b3, sums, keep, send, sum_out):
    rows = keep.shape[0]
    group = 2 * rows
    b = b0[...] + sum(r[:group, :].astype(f32) for r in (b1, b2, b3))
    keep[...] = b[:rows, :]
    send[:rows, :] = b[rows:, :].astype(bf16)
    total = in_pairs(sums[...], *(read_sums(r[group:, :]) for r in (b1, b2, b3)))
    sum_out[...] = total
    send[rows:, :] = pieces_of(total, send.shape[1])


def final_a_body(keep, came, sign, diag_query, more_out):
    feat = diag_query.shape[1]
    more = more_out.shape[1]
    a = keep[...] + came[...].astype(f32)
    diag_query[...] = sign[...] * a[:, :feat]
    more_out[...] = sign[:, :more] * a[:, feat:]


def final_b_body(more_in, keep, came, sums, sign, diag_key, mean_out, *, count):
    rows = diag_key.shape[0]
    more = more_in.shape[1]
    diag_key[:, :more] = more_in[...]
    diag_key[:, more:] = sign[:, more:] * (keep[...] + came[:rows, :].astype(f32))
    total = sums[...] + read_sums(came[rows:, :])
    lane = lax.broadcasted_iota(i32, (1, total.shape[1]), 1)
    for i in range(2):
        mean_out[i] = jnp.sum(jnp.where(lane == i, total[0:1, :], 0.0)) * (1.0 / count)


def flip(value, moves):
    axes = tuple(axis for axis, _ in moves)
    sizes = [lax.axis_size(axis) for axis in axes]

    def target(index):
        where = []
        for size in reversed(sizes):
            where.append(index % size)
            index //= size
        where = [f(w) for (_, f), w in zip(moves, reversed(where))]
        result = 0
        for w, size in zip(where, sizes):
            result = result * size + w
        return result

    count = int(np.prod(sizes))
    return lax.ppermute(value, axes if len(axes) > 1 else axes[0], [(i, target(i)) for i in range(count)])


def xor(axis, mask):
    return (axis, lambda i: i ^ mask)


def add(axis, k):
    return (axis, lambda i: (i + k) % lax.axis_size(axis))


def local(tokens, targets, loss_weights, segments, probe_model, probe_heads, norm_gain, w_query, w_key, w_value, w_out):
    length, width = tokens.shape
    feat = w_query.shape[1]
    heads = feat // HEAD_DIM
    half = width // 2
    groups = lax.axis_size(DP)
    entries = width * feat * lax.axis_size(MP)
    table = jnp.asarray(np.concatenate(rope_tables(length)))
    head_bits = probe_heads[0]
    mat = shape((length, feat), bf16)
    square = shape((heads, length, length), f32)
    half16, half32 = shape((length, half), bf16), shape((length, half), f32)
    product = 2 * length * width * feat
    small = 2 * length * length * HEAD_DIM * heads
    weight = pltpu.VMEM((width, feat), bf16)

    normed, q, k, v, p, send, attended, w_out = call(
        forward_body,
        (shape((length, width), bf16), mat, mat, mat, square, half16, mat, shape((feat, width), bf16)),
        [HBM] * 8,
        [
            pltpu.VMEM((length, width), bf16), pltpu.VMEM((1, width), f32), weight, weight,
            pltpu.VMEM((2 * length, HEAD_DIM), f32), pltpu.VMEM((1, length), i32),
            weight, pltpu.SemaphoreType.DMA((8,)),
        ],
        4 * product + 4 * small, 12 * MIB, 32,
    )(*map(in_hbm, (tokens, norm_gain[None, :], w_query, w_key, table, segments, w_value, w_out)))
    mate = [xor("c", 1)]
    far = [xor("yh", 1)]
    came = flip(send, mate)
    along_z, along_x = [[add("z", i)] for i in (1, 2, 3)], [[add("x", i)] for i in (1, 2, 3)]
    sends = call(
        transpose_body,
        (shape((width // 4, length), bf16),) * 8,
        [VMEM] * 2,
        [pltpu.VMEM((width, length), bf16)],
        0, 3 * MIB, 16,
    )(normed, probe_model)
    own = call(out_own_body, half32, [VMEM] * 2, (), product // 2, 2 * MIB, 16)(attended, w_out)
    near = (own + came.astype(f32)).astype(bf16)
    there = flip(near, far)

    dq, dk, r, ds, d_send, d_own = call(
        tangent_body,
        (mat, mat, shape((length, feat), f32), square, half16, half32),
        [VMEM] * 9,
        [pltpu.VMEM((width, feat), bf16)],
        2 * product + 4 * small, 8 * MIB, 32, (near, sends[0]),
    )(normed, probe_model, head_bits, table, q, k, v, p, w_out)
    d_near = (d_own + flip(d_send, mate).astype(f32)).astype(bf16)
    d_there = flip(d_near, far)
    xq = [sends[0]] + [flip(m, where) for m, where in zip(sends[1:4], along_z)]
    xk = [sends[4]] + [flip(m, where) for m, where in zip(sends[5:8], along_x)]

    rows = width // 32
    base, row_weight, sign = call(
        functools.partial(base_body, groups=groups),
        (half32, shape((length, HEAD_DIM), f32), shape((rows, feat), f32)),
        [VMEM] * 3,
        (), 0, 3 * MIB, 16, (d_own,),
    )(tokens, targets, loss_weights[None, :])

    res_own = call(residual_body, half16, [VMEM] * 4, (), 0, 3 * MIB, 16, (d_near,))(near, there, base, row_weight)
    res_mate = flip(res_own, mate)
    hq, hk = call(
        second_body,
        (shape((length, feat), f32),) * 2,
        [VMEM] * 10,
        (), product + 5 * small, 6 * MIB, 24,
    )(res_own, res_mate, w_out, q, k, v, dq, dk, p, ds)

    d_res_own = call(d_residual_body, half16, [VMEM] * 3, (), 0, 2 * MIB, 16, (hq,))(d_near, d_there, row_weight)
    d_res_mate = flip(d_res_own, mate)
    back_own = call(
        back_own_body, shape((length, feat), f32), [VMEM] * 2, (), product // 2, 2 * MIB, 16
    )(d_res_own, w_out)
    cut = 5 * feat // 4
    rest = 2 * feat - cut
    small_sums = shape((16, HEAD_DIM), f32)
    ya, yb, sums = call(
        third_body,
        (shape((length, cut), bf16), shape((length, rest), bf16), small_sums),
        [VMEM] * 12,
        (), product + 3 * small, 6 * MIB, 24,
    )(back_own, d_res_mate, w_out, q, k, v, p, hq, hk, r, head_bits, table)
    ya_in = [ya] + [flip(ya, where) for where in along_z]
    sums = sums + flip(sums, mate)
    yb, sums = call(stamp_body, (shape((length + 16, rest), bf16), small_sums), [VMEM] * 3, (), 0, MIB, 16)(
        yb, sums, flip(sums, far)
    )
    yb_in = [yb] + [flip(yb, where) for where in along_x]

    group = 2 * rows
    part, keep = shape((group, cut), bf16), shape((group, cut), f32)
    a = call(
        estimate_a_body,
        (keep, part, part, part),
        [VMEM] * 8,
        (), product, 3 * MIB, 24,
    )(*xq, *ya_in)
    part, keep = shape((group + 16, rest), bf16), shape((group, rest), f32)
    *b, sums = call(
        estimate_b_body,
        (keep, part, part, part, small_sums),
        [VMEM] * 9,
        (), product, 3 * MIB, 24,
    )(*xk, *yb_in, sums)
    a_in = [flip(part, where) for part, where in zip(a[1:], along_x)]
    b_in = [flip(part, where) for part, where in zip(b[1:], along_z)]
    keep_a, send_a = call(
        middle_a_body, (shape((rows, cut), f32), shape((rows, cut), bf16)), [VMEM] * 4, (), 0, MIB, 16
    )(a[0], *a_in)
    keep_b, send_b, sums = call(
        middle_b_body,
        (shape((rows, rest), f32), shape((rows + 16, rest), bf16), small_sums),
        [VMEM] * 5,
        (), 0, MIB, 16,
    )(b[0], *b_in, sums)
    side = [xor("yl", 1)]
    block = shape((rows, feat), f32)
    came_a, came_b = flip(send_a, side), flip(send_b, side)
    diag_query, more = call(
        final_a_body, (block, shape((rows, cut - feat), f32)), [VMEM] * 3, (), 0, MIB, 16
    )(keep_a, came_a, sign)
    diag_key, mean = call(
        functools.partial(final_b_body, count=groups * entries),
        (block, shape((2,), f32)),
        [VMEM] * 5,
        (), 0, MIB, 16,
    )(more, keep_b, came_b, sums, sign)
    return diag_query, diag_key, mean


def solution(mesh):
    torus = Mesh(mesh.devices.reshape(4, 4, 2, 2, 2), ("x", "z", "yl", "yh", "c"))
    return jax.shard_map(
        local,
        mesh=torus,
        in_specs=(
            P(DP, None),
            P(DP, None),
            P(DP),
            P(DP, None),
            P(DP, None),
            P(DP, None, MP),
            P(),
            P(None, MP),
            P(None, MP),
            P(None, MP),
            P(MP, None),
        ),
        out_specs=(P(DP, MP), P(DP, MP), P()),
        check_vma=False,
    )
```

```python
import functools

import jax
import jax.numpy as jnp
import numpy as np
from jax import lax
from jax.experimental import pallas as pl
from jax.experimental.pallas import tpu as pltpu
from jax.sharding import Mesh
from jax.sharding import PartitionSpec as P


HEAD_DIM = 128
PRIME = 32749
EPSILON = 1e-06
SCALE = HEAD_DIM**-0.5
MIB = 1 << 20
DP = ("x", "z", "yl")
MP = ("yh", "c")
bf16, f32, i32 = jnp.bfloat16, jnp.float32, jnp.int32
VMEM = pl.BlockSpec(memory_space=pltpu.VMEM)
ANY = pl.BlockSpec(memory_space=pl.ANY)
HBM = pl.BlockSpec(memory_space=pltpu.HBM)
SMEM = pl.BlockSpec(memory_space=pltpu.SMEM)


def shape(dims, kind):
    return jax.ShapeDtypeStruct(dims, kind)


def call(body, outs, ins, scratch=(), flops=0, moved=0, limit=24, after=()):
    count = len(ins)

    def whole(*refs):
        return body(*refs[:count], *refs[count + len(after) :])

    kernel = pl.pallas_call(
        whole,
        out_shape=outs,
        in_specs=list(ins) + [ANY] * len(after),
        out_specs=jax.tree.map(lambda out: VMEM if len(out.shape) > 1 else SMEM, outs),
        scratch_shapes=scratch,
        cost_estimate=pl.CostEstimate(flops=flops, bytes_accessed=moved, transcendentals=0),
        compiler_params=pltpu.CompilerParams(vmem_limit_bytes=limit * MIB),
    )

    def run(*args):
        return kernel(*args, *after)

    return run


def in_hbm(value):
    return pltpu.with_memory_space_constraint(value, pltpu.HBM)


def dot(a, b):
    return jnp.dot(a, b, preferred_element_type=f32)


def dot_nt(a, b):
    return lax.dot_general(a, b, (((1,), (1,)), ((), ())), preferred_element_type=f32)


def dot_tn(a, b):
    return lax.dot_general(a, b, (((0,), (0,)), ((), ())), preferred_element_type=f32)


def head(h):
    return slice(h * HEAD_DIM, (h + 1) * HEAD_DIM)


def rotate(x, cosine, sine):
    return x * cosine + pltpu.roll(x, HEAD_DIM // 2, 1) * sine


def rope_tables(length):
    position = np.arange(length, dtype=np.float32)
    exponent = np.arange(0, HEAD_DIM, 2, dtype=np.float32) / np.float32(HEAD_DIM)
    frequency = np.power(10000.0, -exponent.astype(np.float64)).astype(np.float32)
    angles = (position[:, None] * frequency[None, :]).astype(np.float64)
    cosine, sine = np.cos(angles), np.sin(angles)
    return (
        np.concatenate([cosine, cosine], axis=1).astype(np.float32),
        np.concatenate([-sine, sine], axis=1).astype(np.float32),
    )


def split3(value):
    high = value.astype(bf16)
    rest = value - high.astype(f32)
    middle = rest.astype(bf16)
    low = (rest - middle.astype(f32)).astype(bf16)
    return high, middle, low


def pieces_of(value, columns):
    pieces = split3(value)
    blank = columns // value.shape[1] - len(pieces)
    return jnp.concatenate([*pieces] + [jnp.zeros(value.shape, bf16)] * blank, axis=1)


def read_sums(part):
    return sum(part[:, i * HEAD_DIM : (i + 1) * HEAD_DIM].astype(f32) for i in range(3))


def in_pairs(own, first, second, third):
    return (own + second) + (first + third)


def columns_of(half, own):
    core = lax.axis_index("c")
    return pl.ds(pl.multiple_of((core if own else 1 - core) * half, half), half)


def forward_body(
    tok_hbm, gain_hbm, wq_hbm, wk_hbm, table_hbm, seg_hbm, wv_hbm, wo_hbm,
    normed_out, q_out, k_out, v_out, p_out, send_out, attended_out, wo,
    tok, gain, wq, wk, table, seg, wv, sems,
):
    sources = (tok_hbm, gain_hbm, wq_hbm, wk_hbm, table_hbm, seg_hbm, wv_hbm, wo_hbm)
    places = (tok, gain, wq, wk, table, seg, wv, wo)
    copies = [pltpu.make_async_copy(s, d, sems.at[i]) for i, (s, d) in enumerate(zip(sources, places))]
    for copy in copies[:3]:
        copy.start()
    length = tok.shape[0]
    heads = q_out.shape[1] // HEAD_DIM
    half = send_out.shape[1]
    copies[0].wait()
    for copy in copies[3:]:
        copy.start()
    copies[1].wait()
    tokens = tok[...].astype(f32)
    inverse = lax.rsqrt(jnp.mean(tokens * tokens, axis=1, keepdims=True) + EPSILON)
    normed = (tokens * inverse * gain[...]).astype(bf16)
    normed_out[...] = normed
    copies[2].wait()
    query = dot(normed, wq[...])
    copies[3].wait()
    keys = dot(normed, wk[...])
    for copy in copies[4:7]:
        copy.wait()
    values = dot(normed, wv[...]).astype(bf16)
    v_out[...] = values
    document = jnp.broadcast_to(seg[...].astype(f32), (length, length))
    row = lax.broadcasted_iota(i32, (length, length), 0)
    col = lax.broadcasted_iota(i32, (length, length), 1)
    allowed = (row >= col) & (document == document.T)
    attended = []
    for h in range(heads):
        q = rotate(query[:, head(h)], table[:length], table[length:])
        k = rotate(keys[:, head(h)], table[:length], table[length:])
        q_high, k_high = q.astype(bf16), k.astype(bf16)
        q_low = (q - q_high.astype(f32)).astype(bf16)
        k_low = (k - k_high.astype(f32)).astype(bf16)
        q_out[:, head(h)] = q_high
        k_out[:, head(h)] = k_high
        scores = dot_nt(
            jnp.concatenate([q_high, q_low], axis=1), jnp.concatenate([k_high, k_high], axis=1)
        ) + dot_nt(q_high, k_low)
        raised = jnp.where(allowed, jnp.exp(scores * SCALE), 0.0)
        weights = raised * (1.0 / jnp.sum(raised, axis=1, keepdims=True))
        p_out[h] = weights
        attended.append(dot(weights.astype(bf16), values[:, head(h)]).astype(bf16))
    attended = jnp.concatenate(attended, axis=1)
    copies[7].wait()
    attended_out[...] = attended
    send_out[...] = dot(attended, wo[:, columns_of(half, False)]).astype(bf16)


def out_own_body(attended, wo, out):
    out[...] = dot(attended[...], wo[:, columns_of(out.shape[1], True)])


def small_mod(value):
    estimate = jnp.floor(value.astype(f32) * (1.0 / PRIME)).astype(i32)
    rest = value - estimate * PRIME
    rest = jnp.where(rest < 0, rest + PRIME, rest)
    return jnp.where(rest >= PRIME, rest - PRIME, rest)


def square_state(row0, col0, dims):
    row = row0 + lax.broadcasted_iota(i32, dims, 0)
    col = col0 + lax.broadcasted_iota(i32, dims, 1)
    mixed = small_mod(row * 1103 + col * 2713 + 7)
    return mixed, small_mod(mixed * mixed)


def sign_of(square):
    tenth = square * 0.1 + 0.05
    return jnp.where(tenth - jnp.floor(tenth) < 0.5, 1.0, -1.0)


STEP = 16
SHIFT = (1103 * STEP) % PRIME


def wrap(value):
    return jnp.where(value >= PRIME, value - PRIME, value)


def fill_pattern(col0, out):
    width, columns = out.shape
    mixed, square = square_state(0, col0, (STEP, columns))
    change = small_mod(mixed * (2 * SHIFT % PRIME) + SHIFT * SHIFT % PRIME)
    second = float(2 * SHIFT * SHIFT % PRIME)

    def step(i, state):
        square, change = state
        out[pl.ds(pl.multiple_of(i * STEP, STEP), STEP), :] = sign_of(square).astype(bf16)
        return wrap(square + change), wrap(change + second)

    lax.fori_loop(0, width // STEP, step, (square.astype(f32), change.astype(f32)))


def tangent_body(
    normed, model_bits, head_bits, table, q_ref, k_ref, v_ref, p_ref, wo,
    dq_out, dk_out, r_out, ds_out, send_out, own_out,
    pattern,
):
    heads = q_ref.shape[1] // HEAD_DIM
    half = send_out.shape[1]
    feat = q_ref.shape[1]
    core = lax.axis_index("c")
    fill_pattern((lax.axis_index("yh") * 2 + core) * feat, pattern)
    sign = (2 * model_bits[...] - 1).astype(f32).astype(bf16)
    product = dot(normed[...] * sign, pattern[...])
    r_out[...] = product
    signs = (2 * head_bits[...] - 1).astype(f32)
    d_query = product * signs[0:1, :]
    d_keys = product * signs[1:2, :]
    cosine, sine = table[: table.shape[0] // 2], table[table.shape[0] // 2 :]
    tangents = []
    for h in range(heads):
        dq = rotate(d_query[:, head(h)], cosine, sine).astype(bf16)
        dk = rotate(d_keys[:, head(h)], cosine, sine).astype(bf16)
        dq_out[:, head(h)] = dq
        dk_out[:, head(h)] = dk
        d_scores = dot_nt(
            jnp.concatenate([dq, q_ref[:, head(h)]], axis=1),
            jnp.concatenate([k_ref[:, head(h)], dk], axis=1),
        ) * SCALE
        weights = p_ref[h]
        centred = d_scores - jnp.sum(weights * d_scores, axis=1, keepdims=True)
        ds_out[h] = centred
        tangents.append(dot((weights * centred).astype(bf16), v_ref[:, head(h)]).astype(bf16))
    tangents = jnp.concatenate(tangents, axis=1)
    mine = pl.multiple_of(core * half, half)
    other = pl.multiple_of((1 - core) * half, half)
    send_out[...] = dot(tangents, wo[:, pl.ds(other, half)]).astype(bf16)
    own_out[...] = dot(tangents, wo[:, pl.ds(mine, half)])


def base_body(tokens, targets, loss_weights, base_out, weight_out, sign_out, *, groups):
    half = base_out.shape[1]
    length = base_out.shape[0]
    mine = pl.multiple_of(lax.axis_index("c") * half, half)
    base_out[...] = tokens[:, pl.ds(mine, half)].astype(f32) - targets[:, pl.ds(mine, half)].astype(f32)
    weight_out[...] = jnp.broadcast_to(loss_weights[...] * (1.0 / length), (HEAD_DIM, length)).T
    rows, feat = sign_out.shape
    x, z, yl = (lax.axis_index(axis) for axis in DP)
    row0 = ((x * 4 + z) * 2 + yl) * rows
    col0 = (lax.axis_index("yh") * 2 + lax.axis_index("c")) * feat
    _, square = square_state(row0, col0, (rows, feat))
    sign_out[...] = sign_of(square.astype(f32)) * (1.0 / groups)


def residual_body(near, far, base, weight, out):
    out[...] = ((near[...].astype(f32) + far[...].astype(f32) + base[...]) * weight[:, 0:1]).astype(bf16)


def d_residual_body(near, far, weight, out):
    out[...] = ((near[...].astype(f32) + far[...].astype(f32)) * weight[:, 0:1]).astype(bf16)


def back_of(res_own, res_mate, wo):
    half = res_own.shape[1]
    own = dot_nt(res_own[...], wo[:, columns_of(half, True)])
    return (own + dot_nt(res_mate[...], wo[:, columns_of(half, False)])).astype(bf16)


def back_own_body(res_own, wo, out):
    out[...] = dot_nt(res_own[...], wo[:, columns_of(res_own.shape[1], True)])


def second_body(res_own, res_mate, wo, q_ref, k_ref, v_ref, dq_ref, dk_ref, p_ref, ds_ref, hq_out, hk_out):
    back = back_of(res_own, res_mate, wo)
    for h in range(q_ref.shape[1] // HEAD_DIM):
        s = head(h)
        weights = p_ref[h]
        u = dot_nt(back[:, s], v_ref[:, s])
        first = weights * (u - jnp.sum(weights * u, axis=1, keepdims=True))
        curved = first * ds_ref[h]
        second = curved - weights * jnp.sum(curved, axis=1, keepdims=True)
        first, second = first.astype(bf16), second.astype(bf16)
        hq_out[:, s] = dot(first, dk_ref[:, s]) + dot(second, k_ref[:, s])
        hk_out[:, s] = dot_tn(first, dq_ref[:, s]) + dot_tn(second, q_ref[:, s])


def third_body(
    back_own, res_mate, wo, q_ref, k_ref, v_ref, p_ref, hq_ref, hk_ref, r_ref, head_bits, table,
    ya_out, yb_out, sum_out,
):
    feat = q_ref.shape[1]
    back = (back_own[...] + dot_nt(res_mate[...], wo[:, columns_of(res_mate.shape[1], False)])).astype(bf16)
    signs = (2 * head_bits[...] - 1).astype(f32)
    cosine, sine = table[: table.shape[0] // 2], table[table.shape[0] // 2 :]
    totals = [0.0, 0.0]
    for h in range(feat // HEAD_DIM):
        s = head(h)
        weights = p_ref[h]
        u = dot_nt(back[:, s], v_ref[:, s])
        first = (weights * (u - jnp.sum(weights * u, axis=1, keepdims=True))).astype(bf16)
        hq = (hq_ref[:, s] + dot(first, k_ref[:, s])) * SCALE
        hk = (hk_ref[:, s] + dot_tn(first, q_ref[:, s])) * SCALE
        product = r_ref[:, s]
        for i, gradient in enumerate((hq, hk)):
            y = rotate(gradient, cosine, -sine) * signs[i : i + 1, s]
            y = y.astype(bf16)
            column, cut = i * feat + h * HEAD_DIM, ya_out.shape[1]
            if column < cut:
                ya_out[:, column : column + HEAD_DIM] = y
            else:
                yb_out[:, column - cut : column - cut + HEAD_DIM] = y
            totals[i] = totals[i] + jnp.sum(product * y.astype(f32), axis=0, keepdims=True)
    pair = [jnp.sum(t, axis=1, keepdims=True) for t in totals]
    lane = lax.broadcasted_iota(i32, sum_out.shape, 1)
    total = jnp.where(lane == 0, pair[0], jnp.where(lane == 1, pair[1], 0.0))
    sum_out[...] = total


def stamp_body(y, near, far, out, sum_out):
    length = y.shape[0]
    total = near[...] + far[...]
    sum_out[...] = total
    out[:length, :] = y[...]
    out[length:, :] = pieces_of(total, out.shape[1])


def transpose_body(normed, model_bits, *refs):
    outs, whole = refs[:8], refs[8]
    sign = (2 * model_bits[...] - 1).astype(f32).astype(bf16)
    signed = normed[...] * sign
    for i in range(whole.shape[0] // HEAD_DIM):
        whole[i * HEAD_DIM : (i + 1) * HEAD_DIM, :] = signed[:, i * HEAD_DIM : (i + 1) * HEAD_DIM].T
    rows = whole.shape[0] // 32
    x, z, yl = (lax.axis_index(axis) for axis in DP)
    for which in range(2):
        for far in range(4):
            for step in range(4):
                to_x = lax.rem(x + (step if which == 0 else far), 4)
                to_z = lax.rem(z + (far if which == 0 else step), 4)
                for ey in range(2):
                    to_y = yl if ey == 0 else 1 - yl
                    start = pl.multiple_of(((to_x * 4 + to_z) * 2 + to_y) * rows, rows)
                    at = (step * 2 + ey) * rows
                    outs[which * 4 + far][at : at + rows, :] = whole[pl.ds(start, rows), :]


def rows_times(x_parts, y_parts):
    length = x_parts[0].shape[1]
    return sum(dot(a[...], b[:length, :]) for a, b in zip(x_parts, y_parts))


def estimate_a_body(*refs):
    outs = refs[8:]
    group = outs[0].shape[0]
    whole = rows_times(refs[:4], refs[4:8])
    for step, out in enumerate(outs):
        out[...] = whole[step * group : (step + 1) * group, :].astype(out.dtype)


def estimate_b_body(*refs):
    y_parts, sums, keep, send, sum_out = refs[4:8], refs[8], refs[9], refs[10], refs[11]
    length = refs[0].shape[1]
    group = keep.shape[0]
    rows = group // 4
    total = in_pairs(sums[...], *(read_sums(y[length:, :]) for y in y_parts[1:]))
    sum_out[...] = total
    whole = rows_times(refs[:4], y_parts)
    for step in range(4):
        at = slice(step * rows, (step + 1) * rows)
        keep[at, :] = whole[2 * step * rows : (2 * step + 1) * rows, :]
        send[at, :] = whole[(2 * step + 1) * rows : (2 * step + 2) * rows, :].astype(bf16)
    send[group:, :] = pieces_of(total, send.shape[1])


def middle_a_body(a0, a1, a2, a3, keep, send):
    rows = keep.shape[0]
    a = a0[...] + sum(r[...].astype(f32) for r in (a1, a2, a3))
    keep[...] = a[:rows, :]
    send[...] = a[rows:, :].astype(bf16)


def middle_b_body(keep, came, sums, b0, b1, b2, b3, sum_out):
    group = keep.shape[0]
    rows = group // 4
    whole = keep[...] + came[:group, :].astype(f32)
    total = sums[...] + read_sums(came[group:, :])
    sum_out[...] = total
    b0[...] = whole[:rows, :]
    for step, out in ((1, b1), (2, b2), (3, b3)):
        out[:rows, :] = whole[step * rows : (step + 1) * rows, :].astype(bf16)
        out[rows:, :] = pieces_of(total, out.shape[1])


def final_b_body(b0, b1, b2, b3, sums, sign, tail, mean_out, *, count):
    rows, rest = b0.shape
    signs = sign[:, sign.shape[1] - rest :]
    tail[...] = signs * (b0[...] + sum(r[:rows, :].astype(f32) for r in (b1, b2, b3)))
    total = in_pairs(sums[...], *(read_sums(r[rows:, :]) for r in (b1, b2, b3)))
    lane = lax.broadcasted_iota(i32, (1, total.shape[1]), 1)
    for i in range(2):
        mean_out[i] = jnp.sum(jnp.where(lane == i, total[0:1, :], 0.0)) * (1.0 / count)


def final_a_body(keep, came, sign, tail, diag_query, diag_key):
    feat = diag_query.shape[1]
    more = keep.shape[1] - feat
    a = keep[...] + came[...].astype(f32)
    diag_query[...] = sign[...] * a[:, :feat]
    diag_key[:, :more] = sign[:, :more] * a[:, feat:]
    diag_key[:, more:] = tail[...]


def flip(value, moves):
    axes = tuple(axis for axis, _ in moves)
    sizes = [lax.axis_size(axis) for axis in axes]

    def target(index):
        where = []
        for size in reversed(sizes):
            where.append(index % size)
            index //= size
        where = [f(w) for (_, f), w in zip(moves, reversed(where))]
        result = 0
        for w, size in zip(where, sizes):
            result = result * size + w
        return result

    count = int(np.prod(sizes))
    return lax.ppermute(value, axes if len(axes) > 1 else axes[0], [(i, target(i)) for i in range(count)])


def xor(axis, mask):
    return (axis, lambda i: i ^ mask)


def add(axis, k):
    return (axis, lambda i: (i + k) % lax.axis_size(axis))


def local(tokens, targets, loss_weights, segments, probe_model, probe_heads, norm_gain, w_query, w_key, w_value, w_out):
    length, width = tokens.shape
    feat = w_query.shape[1]
    heads = feat // HEAD_DIM
    half = width // 2
    groups = lax.axis_size(DP)
    entries = width * feat * lax.axis_size(MP)
    table = jnp.asarray(np.concatenate(rope_tables(length)))
    head_bits = probe_heads[0]
    mat = shape((length, feat), bf16)
    square = shape((heads, length, length), f32)
    half16, half32 = shape((length, half), bf16), shape((length, half), f32)
    product = 2 * length * width * feat
    small = 2 * length * length * HEAD_DIM * heads
    weight = pltpu.VMEM((width, feat), bf16)

    normed, q, k, v, p, send, attended, w_out = call(
        forward_body,
        (shape((length, width), bf16), mat, mat, mat, square, half16, mat, shape((feat, width), bf16)),
        [HBM] * 8,
        [
            pltpu.VMEM((length, width), bf16), pltpu.VMEM((1, width), f32), weight, weight,
            pltpu.VMEM((2 * length, HEAD_DIM), f32), pltpu.VMEM((1, length), i32),
            weight, pltpu.SemaphoreType.DMA((8,)),
        ],
        4 * product + 4 * small, 12 * MIB, 32,
    )(*map(in_hbm, (tokens, norm_gain[None, :], w_query, w_key, table, segments, w_value, w_out)))
    mate = [xor("c", 1)]
    far = [xor("yh", 1)]
    came = flip(send, mate)
    along_z, along_x = [[add("z", i)] for i in (1, 2, 3)], [[add("x", i)] for i in (1, 2, 3)]
    sends = call(
        transpose_body,
        (shape((width // 4, length), bf16),) * 8,
        [VMEM] * 2,
        [pltpu.VMEM((width, length), bf16)],
        0, 3 * MIB, 16,
    )(normed, probe_model)
    own = call(out_own_body, half32, [VMEM] * 2, (), product // 2, 2 * MIB, 16)(attended, w_out)
    near = (own + came.astype(f32)).astype(bf16)
    there = flip(near, far)

    dq, dk, r, ds, d_send, d_own = call(
        tangent_body,
        (mat, mat, shape((length, feat), f32), square, half16, half32),
        [VMEM] * 9,
        [pltpu.VMEM((width, feat), bf16)],
        2 * product + 4 * small, 8 * MIB, 32, (near, sends[0]),
    )(normed, probe_model, head_bits, table, q, k, v, p, w_out)
    d_near = (d_own + flip(d_send, mate).astype(f32)).astype(bf16)
    d_there = flip(d_near, far)
    xq = [sends[0]] + [flip(m, where) for m, where in zip(sends[1:4], along_z)]
    xk = [sends[4]] + [flip(m, where) for m, where in zip(sends[5:8], along_x)]

    rows = width // 32
    base, row_weight, sign = call(
        functools.partial(base_body, groups=groups),
        (half32, shape((length, HEAD_DIM), f32), shape((rows, feat), f32)),
        [VMEM] * 3,
        (), 0, 3 * MIB, 16, (d_own,),
    )(tokens, targets, loss_weights[None, :])

    res_own = call(residual_body, half16, [VMEM] * 4, (), 0, 3 * MIB, 16, (d_near,))(near, there, base, row_weight)
    res_mate = flip(res_own, mate)
    hq, hk = call(
        second_body,
        (shape((length, feat), f32),) * 2,
        [VMEM] * 10,
        (), product + 5 * small, 6 * MIB, 24,
    )(res_own, res_mate, w_out, q, k, v, dq, dk, p, ds)

    d_res_own = call(d_residual_body, half16, [VMEM] * 3, (), 0, 2 * MIB, 16, (hq,))(d_near, d_there, row_weight)
    d_res_mate = flip(d_res_own, mate)
    back_own = call(
        back_own_body, shape((length, feat), f32), [VMEM] * 2, (), product // 2, 2 * MIB, 16
    )(d_res_own, w_out)
    cut = 5 * feat // 4
    rest = 2 * feat - cut
    small_sums = shape((16, HEAD_DIM), f32)
    ya, yb, sums = call(
        third_body,
        (shape((length, cut), bf16), shape((length, rest), bf16), small_sums),
        [VMEM] * 12,
        (), product + 3 * small, 6 * MIB, 24,
    )(back_own, d_res_mate, w_out, q, k, v, p, hq, hk, r, head_bits, table)
    ya_in = [ya] + [flip(ya, where) for where in along_z]
    sums = sums + flip(sums, mate)
    yb, sums = call(stamp_body, (shape((length + 16, rest), bf16), small_sums), [VMEM] * 3, (), 0, MIB, 16)(
        yb, sums, flip(sums, far)
    )
    yb_in = [yb] + [flip(yb, where) for where in along_x]

    group = 2 * rows
    part, keep = shape((group, cut), bf16), shape((group, cut), f32)
    a = call(
        estimate_a_body,
        (keep, part, part, part),
        [VMEM] * 8,
        (), product, 3 * MIB, 24,
    )(*xq, *ya_in)
    side = [xor("yl", 1)]
    keep_b, send_b, sums = call(
        estimate_b_body,
        (shape((4 * rows, rest), f32), shape((4 * rows + 16, rest), bf16), small_sums),
        [VMEM] * 9,
        (), product, 3 * MIB, 24,
    )(*xk, *yb_in, sums)
    came_b = flip(send_b, side)
    a_in = [flip(part, where) for part, where in zip(a[1:], along_x)]
    part = shape((rows + 16, rest), bf16)
    *b, sums = call(
        middle_b_body,
        (shape((rows, rest), f32), part, part, part, small_sums),
        [VMEM] * 3,
        (), 0, MIB, 16,
    )(keep_b, came_b, sums)
    b_in = [flip(part, where) for part, where in zip(b[1:], along_z)]
    keep_a, send_a = call(
        middle_a_body, (shape((rows, cut), f32), shape((rows, cut), bf16)), [VMEM] * 4, (), 0, MIB, 16
    )(a[0], *a_in)
    came_a = flip(send_a, side)
    tail, mean = call(
        functools.partial(final_b_body, count=groups * entries),
        (shape((rows, rest), f32), shape((2,), f32)),
        [VMEM] * 6,
        (), 0, MIB, 16,
    )(b[0], *b_in, sums, sign)
    block = shape((rows, feat), f32)
    diag_query, diag_key = call(final_a_body, (block, block), [VMEM] * 4, (), 0, MIB, 16)(keep_a, came_a, sign, tail)
    return diag_query, diag_key, mean


def solution(mesh):
    torus = Mesh(mesh.devices.reshape(4, 4, 2, 2, 2), ("x", "z", "yl", "yh", "c"))
    return jax.shard_map(
        local,
        mesh=torus,
        in_specs=(
            P(DP, None),
            P(DP, None),
            P(DP),
            P(DP, None),
            P(DP, None),
            P(DP, None, MP),
            P(),
            P(None, MP),
            P(None, MP),
            P(None, MP),
            P(MP, None),
        ),
        out_specs=(P(DP, MP), P(DP, MP), P()),
        check_vma=False,
    )
```

```python
import functools

import jax
import jax.numpy as jnp
import numpy as np
from jax import lax
from jax.experimental import pallas as pl
from jax.experimental.pallas import tpu as pltpu
from jax.sharding import Mesh
from jax.sharding import PartitionSpec as P


HEAD_DIM = 128
PRIME = 32749
EPSILON = 1e-06
SCALE = HEAD_DIM**-0.5
MIB = 1 << 20
DP = ("x", "z", "yl")
MP = ("yh", "c")
bf16, f32, i32 = jnp.bfloat16, jnp.float32, jnp.int32
VMEM = pl.BlockSpec(memory_space=pltpu.VMEM)
ANY = pl.BlockSpec(memory_space=pl.ANY)
HBM = pl.BlockSpec(memory_space=pltpu.HBM)
SMEM = pl.BlockSpec(memory_space=pltpu.SMEM)


def shape(dims, kind):
    return jax.ShapeDtypeStruct(dims, kind)


def call(body, outs, ins, scratch=(), flops=0, moved=0, limit=24, after=()):
    count = len(ins)

    def whole(*refs):
        return body(*refs[:count], *refs[count + len(after) :])

    kernel = pl.pallas_call(
        whole,
        out_shape=outs,
        in_specs=list(ins) + [ANY] * len(after),
        out_specs=jax.tree.map(lambda out: VMEM if len(out.shape) > 1 else SMEM, outs),
        scratch_shapes=scratch,
        cost_estimate=pl.CostEstimate(flops=flops, bytes_accessed=moved, transcendentals=0),
        compiler_params=pltpu.CompilerParams(vmem_limit_bytes=limit * MIB),
    )

    def run(*args):
        return kernel(*args, *after)

    return run


def in_hbm(value):
    return pltpu.with_memory_space_constraint(value, pltpu.HBM)


def dot(a, b):
    return jnp.dot(a, b, preferred_element_type=f32)


def dot_nt(a, b):
    return lax.dot_general(a, b, (((1,), (1,)), ((), ())), preferred_element_type=f32)


def dot_tn(a, b):
    return lax.dot_general(a, b, (((0,), (0,)), ((), ())), preferred_element_type=f32)


def head(h):
    return slice(h * HEAD_DIM, (h + 1) * HEAD_DIM)


def rotate(x, cosine, sine):
    return x * cosine + pltpu.roll(x, HEAD_DIM // 2, 1) * sine


def rope_tables(length):
    position = np.arange(length, dtype=np.float32)
    exponent = np.arange(0, HEAD_DIM, 2, dtype=np.float32) / np.float32(HEAD_DIM)
    frequency = np.power(10000.0, -exponent.astype(np.float64)).astype(np.float32)
    angles = (position[:, None] * frequency[None, :]).astype(np.float64)
    cosine, sine = np.cos(angles), np.sin(angles)
    return (
        np.concatenate([cosine, cosine], axis=1).astype(np.float32),
        np.concatenate([-sine, sine], axis=1).astype(np.float32),
    )


def split3(value):
    high = value.astype(bf16)
    rest = value - high.astype(f32)
    middle = rest.astype(bf16)
    low = (rest - middle.astype(f32)).astype(bf16)
    return high, middle, low


def pieces_of(value, columns):
    pieces = split3(value)
    blank = columns // value.shape[1] - len(pieces)
    return jnp.concatenate([*pieces] + [jnp.zeros(value.shape, bf16)] * blank, axis=1)


def read_sums(part):
    return sum(part[:, i * HEAD_DIM : (i + 1) * HEAD_DIM].astype(f32) for i in range(3))


def in_pairs(own, first, second, third):
    return (own + second) + (first + third)


def columns_of(half, own):
    core = lax.axis_index("c")
    return pl.ds(pl.multiple_of((core if own else 1 - core) * half, half), half)


def forward_body(
    tok_hbm, gain_hbm, wq_hbm, wk_hbm, table_hbm, seg_hbm, wv_hbm, wo_hbm,
    normed_out, q_out, k_out, v_out, p_out, send_out, attended_out, wo,
    tok, gain, wq, wk, table, seg, wv, sems,
):
    sources = (tok_hbm, gain_hbm, wq_hbm, wk_hbm, table_hbm, seg_hbm, wv_hbm, wo_hbm)
    places = (tok, gain, wq, wk, table, seg, wv, wo)
    copies = [pltpu.make_async_copy(s, d, sems.at[i]) for i, (s, d) in enumerate(zip(sources, places))]
    for copy in copies[:3]:
        copy.start()
    length = tok.shape[0]
    heads = q_out.shape[1] // HEAD_DIM
    half = send_out.shape[1]
    copies[0].wait()
    for copy in copies[3:]:
        copy.start()
    copies[1].wait()
    tokens = tok[...].astype(f32)
    inverse = lax.rsqrt(jnp.mean(tokens * tokens, axis=1, keepdims=True) + EPSILON)
    normed = (tokens * inverse * gain[...]).astype(bf16)
    normed_out[...] = normed
    copies[2].wait()
    query = dot(normed, wq[...])
    copies[3].wait()
    keys = dot(normed, wk[...])
    for copy in copies[4:7]:
        copy.wait()
    values = dot(normed, wv[...]).astype(bf16)
    v_out[...] = values
    document = jnp.broadcast_to(seg[...].astype(f32), (length, length))
    row = lax.broadcasted_iota(i32, (length, length), 0)
    col = lax.broadcasted_iota(i32, (length, length), 1)
    allowed = (row >= col) & (document == document.T)
    attended = []
    for h in range(heads):
        q = rotate(query[:, head(h)], table[:length], table[length:])
        k = rotate(keys[:, head(h)], table[:length], table[length:])
        q_high, k_high = q.astype(bf16), k.astype(bf16)
        q_low = (q - q_high.astype(f32)).astype(bf16)
        k_low = (k - k_high.astype(f32)).astype(bf16)
        q_out[:, head(h)] = q_high
        k_out[:, head(h)] = k_high
        scores = dot_nt(
            jnp.concatenate([q_high, q_low], axis=1), jnp.concatenate([k_high, k_high], axis=1)
        ) + dot_nt(q_high, k_low)
        raised = jnp.where(allowed, jnp.exp(scores * SCALE), 0.0)
        weights = raised * (1.0 / jnp.sum(raised, axis=1, keepdims=True))
        p_out[h] = weights
        attended.append(dot(weights.astype(bf16), values[:, head(h)]).astype(bf16))
    attended = jnp.concatenate(attended, axis=1)
    copies[7].wait()
    attended_out[...] = attended
    send_out[...] = dot(attended, wo[:, columns_of(half, False)]).astype(bf16)


def out_own_body(attended, wo, out):
    out[...] = dot(attended[...], wo[:, columns_of(out.shape[1], True)])


def small_mod(value):
    estimate = jnp.floor(value.astype(f32) * (1.0 / PRIME)).astype(i32)
    rest = value - estimate * PRIME
    rest = jnp.where(rest < 0, rest + PRIME, rest)
    return jnp.where(rest >= PRIME, rest - PRIME, rest)


def square_state(row0, col0, dims):
    row = row0 + lax.broadcasted_iota(i32, dims, 0)
    col = col0 + lax.broadcasted_iota(i32, dims, 1)
    mixed = small_mod(row * 1103 + col * 2713 + 7)
    return mixed, small_mod(mixed * mixed)


def sign_of(square):
    tenth = square * 0.1 + 0.05
    return jnp.where(tenth - jnp.floor(tenth) < 0.5, 1.0, -1.0)


STEP = 16
SHIFT = (1103 * STEP) % PRIME


def wrap(value):
    return jnp.where(value >= PRIME, value - PRIME, value)


def fill_pattern(col0, out):
    width, columns = out.shape
    mixed, square = square_state(0, col0, (STEP, columns))
    change = small_mod(mixed * (2 * SHIFT % PRIME) + SHIFT * SHIFT % PRIME)
    second = float(2 * SHIFT * SHIFT % PRIME)

    def step(i, state):
        square, change = state
        out[pl.ds(pl.multiple_of(i * STEP, STEP), STEP), :] = sign_of(square).astype(bf16)
        return wrap(square + change), wrap(change + second)

    lax.fori_loop(0, width // STEP, step, (square.astype(f32), change.astype(f32)))


def tangent_body(
    normed, model_bits, head_bits, table, q_ref, k_ref, v_ref, p_ref, wo,
    dq_out, dk_out, r_out, ds_out, send_out, own_out,
    pattern,
):
    heads = q_ref.shape[1] // HEAD_DIM
    half = send_out.shape[1]
    feat = q_ref.shape[1]
    core = lax.axis_index("c")
    fill_pattern((lax.axis_index("yh") * 2 + core) * feat, pattern)
    sign = (2 * model_bits[...] - 1).astype(f32).astype(bf16)
    product = dot(normed[...] * sign, pattern[...])
    r_out[...] = product
    signs = (2 * head_bits[...] - 1).astype(f32)
    d_query = product * signs[0:1, :]
    d_keys = product * signs[1:2, :]
    cosine, sine = table[: table.shape[0] // 2], table[table.shape[0] // 2 :]
    tangents = []
    for h in range(heads):
        dq = rotate(d_query[:, head(h)], cosine, sine).astype(bf16)
        dk = rotate(d_keys[:, head(h)], cosine, sine).astype(bf16)
        dq_out[:, head(h)] = dq
        dk_out[:, head(h)] = dk
        d_scores = dot_nt(
            jnp.concatenate([dq, q_ref[:, head(h)]], axis=1),
            jnp.concatenate([k_ref[:, head(h)], dk], axis=1),
        ) * SCALE
        weights = p_ref[h]
        centred = d_scores - jnp.sum(weights * d_scores, axis=1, keepdims=True)
        ds_out[h] = centred
        tangents.append(dot((weights * centred).astype(bf16), v_ref[:, head(h)]).astype(bf16))
    tangents = jnp.concatenate(tangents, axis=1)
    mine = pl.multiple_of(core * half, half)
    other = pl.multiple_of((1 - core) * half, half)
    send_out[...] = dot(tangents, wo[:, pl.ds(other, half)]).astype(bf16)
    own_out[...] = dot(tangents, wo[:, pl.ds(mine, half)])


def base_body(tokens, targets, loss_weights, base_out, weight_out, sign_out, *, groups):
    half = base_out.shape[1]
    length = base_out.shape[0]
    mine = pl.multiple_of(lax.axis_index("c") * half, half)
    base_out[...] = tokens[:, pl.ds(mine, half)].astype(f32) - targets[:, pl.ds(mine, half)].astype(f32)
    weight_out[...] = jnp.broadcast_to(loss_weights[...] * (1.0 / length), (HEAD_DIM, length)).T
    rows, feat = sign_out.shape
    x, z, yl = (lax.axis_index(axis) for axis in DP)
    row0 = ((x * 4 + z) * 2 + yl) * rows
    col0 = (lax.axis_index("yh") * 2 + lax.axis_index("c")) * feat
    _, square = square_state(row0, col0, (rows, feat))
    sign_out[...] = sign_of(square.astype(f32)) * (1.0 / groups)


def residual_body(near, far, base, weight, out):
    out[...] = ((near[...].astype(f32) + far[...].astype(f32) + base[...]) * weight[:, 0:1]).astype(bf16)


def d_residual_body(near, far, weight, out):
    out[...] = ((near[...].astype(f32) + far[...].astype(f32)) * weight[:, 0:1]).astype(bf16)


def back_of(res_own, res_mate, wo):
    half = res_own.shape[1]
    own = dot_nt(res_own[...], wo[:, columns_of(half, True)])
    return (own + dot_nt(res_mate[...], wo[:, columns_of(half, False)])).astype(bf16)


def back_own_body(res_own, wo, out):
    out[...] = dot_nt(res_own[...], wo[:, columns_of(res_own.shape[1], True)])


def second_body(res_own, res_mate, wo, q_ref, k_ref, v_ref, dq_ref, dk_ref, p_ref, ds_ref, hq_out, hk_out):
    back = back_of(res_own, res_mate, wo)
    for h in range(q_ref.shape[1] // HEAD_DIM):
        s = head(h)
        weights = p_ref[h]
        u = dot_nt(back[:, s], v_ref[:, s])
        first = weights * (u - jnp.sum(weights * u, axis=1, keepdims=True))
        curved = first * ds_ref[h]
        second = curved - weights * jnp.sum(curved, axis=1, keepdims=True)
        first, second = first.astype(bf16), second.astype(bf16)
        hq_out[:, s] = dot(first, dk_ref[:, s]) + dot(second, k_ref[:, s])
        hk_out[:, s] = dot_tn(first, dq_ref[:, s]) + dot_tn(second, q_ref[:, s])


def third_body(
    back_own, res_mate, wo, q_ref, k_ref, v_ref, p_ref, hq_ref, hk_ref, r_ref, head_bits, table,
    ya_out, yb_out, sum_out,
):
    feat = q_ref.shape[1]
    back = (back_own[...] + dot_nt(res_mate[...], wo[:, columns_of(res_mate.shape[1], False)])).astype(bf16)
    signs = (2 * head_bits[...] - 1).astype(f32)
    cosine, sine = table[: table.shape[0] // 2], table[table.shape[0] // 2 :]
    totals = [0.0, 0.0]
    for h in range(feat // HEAD_DIM):
        s = head(h)
        weights = p_ref[h]
        u = dot_nt(back[:, s], v_ref[:, s])
        first = (weights * (u - jnp.sum(weights * u, axis=1, keepdims=True))).astype(bf16)
        hq = (hq_ref[:, s] + dot(first, k_ref[:, s])) * SCALE
        hk = (hk_ref[:, s] + dot_tn(first, q_ref[:, s])) * SCALE
        product = r_ref[:, s]
        for i, gradient in enumerate((hq, hk)):
            y = rotate(gradient, cosine, -sine) * signs[i : i + 1, s]
            y = y.astype(bf16)
            column, cut = i * feat + h * HEAD_DIM, ya_out.shape[1]
            if column < cut:
                ya_out[:, column : column + HEAD_DIM] = y
            else:
                yb_out[:, column - cut : column - cut + HEAD_DIM] = y
            totals[i] = totals[i] + jnp.sum(product * y.astype(f32), axis=0, keepdims=True)
    pair = [jnp.sum(t, axis=1, keepdims=True) for t in totals]
    lane = lax.broadcasted_iota(i32, sum_out.shape, 1)
    total = jnp.where(lane == 0, pair[0], jnp.where(lane == 1, pair[1], 0.0))
    sum_out[...] = total


def stamp_body(y, near, far, out, sum_out):
    length = y.shape[0]
    total = near[...] + far[...]
    sum_out[...] = total
    out[:length, :] = y[...]
    out[length:, :] = pieces_of(total, out.shape[1])


def transpose_body(normed, model_bits, *refs):
    outs, whole = refs[:8], refs[8]
    sign = (2 * model_bits[...] - 1).astype(f32).astype(bf16)
    signed = normed[...] * sign
    for i in range(whole.shape[0] // HEAD_DIM):
        whole[i * HEAD_DIM : (i + 1) * HEAD_DIM, :] = signed[:, i * HEAD_DIM : (i + 1) * HEAD_DIM].T
    rows = whole.shape[0] // 32
    x, z, yl = (lax.axis_index(axis) for axis in DP)
    for which in range(2):
        for far in range(4):
            for step in range(4):
                to_x = lax.rem(x + (step if which == 0 else far), 4)
                to_z = lax.rem(z + (far if which == 0 else step), 4)
                for ey in range(2):
                    to_y = yl if ey == 0 else 1 - yl
                    start = pl.multiple_of(((to_x * 4 + to_z) * 2 + to_y) * rows, rows)
                    at = (step * 2 + ey) * rows
                    outs[which * 4 + far][at : at + rows, :] = whole[pl.ds(start, rows), :]


def rows_times(x_parts, y_parts):
    length = x_parts[0].shape[1]
    return sum(dot(a[...], b[:length, :]) for a, b in zip(x_parts, y_parts))


def part_body(*refs):
    count = len(refs) // 2
    refs[-1][...] = rows_times(refs[:count], refs[count:-1])


def estimate_a_body(before, x_last, y_last, *outs):
    group = outs[0].shape[0]
    whole = before[...] + rows_times([x_last], [y_last])
    for step, out in enumerate(outs):
        out[...] = whole[step * group : (step + 1) * group, :].astype(out.dtype)


def estimate_b_body(*refs):
    before, x_parts, y_parts, (sums, keep, send, sum_out) = refs[0], refs[1:3], refs[3:6], refs[6:]
    length = x_parts[0].shape[1]
    group = keep.shape[0]
    rows = group // 4
    total = in_pairs(sums[...], *(read_sums(y[length:, :]) for y in y_parts))
    sum_out[...] = total
    whole = before[...] + rows_times(x_parts, y_parts[1:])
    for step in range(4):
        at = slice(step * rows, (step + 1) * rows)
        keep[at, :] = whole[2 * step * rows : (2 * step + 1) * rows, :]
        send[at, :] = whole[(2 * step + 1) * rows : (2 * step + 2) * rows, :].astype(bf16)
    send[group:, :] = pieces_of(total, send.shape[1])


def middle_a_body(a0, a1, a2, a3, keep, send):
    rows = keep.shape[0]
    a = a0[...] + sum(r[...].astype(f32) for r in (a1, a2, a3))
    keep[...] = a[:rows, :]
    send[...] = a[rows:, :].astype(bf16)


def middle_b_body(keep, came, sums, b0, b1, b2, b3, sum_out):
    group = keep.shape[0]
    rows = group // 4
    whole = keep[...] + came[:group, :].astype(f32)
    total = sums[...] + read_sums(came[group:, :])
    sum_out[...] = total
    b0[...] = whole[:rows, :]
    for step, out in ((1, b1), (2, b2), (3, b3)):
        out[:rows, :] = whole[step * rows : (step + 1) * rows, :].astype(bf16)
        out[rows:, :] = pieces_of(total, out.shape[1])


def final_b_body(b0, b1, b2, b3, sums, sign, tail, mean_out, *, count):
    rows, rest = b0.shape
    signs = sign[:, sign.shape[1] - rest :]
    tail[...] = signs * (b0[...] + sum(r[:rows, :].astype(f32) for r in (b1, b2, b3)))
    total = in_pairs(sums[...], *(read_sums(r[rows:, :]) for r in (b1, b2, b3)))
    lane = lax.broadcasted_iota(i32, (1, total.shape[1]), 1)
    for i in range(2):
        mean_out[i] = jnp.sum(jnp.where(lane == i, total[0:1, :], 0.0)) * (1.0 / count)


def final_a_body(keep, came, sign, tail, diag_query, diag_key):
    feat = diag_query.shape[1]
    more = keep.shape[1] - feat
    a = keep[...] + came[...].astype(f32)
    diag_query[...] = sign[...] * a[:, :feat]
    diag_key[:, :more] = sign[:, :more] * a[:, feat:]
    diag_key[:, more:] = tail[...]


def flip(value, moves):
    axes = tuple(axis for axis, _ in moves)
    sizes = [lax.axis_size(axis) for axis in axes]

    def target(index):
        where = []
        for size in reversed(sizes):
            where.append(index % size)
            index //= size
        where = [f(w) for (_, f), w in zip(moves, reversed(where))]
        result = 0
        for w, size in zip(where, sizes):
            result = result * size + w
        return result

    count = int(np.prod(sizes))
    return lax.ppermute(value, axes if len(axes) > 1 else axes[0], [(i, target(i)) for i in range(count)])


def xor(axis, mask):
    return (axis, lambda i: i ^ mask)


def add(axis, k):
    return (axis, lambda i: (i + k) % lax.axis_size(axis))


def local(tokens, targets, loss_weights, segments, probe_model, probe_heads, norm_gain, w_query, w_key, w_value, w_out):
    length, width = tokens.shape
    feat = w_query.shape[1]
    heads = feat // HEAD_DIM
    half = width // 2
    groups = lax.axis_size(DP)
    entries = width * feat * lax.axis_size(MP)
    table = jnp.asarray(np.concatenate(rope_tables(length)))
    head_bits = probe_heads[0]
    mat = shape((length, feat), bf16)
    square = shape((heads, length, length), f32)
    half16, half32 = shape((length, half), bf16), shape((length, half), f32)
    product = 2 * length * width * feat
    small = 2 * length * length * HEAD_DIM * heads
    weight = pltpu.VMEM((width, feat), bf16)

    normed, q, k, v, p, send, attended, w_out = call(
        forward_body,
        (shape((length, width), bf16), mat, mat, mat, square, half16, mat, shape((feat, width), bf16)),
        [HBM] * 8,
        [
            pltpu.VMEM((length, width), bf16), pltpu.VMEM((1, width), f32), weight, weight,
            pltpu.VMEM((2 * length, HEAD_DIM), f32), pltpu.VMEM((1, length), i32),
            weight, pltpu.SemaphoreType.DMA((8,)),
        ],
        4 * product + 4 * small, 12 * MIB, 32,
    )(*map(in_hbm, (tokens, norm_gain[None, :], w_query, w_key, table, segments, w_value, w_out)))
    mate = [xor("c", 1)]
    far = [xor("yh", 1)]
    came = flip(send, mate)
    along_z, along_x = [[add("z", i)] for i in (1, 2, 3)], [[add("x", i)] for i in (1, 2, 3)]
    sends = call(
        transpose_body,
        (shape((width // 4, length), bf16),) * 8,
        [VMEM] * 2,
        [pltpu.VMEM((width, length), bf16)],
        0, 3 * MIB, 16,
    )(normed, probe_model)
    own = call(out_own_body, half32, [VMEM] * 2, (), product // 2, 2 * MIB, 16)(attended, w_out)
    near = (own + came.astype(f32)).astype(bf16)
    there = flip(near, far)

    dq, dk, r, ds, d_send, d_own = call(
        tangent_body,
        (mat, mat, shape((length, feat), f32), square, half16, half32),
        [VMEM] * 9,
        [pltpu.VMEM((width, feat), bf16)],
        2 * product + 4 * small, 8 * MIB, 32, (near, sends[0]),
    )(normed, probe_model, head_bits, table, q, k, v, p, w_out)
    d_near = (d_own + flip(d_send, mate).astype(f32)).astype(bf16)
    d_there = flip(d_near, far)
    xq = [sends[0]] + [flip(m, where) for m, where in zip(sends[1:4], along_z)]
    xk = [sends[4]] + [flip(m, where) for m, where in zip(sends[5:8], along_x)]

    rows = width // 32
    base, row_weight, sign = call(
        functools.partial(base_body, groups=groups),
        (half32, shape((length, HEAD_DIM), f32), shape((rows, feat), f32)),
        [VMEM] * 3,
        (), 0, 3 * MIB, 16, (d_own,),
    )(tokens, targets, loss_weights[None, :])

    res_own = call(residual_body, half16, [VMEM] * 4, (), 0, 3 * MIB, 16, (d_near,))(near, there, base, row_weight)
    res_mate = flip(res_own, mate)
    hq, hk = call(
        second_body,
        (shape((length, feat), f32),) * 2,
        [VMEM] * 10,
        (), product + 5 * small, 6 * MIB, 24,
    )(res_own, res_mate, w_out, q, k, v, dq, dk, p, ds)

    d_res_own = call(d_residual_body, half16, [VMEM] * 3, (), 0, 2 * MIB, 16, (hq,))(d_near, d_there, row_weight)
    d_res_mate = flip(d_res_own, mate)
    back_own = call(
        back_own_body, shape((length, feat), f32), [VMEM] * 2, (), product // 2, 2 * MIB, 16
    )(d_res_own, w_out)
    cut = 5 * feat // 4
    rest = 2 * feat - cut
    small_sums = shape((16, HEAD_DIM), f32)
    ya, yb, sums = call(
        third_body,
        (shape((length, cut), bf16), shape((length, rest), bf16), small_sums),
        [VMEM] * 12,
        (), product + 3 * small, 6 * MIB, 24,
    )(back_own, d_res_mate, w_out, q, k, v, p, hq, hk, r, head_bits, table)
    ya_in = [ya] + [flip(ya, where) for where in along_z]
    sums = sums + flip(sums, mate)
    yb, sums = call(stamp_body, (shape((length + 16, rest), bf16), small_sums), [VMEM] * 3, (), 0, MIB, 16)(
        yb, sums, flip(sums, far)
    )
    yb_in = [yb] + [flip(yb, where) for where in along_x]

    group = 2 * rows
    near_first = (0, 1, 3)
    part_a = call(part_body, shape((4 * group, cut), f32), [VMEM] * 6, (), 3 * product // 4, 3 * MIB, 16)(
        *(xq[i] for i in near_first), *(ya_in[i] for i in near_first)
    )
    part_b = call(part_body, shape((4 * group, rest), f32), [VMEM] * 4, (), product // 2, 3 * MIB, 16, (part_a,))(
        *xk[:2], *yb_in[:2]
    )
    part, keep = shape((group, cut), bf16), shape((group, cut), f32)
    a = call(
        estimate_a_body,
        (keep, part, part, part),
        [VMEM] * 3,
        (), product // 4, 3 * MIB, 24,
    )(part_a, xq[2], ya_in[2])
    side = [xor("yl", 1)]
    keep_b, send_b, sums = call(
        estimate_b_body,
        (shape((4 * rows, rest), f32), shape((4 * rows + 16, rest), bf16), small_sums),
        [VMEM] * 7,
        (), product // 2, 3 * MIB, 24, (a[0],),
    )(part_b, *xk[2:], *yb_in[1:], sums)
    came_b = flip(send_b, side)
    a_in = [flip(part, where) for part, where in zip(a[1:], along_x)]
    part = shape((rows + 16, rest), bf16)
    *b, sums = call(
        middle_b_body,
        (shape((rows, rest), f32), part, part, part, small_sums),
        [VMEM] * 3,
        (), 0, MIB, 16,
    )(keep_b, came_b, sums)
    b_in = [flip(part, where) for part, where in zip(b[1:], along_z)]
    keep_a, send_a = call(
        middle_a_body, (shape((rows, cut), f32), shape((rows, cut), bf16)), [VMEM] * 4, (), 0, MIB, 16
    )(a[0], *a_in)
    came_a = flip(send_a, side)
    tail, mean = call(
        functools.partial(final_b_body, count=groups * entries),
        (shape((rows, rest), f32), shape((2,), f32)),
        [VMEM] * 6,
        (), 0, MIB, 16,
    )(b[0], *b_in, sums, sign)
    block = shape((rows, feat), f32)
    diag_query, diag_key = call(final_a_body, (block, block), [VMEM] * 4, (), 0, MIB, 16)(keep_a, came_a, sign, tail)
    return diag_query, diag_key, mean


def solution(mesh):
    torus = Mesh(mesh.devices.reshape(4, 4, 2, 2, 2), ("x", "z", "yl", "yh", "c"))
    return jax.shard_map(
        local,
        mesh=torus,
        in_specs=(
            P(DP, None),
            P(DP, None),
            P(DP),
            P(DP, None),
            P(DP, None),
            P(DP, None, MP),
            P(),
            P(None, MP),
            P(None, MP),
            P(None, MP),
            P(MP, None),
        ),
        out_specs=(P(DP, MP), P(DP, MP), P()),
        check_vma=False,
    )
```

```python
import functools

import jax
import jax.numpy as jnp
import numpy as np
from jax import lax
from jax.experimental import pallas as pl
from jax.experimental.pallas import tpu as pltpu
from jax.sharding import Mesh
from jax.sharding import PartitionSpec as P


HEAD_DIM = 128
PRIME = 32749
EPSILON = 1e-06
SCALE = HEAD_DIM**-0.5
MIB = 1 << 20
DP = ("x", "z", "yl")
MP = ("yh", "c")
bf16, f32, i32 = jnp.bfloat16, jnp.float32, jnp.int32
VMEM = pl.BlockSpec(memory_space=pltpu.VMEM)
ANY = pl.BlockSpec(memory_space=pl.ANY)
HBM = pl.BlockSpec(memory_space=pltpu.HBM)
SMEM = pl.BlockSpec(memory_space=pltpu.SMEM)


def shape(dims, kind):
    return jax.ShapeDtypeStruct(dims, kind)


def call(body, outs, ins, scratch=(), flops=0, moved=0, limit=24, after=()):
    count = len(ins)

    def whole(*refs):
        return body(*refs[:count], *refs[count + len(after) :])

    kernel = pl.pallas_call(
        whole,
        out_shape=outs,
        in_specs=list(ins) + [ANY] * len(after),
        out_specs=jax.tree.map(lambda out: VMEM if len(out.shape) > 1 else SMEM, outs),
        scratch_shapes=scratch,
        cost_estimate=pl.CostEstimate(flops=flops, bytes_accessed=moved, transcendentals=0),
        compiler_params=pltpu.CompilerParams(vmem_limit_bytes=limit * MIB),
    )

    def run(*args):
        return kernel(*args, *after)

    return run


def in_hbm(value):
    return pltpu.with_memory_space_constraint(value, pltpu.HBM)


def dot(a, b):
    return jnp.dot(a, b, preferred_element_type=f32)


def dot_nt(a, b):
    return lax.dot_general(a, b, (((1,), (1,)), ((), ())), preferred_element_type=f32)


def dot_tn(a, b):
    return lax.dot_general(a, b, (((0,), (0,)), ((), ())), preferred_element_type=f32)


def head(h):
    return slice(h * HEAD_DIM, (h + 1) * HEAD_DIM)


def rotate(x, cosine, sine):
    return x * cosine + pltpu.roll(x, HEAD_DIM // 2, 1) * sine


def rope_tables(length):
    position = np.arange(length, dtype=np.float32)
    exponent = np.arange(0, HEAD_DIM, 2, dtype=np.float32) / np.float32(HEAD_DIM)
    frequency = np.power(10000.0, -exponent.astype(np.float64)).astype(np.float32)
    angles = (position[:, None] * frequency[None, :]).astype(np.float64)
    cosine, sine = np.cos(angles), np.sin(angles)
    return (
        np.concatenate([cosine, cosine], axis=1).astype(np.float32),
        np.concatenate([-sine, sine], axis=1).astype(np.float32),
    )


def split3(value):
    high = value.astype(bf16)
    rest = value - high.astype(f32)
    middle = rest.astype(bf16)
    low = (rest - middle.astype(f32)).astype(bf16)
    return high, middle, low


def pieces_of(value, columns):
    pieces = split3(value)
    blank = columns // value.shape[1] - len(pieces)
    return jnp.concatenate([*pieces] + [jnp.zeros(value.shape, bf16)] * blank, axis=1)


def read_sums(part):
    return sum(part[:, i * HEAD_DIM : (i + 1) * HEAD_DIM].astype(f32) for i in range(3))


def in_pairs(own, first, second, third):
    return (own + second) + (first + third)


def columns_of(half, own):
    core = lax.axis_index("c")
    return pl.ds(pl.multiple_of((core if own else 1 - core) * half, half), half)


def forward_body(
    tok_hbm, gain_hbm, wq_hbm, wk_hbm, table_hbm, seg_hbm, wv_hbm, wo_hbm,
    normed_out, q_out, k_out, v_out, p_out, send_out, attended_out, wo,
    tok, gain, wq, wk, table, seg, wv, sems,
):
    sources = (tok_hbm, gain_hbm, wq_hbm, wk_hbm, table_hbm, seg_hbm, wv_hbm, wo_hbm)
    places = (tok, gain, wq, wk, table, seg, wv, wo)
    copies = [pltpu.make_async_copy(s, d, sems.at[i]) for i, (s, d) in enumerate(zip(sources, places))]
    for i in (5, 0, 1, 2):
        copies[i].start()
    length = tok.shape[0]
    heads = q_out.shape[1] // HEAD_DIM
    half = send_out.shape[1]
    copies[5].wait()
    document = jnp.broadcast_to(seg[...].astype(f32), (length, length))
    row = lax.broadcasted_iota(i32, (length, length), 0)
    col = lax.broadcasted_iota(i32, (length, length), 1)
    allowed = (row >= col) & (document == document.T)
    copies[0].wait()
    for i in (3, 4, 6, 7):
        copies[i].start()
    copies[1].wait()
    tokens = tok[...].astype(f32)
    inverse = lax.rsqrt(jnp.mean(tokens * tokens, axis=1, keepdims=True) + EPSILON)
    normed = (tokens * inverse * gain[...]).astype(bf16)
    normed_out[...] = normed
    copies[2].wait()
    query = dot(normed, wq[...])
    copies[3].wait()
    keys = dot(normed, wk[...])
    copies[4].wait()
    copies[6].wait()
    values = dot(normed, wv[...]).astype(bf16)
    v_out[...] = values
    attended = []
    for h in range(heads):
        q = rotate(query[:, head(h)], table[:length], table[length:])
        k = rotate(keys[:, head(h)], table[:length], table[length:])
        q_high, k_high = q.astype(bf16), k.astype(bf16)
        q_low = (q - q_high.astype(f32)).astype(bf16)
        k_low = (k - k_high.astype(f32)).astype(bf16)
        q_out[:, head(h)] = q_high
        k_out[:, head(h)] = k_high
        scores = dot_nt(
            jnp.concatenate([q_high, q_low], axis=1), jnp.concatenate([k_high, k_high], axis=1)
        ) + dot_nt(q_high, k_low)
        raised = jnp.where(allowed, jnp.exp(scores * SCALE), 0.0)
        weights = raised * (1.0 / jnp.sum(raised, axis=1, keepdims=True))
        p_out[h] = weights
        attended.append(dot(weights.astype(bf16), values[:, head(h)]).astype(bf16))
    attended = jnp.concatenate(attended, axis=1)
    copies[7].wait()
    attended_out[...] = attended
    send_out[...] = dot(attended, wo[:, columns_of(half, False)]).astype(bf16)


def out_own_body(attended, wo, out):
    out[...] = dot(attended[...], wo[:, columns_of(out.shape[1], True)])


def small_mod(value):
    estimate = jnp.floor(value.astype(f32) * (1.0 / PRIME)).astype(i32)
    rest = value - estimate * PRIME
    rest = jnp.where(rest < 0, rest + PRIME, rest)
    return jnp.where(rest >= PRIME, rest - PRIME, rest)


def square_state(row0, col0, dims):
    row = row0 + lax.broadcasted_iota(i32, dims, 0)
    col = col0 + lax.broadcasted_iota(i32, dims, 1)
    mixed = small_mod(row * 1103 + col * 2713 + 7)
    return mixed, small_mod(mixed * mixed)


def sign_of(square):
    tenth = square * 0.1 + 0.05
    return jnp.where(tenth - jnp.floor(tenth) < 0.5, 1.0, -1.0)


STEP = 16
SHIFT = (1103 * STEP) % PRIME


def wrap(value):
    return jnp.where(value >= PRIME, value - PRIME, value)


def fill_pattern(col0, out):
    width, columns = out.shape
    mixed, square = square_state(0, col0, (STEP, columns))
    change = small_mod(mixed * (2 * SHIFT % PRIME) + SHIFT * SHIFT % PRIME)
    second = float(2 * SHIFT * SHIFT % PRIME)

    def step(i, state):
        square, change = state
        out[pl.ds(pl.multiple_of(i * STEP, STEP), STEP), :] = sign_of(square).astype(bf16)
        return wrap(square + change), wrap(change + second)

    lax.fori_loop(0, width // STEP, step, (square.astype(f32), change.astype(f32)))


def tangent_body(
    normed, model_bits, head_bits, table, q_ref, k_ref, v_ref, p_ref, wo,
    dq_out, dk_out, r_out, ds_out, send_out, own_out,
    pattern,
):
    heads = q_ref.shape[1] // HEAD_DIM
    half = send_out.shape[1]
    feat = q_ref.shape[1]
    core = lax.axis_index("c")
    fill_pattern((lax.axis_index("yh") * 2 + core) * feat, pattern)
    sign = (2 * model_bits[...] - 1).astype(f32).astype(bf16)
    product = dot(normed[...] * sign, pattern[...])
    r_out[...] = product
    signs = (2 * head_bits[...] - 1).astype(f32)
    d_query = product * signs[0:1, :]
    d_keys = product * signs[1:2, :]
    cosine, sine = table[: table.shape[0] // 2], table[table.shape[0] // 2 :]
    tangents = []
    for h in range(heads):
        dq = rotate(d_query[:, head(h)], cosine, sine).astype(bf16)
        dk = rotate(d_keys[:, head(h)], cosine, sine).astype(bf16)
        dq_out[:, head(h)] = dq
        dk_out[:, head(h)] = dk
        d_scores = dot_nt(
            jnp.concatenate([dq, q_ref[:, head(h)]], axis=1),
            jnp.concatenate([k_ref[:, head(h)], dk], axis=1),
        ) * SCALE
        weights = p_ref[h]
        centred = d_scores - jnp.sum(weights * d_scores, axis=1, keepdims=True)
        ds_out[h] = centred
        tangents.append(dot((weights * centred).astype(bf16), v_ref[:, head(h)]).astype(bf16))
    tangents = jnp.concatenate(tangents, axis=1)
    mine = pl.multiple_of(core * half, half)
    other = pl.multiple_of((1 - core) * half, half)
    send_out[...] = dot(tangents, wo[:, pl.ds(other, half)]).astype(bf16)
    own_out[...] = dot(tangents, wo[:, pl.ds(mine, half)])


def base_body(tokens, targets, loss_weights, base_out, weight_out, sign_out, *, groups):
    half = base_out.shape[1]
    length = base_out.shape[0]
    mine = pl.multiple_of(lax.axis_index("c") * half, half)
    base_out[...] = tokens[:, pl.ds(mine, half)].astype(f32) - targets[:, pl.ds(mine, half)].astype(f32)
    weight_out[...] = jnp.broadcast_to(loss_weights[...] * (1.0 / length), (HEAD_DIM, length)).T
    rows, feat = sign_out.shape
    x, z, yl = (lax.axis_index(axis) for axis in DP)
    row0 = ((x * 4 + z) * 2 + yl) * rows
    col0 = (lax.axis_index("yh") * 2 + lax.axis_index("c")) * feat
    _, square = square_state(row0, col0, (rows, feat))
    sign_out[...] = sign_of(square.astype(f32)) * (1.0 / groups)


def residual_body(near, far, base, weight, out):
    out[...] = ((near[...].astype(f32) + far[...].astype(f32) + base[...]) * weight[:, 0:1]).astype(bf16)


def d_residual_body(near, far, weight, out):
    out[...] = ((near[...].astype(f32) + far[...].astype(f32)) * weight[:, 0:1]).astype(bf16)


def back_of(res_own, res_mate, wo):
    half = res_own.shape[1]
    own = dot_nt(res_own[...], wo[:, columns_of(half, True)])
    return (own + dot_nt(res_mate[...], wo[:, columns_of(half, False)])).astype(bf16)


def back_own_body(res_own, wo, out):
    out[...] = dot_nt(res_own[...], wo[:, columns_of(res_own.shape[1], True)])


def second_body(res_own, res_mate, wo, q_ref, k_ref, v_ref, dq_ref, dk_ref, p_ref, ds_ref, hq_out, hk_out):
    back = back_of(res_own, res_mate, wo)
    for h in range(q_ref.shape[1] // HEAD_DIM):
        s = head(h)
        weights = p_ref[h]
        u = dot_nt(back[:, s], v_ref[:, s])
        first = weights * (u - jnp.sum(weights * u, axis=1, keepdims=True))
        curved = first * ds_ref[h]
        second = curved - weights * jnp.sum(curved, axis=1, keepdims=True)
        first, second = first.astype(bf16), second.astype(bf16)
        hq_out[:, s] = dot(first, dk_ref[:, s]) + dot(second, k_ref[:, s])
        hk_out[:, s] = dot_tn(first, dq_ref[:, s]) + dot_tn(second, q_ref[:, s])


def third_body(
    back_own, res_mate, wo, q_ref, k_ref, v_ref, p_ref, hq_ref, hk_ref, r_ref, head_bits, table,
    ya_out, yb_out, sum_out,
):
    feat = q_ref.shape[1]
    back = (back_own[...] + dot_nt(res_mate[...], wo[:, columns_of(res_mate.shape[1], False)])).astype(bf16)
    signs = (2 * head_bits[...] - 1).astype(f32)
    cosine, sine = table[: table.shape[0] // 2], table[table.shape[0] // 2 :]
    totals = [0.0, 0.0]
    for h in range(feat // HEAD_DIM):
        s = head(h)
        weights = p_ref[h]
        u = dot_nt(back[:, s], v_ref[:, s])
        first = (weights * (u - jnp.sum(weights * u, axis=1, keepdims=True))).astype(bf16)
        hq = (hq_ref[:, s] + dot(first, k_ref[:, s])) * SCALE
        hk = (hk_ref[:, s] + dot_tn(first, q_ref[:, s])) * SCALE
        product = r_ref[:, s]
        for i, gradient in enumerate((hq, hk)):
            y = rotate(gradient, cosine, -sine) * signs[i : i + 1, s]
            y = y.astype(bf16)
            column, cut = i * feat + h * HEAD_DIM, ya_out.shape[1]
            if column < cut:
                ya_out[:, column : column + HEAD_DIM] = y
            else:
                yb_out[:, column - cut : column - cut + HEAD_DIM] = y
            totals[i] = totals[i] + jnp.sum(product * y.astype(f32), axis=0, keepdims=True)
    pair = [jnp.sum(t, axis=1, keepdims=True) for t in totals]
    lane = lax.broadcasted_iota(i32, sum_out.shape, 1)
    total = jnp.where(lane == 0, pair[0], jnp.where(lane == 1, pair[1], 0.0))
    sum_out[...] = total


def stamp_body(y, near, far, out, sum_out):
    length = y.shape[0]
    total = near[...] + far[...]
    sum_out[...] = total
    out[:length, :] = y[...]
    out[length:, :] = pieces_of(total, out.shape[1])


def transpose_body(normed, model_bits, *refs):
    outs, whole = refs[:8], refs[8]
    sign = (2 * model_bits[...] - 1).astype(f32).astype(bf16)
    signed = normed[...] * sign
    for i in range(whole.shape[0] // HEAD_DIM):
        whole[i * HEAD_DIM : (i + 1) * HEAD_DIM, :] = signed[:, i * HEAD_DIM : (i + 1) * HEAD_DIM].T
    rows = whole.shape[0] // 32
    x, z, yl = (lax.axis_index(axis) for axis in DP)
    for which in range(2):
        for far in range(4):
            for step in range(4):
                to_x = lax.rem(x + (step if which == 0 else far), 4)
                to_z = lax.rem(z + (far if which == 0 else step), 4)
                for ey in range(2):
                    to_y = yl if ey == 0 else 1 - yl
                    start = pl.multiple_of(((to_x * 4 + to_z) * 2 + to_y) * rows, rows)
                    at = (step * 2 + ey) * rows
                    outs[which * 4 + far][at : at + rows, :] = whole[pl.ds(start, rows), :]


def rows_times(x_parts, y_parts):
    length = x_parts[0].shape[1]
    return sum(dot(a[...], b[:length, :]) for a, b in zip(x_parts, y_parts))


def part_body(*refs):
    count = len(refs) // 2
    refs[-1][...] = rows_times(refs[:count], refs[count:-1])


def estimate_a_body(before, x_last, y_last, *outs):
    group = outs[0].shape[0]
    whole = before[...] + rows_times([x_last], [y_last])
    for step, out in enumerate(outs):
        out[...] = whole[step * group : (step + 1) * group, :].astype(out.dtype)


def estimate_b_body(*refs):
    before, x_parts, y_parts, (sums, keep, send, sum_out) = refs[0], refs[1:3], refs[3:6], refs[6:]
    length = x_parts[0].shape[1]
    group = keep.shape[0]
    rows = group // 4
    total = in_pairs(sums[...], *(read_sums(y[length:, :]) for y in y_parts))
    sum_out[...] = total
    whole = before[...] + rows_times(x_parts, y_parts[1:])
    for step in range(4):
        at = slice(step * rows, (step + 1) * rows)
        keep[at, :] = whole[2 * step * rows : (2 * step + 1) * rows, :]
        send[at, :] = whole[(2 * step + 1) * rows : (2 * step + 2) * rows, :].astype(bf16)
    send[group:, :] = pieces_of(total, send.shape[1])


def middle_a_body(a0, a1, a2, a3, keep, send):
    rows = keep.shape[0]
    a = a0[...] + sum(r[...].astype(f32) for r in (a1, a2, a3))
    keep[...] = a[:rows, :]
    send[...] = a[rows:, :].astype(bf16)


def middle_b_body(keep, came, sums, b0, b1, b2, b3, sum_out):
    group = keep.shape[0]
    rows = group // 4
    whole = keep[...] + came[:group, :].astype(f32)
    total = sums[...] + read_sums(came[group:, :])
    sum_out[...] = total
    b0[...] = whole[:rows, :]
    for step, out in ((1, b1), (2, b2), (3, b3)):
        out[:rows, :] = whole[step * rows : (step + 1) * rows, :].astype(bf16)
        out[rows:, :] = pieces_of(total, out.shape[1])


def final_b_body(b0, b1, b2, b3, sums, sign, tail, mean_out, *, count):
    rows, rest = b0.shape
    signs = sign[:, sign.shape[1] - rest :]
    tail[...] = signs * (b0[...] + sum(r[:rows, :].astype(f32) for r in (b1, b2, b3)))
    total = in_pairs(sums[...], *(read_sums(r[rows:, :]) for r in (b1, b2, b3)))
    lane = lax.broadcasted_iota(i32, (1, total.shape[1]), 1)
    for i in range(2):
        mean_out[i] = jnp.sum(jnp.where(lane == i, total[0:1, :], 0.0)) * (1.0 / count)


def final_a_body(keep, came, sign, tail, diag_query, diag_key):
    feat = diag_query.shape[1]
    more = keep.shape[1] - feat
    a = keep[...] + came[...].astype(f32)
    diag_query[...] = sign[...] * a[:, :feat]
    diag_key[:, :more] = sign[:, :more] * a[:, feat:]
    diag_key[:, more:] = tail[...]


def flip(value, moves):
    axes = tuple(axis for axis, _ in moves)
    sizes = [lax.axis_size(axis) for axis in axes]

    def target(index):
        where = []
        for size in reversed(sizes):
            where.append(index % size)
            index //= size
        where = [f(w) for (_, f), w in zip(moves, reversed(where))]
        result = 0
        for w, size in zip(where, sizes):
            result = result * size + w
        return result

    count = int(np.prod(sizes))
    return lax.ppermute(value, axes if len(axes) > 1 else axes[0], [(i, target(i)) for i in range(count)])


def xor(axis, mask):
    return (axis, lambda i: i ^ mask)


def add(axis, k):
    return (axis, lambda i: (i + k) % lax.axis_size(axis))


def local(tokens, targets, loss_weights, segments, probe_model, probe_heads, norm_gain, w_query, w_key, w_value, w_out):
    length, width = tokens.shape
    feat = w_query.shape[1]
    heads = feat // HEAD_DIM
    half = width // 2
    groups = lax.axis_size(DP)
    entries = width * feat * lax.axis_size(MP)
    table = jnp.asarray(np.concatenate(rope_tables(length)))
    head_bits = probe_heads[0]
    mat = shape((length, feat), bf16)
    square = shape((heads, length, length), f32)
    half16, half32 = shape((length, half), bf16), shape((length, half), f32)
    product = 2 * length * width * feat
    small = 2 * length * length * HEAD_DIM * heads
    weight = pltpu.VMEM((width, feat), bf16)

    normed, q, k, v, p, send, attended, w_out = call(
        forward_body,
        (shape((length, width), bf16), mat, mat, mat, square, half16, mat, shape((feat, width), bf16)),
        [HBM] * 8,
        [
            pltpu.VMEM((length, width), bf16), pltpu.VMEM((1, width), f32), weight, weight,
            pltpu.VMEM((2 * length, HEAD_DIM), f32), pltpu.VMEM((1, length), i32),
            weight, pltpu.SemaphoreType.DMA((8,)),
        ],
        4 * product + 4 * small, 12 * MIB, 32,
    )(*map(in_hbm, (tokens, norm_gain[None, :], w_query, w_key, table, segments, w_value, w_out)))
    mate = [xor("c", 1)]
    far = [xor("yh", 1)]
    came = flip(send, mate)
    along_z, along_x = [[add("z", i)] for i in (1, 2, 3)], [[add("x", i)] for i in (1, 2, 3)]
    sends = call(
        transpose_body,
        (shape((width // 4, length), bf16),) * 8,
        [VMEM] * 2,
        [pltpu.VMEM((width, length), bf16)],
        0, 3 * MIB, 16,
    )(normed, probe_model)
    own = call(out_own_body, half32, [VMEM] * 2, (), product // 2, 2 * MIB, 16)(attended, w_out)
    near = (own + came.astype(f32)).astype(bf16)
    there = flip(near, far)

    dq, dk, r, ds, d_send, d_own = call(
        tangent_body,
        (mat, mat, shape((length, feat), f32), square, half16, half32),
        [VMEM] * 9,
        [pltpu.VMEM((width, feat), bf16)],
        2 * product + 4 * small, 8 * MIB, 32, (near, sends[0]),
    )(normed, probe_model, head_bits, table, q, k, v, p, w_out)
    d_near = (d_own + flip(d_send, mate).astype(f32)).astype(bf16)
    d_there = flip(d_near, far)
    xq = [sends[0]] + [flip(m, where) for m, where in zip(sends[1:4], along_z)]
    xk = [sends[4]] + [flip(m, where) for m, where in zip(sends[5:8], along_x)]

    rows = width // 32
    base, row_weight, sign = call(
        functools.partial(base_body, groups=groups),
        (half32, shape((length, HEAD_DIM), f32), shape((rows, feat), f32)),
        [VMEM] * 3,
        (), 0, 3 * MIB, 16, (d_own,),
    )(tokens, targets, loss_weights[None, :])

    res_own = call(residual_body, half16, [VMEM] * 4, (), 0, 3 * MIB, 16, (d_near,))(near, there, base, row_weight)
    res_mate = flip(res_own, mate)
    hq, hk = call(
        second_body,
        (shape((length, feat), f32),) * 2,
        [VMEM] * 10,
        (), product + 5 * small, 6 * MIB, 24,
    )(res_own, res_mate, w_out, q, k, v, dq, dk, p, ds)

    d_res_own = call(d_residual_body, half16, [VMEM] * 3, (), 0, 2 * MIB, 16, (hq,))(d_near, d_there, row_weight)
    d_res_mate = flip(d_res_own, mate)
    back_own = call(
        back_own_body, shape((length, feat), f32), [VMEM] * 2, (), product // 2, 2 * MIB, 16
    )(d_res_own, w_out)
    cut = 5 * feat // 4
    rest = 2 * feat - cut
    small_sums = shape((16, HEAD_DIM), f32)
    ya, yb, sums = call(
        third_body,
        (shape((length, cut), bf16), shape((length, rest), bf16), small_sums),
        [VMEM] * 12,
        (), product + 3 * small, 6 * MIB, 24,
    )(back_own, d_res_mate, w_out, q, k, v, p, hq, hk, r, head_bits, table)
    ya_in = [ya] + [flip(ya, where) for where in along_z]
    sums = sums + flip(sums, mate)
    yb, sums = call(stamp_body, (shape((length + 16, rest), bf16), small_sums), [VMEM] * 3, (), 0, MIB, 16)(
        yb, sums, flip(sums, far)
    )
    yb_in = [yb] + [flip(yb, where) for where in along_x]

    group = 2 * rows
    near_first = (0, 1, 3)
    part_a = call(part_body, shape((4 * group, cut), f32), [VMEM] * 6, (), 3 * product // 4, 3 * MIB, 16)(
        *(xq[i] for i in near_first), *(ya_in[i] for i in near_first)
    )
    part_b = call(part_body, shape((4 * group, rest), f32), [VMEM] * 4, (), product // 2, 3 * MIB, 16, (part_a,))(
        *xk[:2], *yb_in[:2]
    )
    part, keep = shape((group, cut), bf16), shape((group, cut), f32)
    a = call(
        estimate_a_body,
        (keep, part, part, part),
        [VMEM] * 3,
        (), product // 4, 3 * MIB, 24,
    )(part_a, xq[2], ya_in[2])
    side = [xor("yl", 1)]
    keep_b, send_b, sums = call(
        estimate_b_body,
        (shape((4 * rows, rest), f32), shape((4 * rows + 16, rest), bf16), small_sums),
        [VMEM] * 7,
        (), product // 2, 3 * MIB, 24, (a[0],),
    )(part_b, *xk[2:], *yb_in[1:], sums)
    came_b = flip(send_b, side)
    a_in = [flip(part, where) for part, where in zip(a[1:], along_x)]
    part = shape((rows + 16, rest), bf16)
    *b, sums = call(
        middle_b_body,
        (shape((rows, rest), f32), part, part, part, small_sums),
        [VMEM] * 3,
        (), 0, MIB, 16,
    )(keep_b, came_b, sums)
    b_in = [flip(part, where) for part, where in zip(b[1:], along_z)]
    keep_a, send_a = call(
        middle_a_body, (shape((rows, cut), f32), shape((rows, cut), bf16)), [VMEM] * 4, (), 0, MIB, 16
    )(a[0], *a_in)
    came_a = flip(send_a, side)
    tail, mean = call(
        functools.partial(final_b_body, count=groups * entries),
        (shape((rows, rest), f32), shape((2,), f32)),
        [VMEM] * 6,
        (), 0, MIB, 16,
    )(b[0], *b_in, sums, sign)
    block = shape((rows, feat), f32)
    diag_query, diag_key = call(final_a_body, (block, block), [VMEM] * 4, (), 0, MIB, 16)(keep_a, came_a, sign, tail)
    return diag_query, diag_key, mean


def solution(mesh):
    torus = Mesh(mesh.devices.reshape(4, 4, 2, 2, 2), ("x", "z", "yl", "yh", "c"))
    return jax.shard_map(
        local,
        mesh=torus,
        in_specs=(
            P(DP, None),
            P(DP, None),
            P(DP),
            P(DP, None),
            P(DP, None),
            P(DP, None, MP),
            P(),
            P(None, MP),
            P(None, MP),
            P(None, MP),
            P(MP, None),
        ),
        out_specs=(P(DP, MP), P(DP, MP), P()),
        check_vma=False,
    )
```
